512 devices in a mesh: row: 16 (over z, core), col: 16 (over x_hi, y), freq: 2 (over x_lo).
Axes of the slice: x: 4 (x_hi: 2, x_lo: 2; x = x_hi * 2 + x_lo), y: 8, z: 8, core: 2. Of those that a mesh axis runs over, the one named last changes fastest.
Arguments:
- spectra: bfloat16 [10240, 4096], P(('row', 'col'), 'freq'), parts along dimension 1, may hold values from -6 to 6
- loading: float32 [20480], P('freq'), parts along dimension 0, may hold values from 0.05 to 0.5
- delays: int32 [10240, 2048], P('row', 'col'), may hold values from 0 to 1023
- bin_index: int32 [2], P('freq'), parts along dimension 0, may hold values from 1 to 1023
Outputs:
- trailing: float32 [20480, 10240], P(('freq', 'row'), 'col'), parts along dimension 0
- panel: float32 [20480, 512], P(('freq', 'row')), parts along dimension 0
- whitened: float32 [2, 20480, 2048], P(None, ('freq', 'row'), 'col'), parts along dimension 1
The draws below stay inside these ranges and needn't reach their ends.
There are 2 independent parts, one for each index of `freq`. The reference program is written for one: setup_inputs(seed, part) draws one part's arguments, and reference() takes and returns one part's arrays. A program takes and returns all parts, laid end to end along the dimension named above; an argument that names none is the same for every part. Nothing has to cross between parts.
All inputs are finite; a program needn't handle non-finite values.
Results may differ from the reference program's by a relative error of at most 0.0003.
Values may be sent and summed in bfloat16 or wider, within the bound.
A program may use at most 64 MiB of HBM per device.

```python
import math
import jax
import jax.numpy as jnp
from jax import lax

C = 10240
SNAP = 1024
PANEL = 512
NFFT = 2048
MAXDELAY = 1024
NSLOW = 2048


def place_ends(drawn, own_key, low, top_value):
    longest = drawn.shape.index(max(drawn.shape))
    spots = []
    for shift in (0, 1):
        where = [jax.random.randint(jax.random.fold_in(own_key, axis), (), 0, length) for axis, length in enumerate(drawn.shape)]
        where[longest] = (where[longest] + shift) % drawn.shape[longest]
        spots.append(tuple(where))
    return drawn.at[spots[0]].set(low).at[spots[1]].set(top_value)


def steps_of(rng, extent, shards, least, largest):
    def one(dim, shards_of):
        draws = jax.random.uniform(jax.random.fold_in(jax.random.fold_in(rng, 6), dim), (shards_of,), jnp.float32, least / len(shards), largest / len(shards))
        return jnp.repeat(jnp.exp(draws), extent[dim] // shards_of).reshape((-1,) + (1,) * (len(extent) - dim - 1))

    level = one(*shards[0])
    for cut in shards[1:]:
        level = level * one(*cut)
    return level


def scatter_about(own_key, shape, spread, limit, split=(), dtype=jnp.bfloat16):
    level = steps_of(own_key, shape, split, -0.22, 0.18) if split else 1.0
    array = jax.random.normal(own_key, shape, jnp.float32) * spread * level
    return jnp.minimum(jnp.maximum(array, -limit), limit).astype(dtype)


def setup_inputs(seed: int = 0, part: int = 0) -> dict:
    keys = jax.random.split(jax.random.key(seed), 5)
    own_keys = jax.random.split(jax.random.fold_in(keys[4], part), 5)
    return {
        "spectra": scatter_about(own_keys[0], (C, 2 * SNAP), 0.7071, 6.0, ((0, 256),)),
        "loading": jnp.clip(jnp.exp(jax.random.uniform(own_keys[1], (C,), jnp.float32, math.log(0.05), math.log(0.5))), 0.05, 0.5),
        "delays": place_ends(jax.random.randint(keys[2], (C, NSLOW), 0, MAXDELAY), jax.random.fold_in(keys[2], 1), 0, MAXDELAY - 1).astype(jnp.int32),
        "bin_index": jax.random.randint(own_keys[3], (1,), 1, NFFT // 2).astype(jnp.int32),
    }


two_pi = 6.283185307179586

def lower_solve(factor, right_side):
    return jax.scipy.linalg.solve_triangular(factor, right_side, lower=True)

def reference(spectra, loading, delays, bin_index):
    csd_full = jnp.dot(spectra.astype(jnp.float32), spectra.T.astype(jnp.float32), preferred_element_type=jnp.float32) / SNAP + jnp.diag(loading)
    factor = jnp.linalg.cholesky(csd_full[:PANEL, :PANEL])
    panel = lower_solve(factor, csd_full[:, :PANEL].T).T
    update = csd_full - jnp.dot(panel.astype(jnp.float32), panel.T.astype(jnp.float32), precision=lax.Precision.HIGHEST, preferred_element_type=jnp.float32)
    keep_rows = jnp.arange(C) >= PANEL
    trailing = jnp.where(keep_rows[:, None] & keep_rows[None, :], update, 0.0)
    phase_int = delays * bin_index[0] % NFFT
    phase_angle = phase_int.astype(jnp.float32) * (two_pi / NFFT)
    steer_full = jnp.concatenate([jnp.cos(phase_angle), jnp.sin(phase_angle)], axis=1)
    solved = lower_solve(factor, steer_full[:PANEL])
    lower_rows = steer_full[PANEL:] - jnp.dot(panel[PANEL:].astype(jnp.float32), solved.astype(jnp.float32), precision=lax.Precision.HIGHEST, preferred_element_type=jnp.float32)
    stacked = jnp.concatenate([solved, lower_rows], axis=0)
    whitened = jnp.stack([stacked[:, :NSLOW], stacked[:, NSLOW:]])
    return (trailing, panel, whitened)
```

```python
import jax
import jax.numpy as jnp
from jax import lax
from jax.experimental import pallas as pl
from jax.experimental.pallas import tpu as pltpu
from jax.sharding import PartitionSpec as P

PANEL = 512
NFFT = 2048
NB = 128
SUB = 40
F32 = jnp.float32
HI = lax.Precision.HIGHEST
MESH = pl.DeviceIdType.MESH
TOP_BLOCKS = 13


def dot_nt(a, b, precision=None):
    return lax.dot_general(
        a, b, (((1,), (1,)), ((), ())), precision=precision, preferred_element_type=F32
    )


def dot_nn(a, b, precision=None):
    return lax.dot_general(
        a, b, (((1,), (0,)), ((), ())), precision=precision, preferred_element_type=F32
    )


def gather_kernel(spec, dly, sr, sc, s0, td, loc, zs, zr, xs, ys, yr, ts, tr, ax, ay, bz, br, bf):
    row = lax.axis_index("row")
    col = lax.axis_index("col")
    z, core = row // 2, row % 2
    xh, y = col // 8, col % 8
    sgn = 1 - 2 * core

    def dev(z_, core_, xh_, y_):
        return {"row": z_ * 2 + core_, "col": xh_ * 8 + y_}

    mate = dev(z, 1 - core, xh, y)
    xmate = dev(z, core, 1 - xh, y)
    yplus = dev(z, core, xh, (y + 1) % 8)
    yminus = dev(z, core, xh, (y + 7) % 8)
    ynext = dev(z, core, xh, (y + sgn + 8) % 8)
    znext = dev((z + sgn + 8) % 8, core, xh, y)
    zprev = dev((z - sgn + 8) % 8, core, xh, y)
    peers = (mate, xmate, yplus, yminus, znext, zprev)

    barrier = pltpu.get_barrier_semaphore()
    for peer in peers:
        pl.semaphore_signal(barrier, inc=1, device_id=peer, device_id_type=MESH)

    drains = []

    def rows(ref, j):
        return ref.at[pl.ds(pl.multiple_of(j * SUB, 8), SUB), :]

    def copy(src, sems, index, target, dst=None):
        return pltpu.make_async_remote_copy(
            src_ref=src,
            dst_ref=src if dst is None else dst,
            send_sem=sems.at[0, index],
            recv_sem=sems.at[1, index],
            device_id=target,
            device_id_type=MESH,
        )

    def send(cond, src, sems, index, target):
        desc = copy(src, sems, index, target)
        if cond is None:
            desc.start()
        else:
            @pl.when(cond)
            def _():
                desc.start()
        drains.append((cond, desc))

    def recv(cond, dst, sems, index):
        desc = copy(dst, sems, index, mate)
        if cond is None:
            desc.wait_recv()
        else:
            @pl.when(cond)
            def _():
                desc.wait_recv()

    own = col
    keep_row = pltpu.make_async_copy(spec, rows(sr, own), loc.at[0])
    keep_row.start()
    is_src = row == 0
    have = own < TOP_BLOCKS
    keep_top = pltpu.make_async_copy(spec, rows(s0, own), loc.at[1])

    @pl.when(is_src & have)
    def _():
        keep_top.start()

    keep_del = pltpu.make_async_copy(dly.at[pl.ds(0, PANEL), :], td, loc.at[2])

    @pl.when(is_src)
    def _():
        keep_del.start()
        keep_del.wait()

    @pl.when(is_src & have)
    def _():
        keep_top.wait()

    keep_row.wait()
    pl.semaphore_wait(barrier, len(peers))

    gets_z = ((core == 0) & (z >= 1) & (z <= 4)) | ((core == 1) & (z >= 5))
    gets_m = jnp.logical_not(is_src | gets_z)
    send_z = ((core == 0) & (z <= 3)) | ((core == 1) & ((z == 0) | (z >= 6)))
    send_m = is_src | gets_z
    for c in range(4):
        piece = s0.at[pl.ds(pl.multiple_of(own * SUB, 8), SUB), pl.ds(c * 512, 512)]
        piece_ok = have
        recv(piece_ok & gets_z, piece, zs, c)
        recv(piece_ok & gets_m, piece, zr, c)
        send(piece_ok & send_z, piece, zs, c, znext)
        send(piece_ok & send_m, piece, zr, c, mate)

    pair = (1 - xh) * 8 + y
    pair_ok = pair < TOP_BLOCKS
    own_top = rows(s0, jnp.minimum(own, TOP_BLOCKS - 1))
    pair_top = rows(s0, jnp.minimum(pair, TOP_BLOCKS - 1))
    send(have, own_top, xs, 0, xmate)
    send(have, own_top, ys, 0, ynext)
    recv(pair_ok, pair_top, xs, 0)
    send(pair_ok, pair_top, ys, 1, ynext)
    steps = 4 - core
    for s in range(1, 5):
        for h in range(2):
            src_xh = xh if h == 0 else 1 - xh
            j = src_xh * 8 + (y - sgn * s + 8) % 8
            ok = (j < TOP_BLOCKS) & (s <= steps)
            part = rows(s0, jnp.minimum(j, TOP_BLOCKS - 1))
            recv(ok, part, ys, 2 * (s - 1) + h)
            if s < 4:
                send(ok & (s < steps), part, ys, 2 * s + h, ynext)
            send(ok, part, yr, 2 * (s - 1) + h, mate)

    own_row = rows(sr, own)
    pair_row = rows(sr, pair)
    send(None, own_row, ax, 0, xmate)
    send(None, own_row, ay, 0, yplus)
    send(None, own_row, ay, 1, yminus)
    recv(None, pair_row, ax, 0)
    send(None, pair_row, ay, 2, yplus)
    send(None, pair_row, ay, 3, yminus)
    for c in range(4):
        piece = td.at[pl.ds(c * 128, 128), :]
        recv(gets_z, piece, ts, c)
        recv(gets_m, piece, tr, c)
        send(send_z, piece, ts, c, znext)
        send(send_m, piece, tr, c, mate)
    for s in range(1, 5):
        for h in range(2):
            src_xh = xh if h == 0 else 1 - xh
            for d, target in ((0, yplus), (1, yminus)):
                if d == 1 and s == 4:
                    continue
                shift = -s if d == 0 else s
                part = rows(sr, src_xh * 8 + (y + shift + 8) % 8)
                index = 4 * (s - 1) + 2 * h + d
                recv(None, part, ay, index)
                if s < 4 - d:
                    send(None, part, ay, index + 4, target)

    zsrc, qsrc = col // 2, col % 2
    at_src = z == zsrc
    is_head = at_src & (core == qsrc)
    is_tail = at_src & (core != qsrc)
    away = jnp.logical_not(at_src)
    far = (sgn * (z - zsrc) + 8) % 8
    whole = pltpu.make_async_copy(sr, sc, loc.at[0])

    @pl.when(is_head)
    def _():
        whole.start()
        whole.wait()

    def half(j, c):
        return sc.at[
            pl.ds(pl.multiple_of(j * SUB, 8), SUB), pl.ds(pl.multiple_of(c * 1024, 1024), 1024)
        ]

    for t in range(16):
        full = rows(sc, t)
        mine = half(t, core)
        send(is_head, full, bf, t, mate)
        recv(is_tail, full, bf, t)
        recv(away, mine, bz, t)
        send(far < 7, mine, bz, t, znext)
        send(away, mine, br, t, mate)

    for s in range(1, 5):
        for h in range(2):
            src_xh = xh if h == 0 else 1 - xh
            j = src_xh * 8 + (y + sgn * s + 8) % 8
            ok = (j < TOP_BLOCKS) & (s <= 3 + core)
            recv(ok, rows(s0, jnp.minimum(j, TOP_BLOCKS - 1)), yr, 2 * (s - 1) + h)
    for t in range(16):
        recv(away, half(t, 1 - core), br, t)
    for cond, desc in drains:
        if cond is None:
            desc.wait_send()
        else:
            @pl.when(cond)
            def _(desc=desc):
                desc.wait_send()


def gather(spectra, delays):
    vmem = pl.BlockSpec(memory_space=pltpu.VMEM)
    dma = pltpu.SemaphoreType.DMA
    return pl.pallas_call(
        gather_kernel,
        out_shape=(
            jax.ShapeDtypeStruct((640, 2048), jnp.bfloat16),
            jax.ShapeDtypeStruct((640, 2048), jnp.bfloat16),
            jax.ShapeDtypeStruct((TOP_BLOCKS * SUB, 2048), jnp.bfloat16),
            jax.ShapeDtypeStruct((PANEL, 128), jnp.int32),
        ),
        in_specs=[vmem] * 2,
        out_specs=(vmem,) * 4,
        scratch_shapes=[
            dma((3,)), dma((2, 4)), dma((2, 4)), dma((2, 1)), dma((2, 8)), dma((2, 8)),
            dma((2, 4)), dma((2, 4)), dma((2, 1)), dma((2, 16)), dma((2, 16)), dma((2, 16)),
            dma((2, 16)),
        ],
        compiler_params=pltpu.CompilerParams(collective_id=0, has_side_effects=True),
        name="gather_blocks",
    )(spectra, delays)


def factor_block(tile):
    lanes = (8, NB)
    sub = lax.broadcasted_iota(jnp.int32, lanes, 0)
    col_id = lax.broadcasted_iota(jnp.int32, (NB, NB), 1)
    row_id = lax.broadcasted_iota(jnp.int32, (NB, NB), 0)
    rest = tile
    aug = jnp.where(row_id == col_id, 1.0, 0.0).astype(F32)
    inverse = []
    for i in range(NB // 8):
        top, eye = rest[:8], aug[:8]
        cols = [jnp.broadcast_to(top[:, 8 * i + b : 8 * i + b + 1], lanes) for b in range(8)]
        scales, rows_t, rows_e, links = [], [], [], []
        for j in range(8):
            scale = lax.rsqrt(jnp.broadcast_to(cols[j][j : j + 1], lanes))
            lower = cols[j] * scale
            below = jnp.where(sub > j, lower, 0.0)
            row_t = jnp.broadcast_to(top[j : j + 1], lanes) * scale
            row_e = jnp.broadcast_to(eye[j : j + 1], lanes) * scale
            top = jnp.where(sub == j, row_t, top - below * row_t)
            eye = jnp.where(sub == j, row_e, eye - below * row_e)
            link = {}
            for b in range(j + 1, 8):
                link[b] = jnp.broadcast_to(lower[b : b + 1], lanes)
                cols[b] = cols[b] - below * link[b]
            scales.append(scale)
            rows_t.append(row_t)
            rows_e.append(row_e)
            links.append(link)
        inverse.append(eye)
        if i == NB // 8 - 1:
            break
        count = NB - 8 * (i + 1)
        rest, aug = rest[8:], aug[8:]
        full = (count, NB)

        def spread(value):
            return jnp.broadcast_to(value[None], (count // 8, 8, NB)).reshape(full)

        parts = [jnp.broadcast_to(rest[:, 8 * i + b : 8 * i + b + 1], full) for b in range(8)]
        for j in range(8):
            lower = parts[j] * spread(scales[j])
            rest = rest - lower * spread(rows_t[j])
            aug = aug - lower * spread(rows_e[j])
            for b in range(j + 1, 8):
                parts[b] = parts[b] - lower * spread(links[j][b])
    return jnp.concatenate(inverse, axis=0)


def factor_kernel(s0, load, low, inv, work):
    head = s0[:PANEL]
    diag = lax.broadcasted_iota(jnp.int32, (PANEL, PANEL), 0) == lax.broadcasted_iota(
        jnp.int32, (PANEL, PANEL), 1
    )
    work[...] = dot_nt(head, head) * (1.0 / 1024) + jnp.where(diag, load[...], 0.0)
    low[...] = jnp.zeros_like(low)

    def step(k, carry):
        at = pl.ds(pl.multiple_of(k * NB, NB), NB)
        inverse = factor_block(work[at, at])
        inv[at, :] = inverse
        panel = dot_nt(work[:, at], inverse, HI)
        below = lax.broadcasted_iota(jnp.int32, (PANEL, NB), 0) >= (k + 1) * NB
        panel = jnp.where(below, panel, 0.0)
        low[:, at] = panel
        work[...] = work[...] - dot_nt(panel, panel, HI)
        return carry

    lax.fori_loop(0, PANEL // NB, step, 0)


def factorize(s0, load):
    vmem = pl.BlockSpec(memory_space=pltpu.VMEM)
    return pl.pallas_call(
        factor_kernel,
        out_shape=(
            jax.ShapeDtypeStruct((PANEL, PANEL), F32),
            jax.ShapeDtypeStruct((PANEL, NB), F32),
        ),
        in_specs=[vmem] * 2,
        out_specs=(vmem,) * 2,
        scratch_shapes=[pltpu.VMEM((PANEL, PANEL), F32)],
        name="factor_head",
    )(s0, load)


def steer_of(delays, bin_value):
    phase = (delays * bin_value) & (NFFT - 1)
    turned = phase + NFFT // 8
    quad = (turned >> 9) & 3
    angle = ((turned & 511) - 256).astype(F32) * (6.283185307179586 / NFFT)
    sq = angle * angle
    cosine = 1.0 + sq * (-0.5 + sq * (1.0 / 24 + sq * (-1.0 / 720 + sq * (1.0 / 40320))))
    sine = angle * (1.0 + sq * (-1.0 / 6 + sq * (1.0 / 120 + sq * (-1.0 / 5040 + sq * (1.0 / 362880)))))
    swap = (quad & 1) == 1
    base_c = jnp.where(swap, sine, cosine)
    base_s = jnp.where(swap, cosine, sine)
    out_c = jnp.where((quad == 1) | (quad == 2), -base_c, base_c)
    out_s = jnp.where(quad >= 2, -base_s, base_s)
    return out_c, out_s


def finish_kernel(spot, bins, sr, sc, s0, low, inv, load_r, load_c, dly, td, trail, panel, white, pc):
    row, col = spot[0], spot[1]
    head = s0[:PANEL]

    def solve_rows(block, load, is_first):
        base = dot_nt(block, head) * (1.0 / 1024)
        diag = lax.broadcasted_iota(jnp.int32, base.shape, 0) == lax.broadcasted_iota(
            jnp.int32, base.shape, 1
        )
        base = base + jnp.where(diag & is_first, load[:, :PANEL], 0.0)
        solved = []
        for k in range(PANEL // NB):
            part = base[:, k * NB : (k + 1) * NB]
            if k:
                known = jnp.concatenate(solved, axis=1)
                part = part - dot_nt(known, low[k * NB : (k + 1) * NB, : k * NB], HI)
            solved.append(dot_nt(part, inv[k * NB : (k + 1) * NB, :], HI))
        return jnp.concatenate(solved, axis=1)

    own = solve_rows(sr[...], load_r[...], row == 0)
    panel[...] = own
    other = solve_rows(sc[...], load_c[...], col == 0)
    shape = (640, 640)
    ids_r = lax.broadcasted_iota(jnp.int32, shape, 0)
    ids_c = lax.broadcasted_iota(jnp.int32, shape, 1)
    tile = dot_nt(sr[...], sc[...]) * (1.0 / 1024)
    tile = tile + jnp.where((ids_r == ids_c) & (row == col), load_r[...], 0.0)
    update = tile - dot_nt(own, other, HI)
    keep = (ids_r + row * 640 >= PANEL) & (ids_c + col * 640 >= PANEL)
    trail[...] = jnp.where(keep, update, 0.0)

    top = jnp.concatenate(steer_of(td[...], bins[0]), axis=1)
    solved = []
    for k in range(PANEL // NB):
        part = top[k * NB : (k + 1) * NB]
        if k:
            known = jnp.concatenate(solved, axis=0)
            part = part - dot_nn(low[k * NB : (k + 1) * NB, : k * NB], known, HI)
        solved.append(dot_nn(inv[k * NB : (k + 1) * NB, :], part, HI))
    solved = jnp.concatenate(solved, axis=0)
    steer = jnp.concatenate(steer_of(dly[...], bins[0]), axis=1)
    lower = steer - dot_nn(own, solved, HI)
    padded = jnp.concatenate([solved, jnp.zeros((640 - PANEL, 256), F32)], axis=0)
    ids = lax.broadcasted_iota(jnp.int32, lower.shape, 0)
    stacked = jnp.where((ids < PANEL) & (row == 0), padded, lower)
    white[0] = stacked[:, :128]
    white[1] = stacked[:, 128:]


def finish(spot, bins, sr, sc, s0, low, inv, load_r, load_c, delays, td):
    vmem = pl.BlockSpec(memory_space=pltpu.VMEM)
    smem = pl.BlockSpec(memory_space=pltpu.SMEM)
    return pl.pallas_call(
        finish_kernel,
        out_shape=(
            jax.ShapeDtypeStruct((640, 640), F32),
            jax.ShapeDtypeStruct((640, PANEL), F32),
            jax.ShapeDtypeStruct((2, 640, 128), F32),
        ),
        in_specs=[smem] * 2 + [vmem] * 9,
        out_specs=(vmem,) * 3,
        scratch_shapes=[pltpu.VMEM((8, 128), F32)],
        name="finish_tiles",
    )(spot, bins, sr, sc, s0, low, inv, load_r, load_c, delays, td)


def on_device(spectra, loading, delays, bin_index):
    row = lax.axis_index("row")
    col = lax.axis_index("col")
    load_r = lax.dynamic_slice_in_dim(loading, row * 640, 640)[None]
    load_c = lax.dynamic_slice_in_dim(loading, col * 640, 640)[None]
    spot = jnp.stack([row, col]).astype(jnp.int32)
    sr, sc, s0, td = gather(spectra, delays)
    low, inv = factorize(s0, loading[None, :PANEL])
    return finish(spot, bin_index, sr, sc, s0, low, inv, load_r, load_c, delays, td)


def solution(mesh):
    return jax.shard_map(
        on_device,
        mesh=mesh,
        in_specs=(P(("row", "col"), "freq"), P("freq"), P("row", "col"), P("freq")),
        out_specs=(
            P(("freq", "row"), "col"),
            P(("freq", "row"), None),
            P(None, ("freq", "row"), "col"),
        ),
        check_vma=False,
    )
```

```python
import jax
import jax.numpy as jnp
from jax import lax
from jax.experimental import pallas as pl
from jax.experimental.pallas import tpu as pltpu
from jax.sharding import PartitionSpec as P

PANEL = 512
NFFT = 2048
NB = 128
SUB = 40
F32 = jnp.float32
HI = lax.Precision.HIGHEST
MESH = pl.DeviceIdType.MESH
TOP_BLOCKS = 13
HOLD = 10
SLOTS = 16 + HOLD + 9


def dot_nt(a, b, precision=None):
    return lax.dot_general(
        a, b, (((1,), (1,)), ((), ())), precision=precision, preferred_element_type=F32
    )


def dot_nn(a, b, precision=None):
    return lax.dot_general(
        a, b, (((1,), (0,)), ((), ())), precision=precision, preferred_element_type=F32
    )


def gather_kernel(
    spec, dly, sr, sc, s0, td, loc, rings, top_mate, top_next, top_back, col_mate, col_next, col_back, del_sems
):
    row = lax.axis_index("row")
    col = lax.axis_index("col")
    z, core = row // 2, row % 2
    xh, y = col // 8, col % 8
    sgn = 1 - 2 * core

    def dev(z_, core_, xh_, y_):
        return {"row": z_ * 2 + core_, "col": xh_ * 8 + y_}

    mate = dev(z, 1 - core, xh, y)
    xmate = dev(z, core, 1 - xh, y)
    yplus = dev(z, core, xh, (y + 1) % 8)
    yminus = dev(z, core, xh, (y + 7) % 8)
    znext = dev((z + sgn + 8) % 8, core, xh, y)
    zprev = dev((z - sgn + 8) % 8, core, xh, y)
    peers = (mate, xmate, yplus, yminus, znext, zprev)

    barrier = pltpu.get_barrier_semaphore()
    for peer in peers:
        pl.semaphore_signal(barrier, inc=1, device_id=peer, device_id_type=MESH)

    def block_of(t):
        s, k = (t + 2) // 4, (t + 2) % 4
        d = (k % 2 + k // 2) % 2
        return ((xh + k % 2) % 2) * 8 + (y + (2 * d - 1) * s + 8) % 8, d

    def rows(ref, j):
        return ref.at[pl.ds(pl.multiple_of(j * SUB, 8), SUB), :]

    def half(ref, j, c):
        return ref.at[
            pl.ds(pl.multiple_of(j * SUB, 8), SUB), pl.ds(pl.multiple_of(c * 1024, 1024), 1024)
        ]

    def copy(src, dst, sems, index, target):
        return pltpu.make_async_remote_copy(
            src_ref=src,
            dst_ref=dst,
            send_sem=sems.at[0, index],
            recv_sem=sems.at[1, index],
            device_id=target,
            device_id_type=MESH,
        )

    def both(t, act):
        j, d = block_of(t)
        part = rows(sr, j)

        @pl.when(t == 0)
        def _():
            act(copy(part, part, rings, 1, xmate))
            act(copy(part, part, rings, 2, yplus))
            act(copy(part, part, rings, 4, yminus))

        @pl.when(t == 1)
        def _():
            act(copy(part, part, rings, 3, yminus))
            act(copy(part, part, rings, 5, yplus))

        @pl.when((t >= 2) & (t <= 11))
        def _():
            act(copy(part, part, rings, t + 4, dev(z, core, xh, (y + 1 - 2 * d + 8) % 8)))

    def ring(t):
        j, _ = block_of(t)
        part = rows(sr, j)

        @pl.when((t >= 1) & (t <= 15))
        def _():
            copy(part, part, rings, t, mate).wait_recv()

        both(t, lambda c: c.start())

    class Cast:
        def __init__(self, hold, origin, zsrc, qsrc, sems):
            self.hold, self.origin = hold, origin
            self.to_mate, self.to_next, self.back = sems
            at_src = z == zsrc
            self.head = at_src & (core == qsrc)
            self.tail = at_src & (core != qsrc)
            self.away = jnp.logical_not(at_src)
            self.far = (sgn * (z - zsrc) + 8) % 8

        def sends(self, t, ok, act):
            full_from, full_to, part_from, part_to = self.refs(t)

            @pl.when(ok & self.head)
            def _():
                act(copy(full_from, full_to, self.to_mate, t, mate))
                act(copy(part_from, part_to, self.to_next, t, znext))

            @pl.when(ok & self.tail)
            def _():
                act(copy(part_to, part_to, self.to_next, t, znext))

            @pl.when(ok & self.away)
            def _():
                act(copy(part_to, part_to, self.back, t, mate))

            @pl.when(ok & self.away & (self.far < 7))
            def _():
                act(copy(part_to, part_to, self.to_next, t, znext))

        def refs(self, t):
            j, _ = block_of(t)
            return rows(self.origin, j), rows(self.hold, j), half(self.origin, j, core), half(self.hold, j, core)

        def other(self, t):
            return half(self.hold, block_of(t)[0], 1 - core)

        def step(self, t, ok):
            _, full, _, part = self.refs(t)

            @pl.when(ok & self.tail)
            def _():
                copy(full, full, self.to_mate, t, mate).wait_recv()

            @pl.when(ok & self.away)
            def _():
                copy(part, part, self.to_next, t, mate).wait_recv()

            self.sends(t, ok, lambda c: c.start())

        def collect(self, t, ok):
            part = self.other(t)

            @pl.when(ok & self.away)
            def _():
                copy(part, part, self.back, t, mate).wait_recv()

    class DelayCast(Cast):
        def refs(self, t):
            mine = pl.ds(pl.multiple_of(core * 256, 256), 256)
            return self.hold, self.hold, self.hold.at[mine, :], self.hold.at[mine, :]

        def other(self, t):
            return self.hold.at[pl.ds(pl.multiple_of((1 - core) * 256, 256), 256), :]

    top = Cast(s0, sr, 0, 0, (top_mate, top_next, top_back))
    side = Cast(sc, sr, col // 2, col % 2, (col_mate, col_next, col_back))
    turns = DelayCast(td, td, 0, 0, (del_sems.at[0], del_sems.at[1], del_sems.at[2]))

    def top_ok(t):
        return (t >= 0) & (t <= 15) & (block_of(t)[0] < TOP_BLOCKS)

    def side_ok(t):
        return (t >= 0) & (t <= 15)

    keep_row = pltpu.make_async_copy(spec, rows(sr, col), loc.at[0])
    keep_row.start()
    keep_del = pltpu.make_async_copy(dly.at[pl.ds(0, PANEL), :], td, loc.at[1])

    @pl.when(row == 0)
    def _():
        keep_del.start()
        keep_del.wait()

    keep_row.wait()
    pl.semaphore_wait(barrier, len(peers))

    late = HOLD * ((row == 1).astype(jnp.int32))
    slow = HOLD * ((col == 1).astype(jnp.int32))
    fast = (row == 0).astype(jnp.int32)
    top_lag = jnp.minimum(z, 1) * (top.far + 1)
    side_lag = slow + side.away.astype(jnp.int32) * (side.far + 2)
    turn_at = 2 * turns.far + 2

    def slot(n, carry):
        at = (1 + fast) * (n - late)
        ring(at)
        ring((at + 2) * fast - 1)
        first = 2 * (n - top_lag)
        top.step(first, top_ok(first))
        top.step(first + 1, top_ok(first + 1))
        turns.step(0, n == turn_at)
        t = n - side_lag
        side.step(t, side_ok(t))
        return carry

    lax.fori_loop(0, SLOTS, slot, 0)

    def tidy(t, carry):
        top.collect(t, top_ok(t))
        side.collect(t, side_ok(t))
        both(t, lambda c: c.wait_send())
        top.sends(t, top_ok(t), lambda c: c.wait_send())
        side.sends(t, side_ok(t), lambda c: c.wait_send())
        return carry

    turns.collect(0, row >= 0)
    turns.sends(0, row >= 0, lambda c: c.wait_send())
    lax.fori_loop(0, 16, tidy, 0)
    keep_top = pltpu.make_async_copy(sr.at[pl.ds(0, TOP_BLOCKS * SUB), :], s0, loc.at[0])
    keep_col = pltpu.make_async_copy(sr, sc, loc.at[1])

    @pl.when(top.head)
    def _():
        keep_top.start()
        keep_top.wait()

    @pl.when(side.head)
    def _():
        keep_col.start()
        keep_col.wait()


def gather(spectra, delays):
    vmem = pl.BlockSpec(memory_space=pltpu.VMEM)
    dma = pltpu.SemaphoreType.DMA
    return pl.pallas_call(
        gather_kernel,
        out_shape=(
            jax.ShapeDtypeStruct((640, 2048), jnp.bfloat16),
            jax.ShapeDtypeStruct((640, 2048), jnp.bfloat16),
            jax.ShapeDtypeStruct((TOP_BLOCKS * SUB, 2048), jnp.bfloat16),
            jax.ShapeDtypeStruct((PANEL, 128), jnp.int32),
        ),
        in_specs=[vmem] * 2,
        out_specs=(vmem,) * 4,
        scratch_shapes=[dma((2,))] + [dma((2, 16))] * 7 + [dma((3, 2, 1))],
        compiler_params=pltpu.CompilerParams(collective_id=0, has_side_effects=True),
        name="gather_blocks",
    )(spectra, delays)


def factor_block(tile):
    lanes = (8, NB)
    sub = lax.broadcasted_iota(jnp.int32, lanes, 0)
    col_id = lax.broadcasted_iota(jnp.int32, (NB, NB), 1)
    row_id = lax.broadcasted_iota(jnp.int32, (NB, NB), 0)
    rest = tile
    aug = jnp.where(row_id == col_id, 1.0, 0.0).astype(F32)
    inverse = []
    for i in range(NB // 8):
        top, eye = rest[:8], aug[:8]
        cols = [jnp.broadcast_to(top[:, 8 * i + b : 8 * i + b + 1], lanes) for b in range(8)]
        scales, rows_t, rows_e, links = [], [], [], []
        for j in range(8):
            scale = lax.rsqrt(jnp.broadcast_to(cols[j][j : j + 1], lanes))
            lower = cols[j] * scale
            below = jnp.where(sub > j, lower, 0.0)
            row_t = jnp.broadcast_to(top[j : j + 1], lanes) * scale
            row_e = jnp.broadcast_to(eye[j : j + 1], lanes) * scale
            top = jnp.where(sub == j, row_t, top - below * row_t)
            eye = jnp.where(sub == j, row_e, eye - below * row_e)
            link = {}
            for b in range(j + 1, 8):
                link[b] = jnp.broadcast_to(lower[b : b + 1], lanes)
                cols[b] = cols[b] - below * link[b]
            scales.append(scale)
            rows_t.append(row_t)
            rows_e.append(row_e)
            links.append(link)
        inverse.append(eye)
        if i == NB // 8 - 1:
            break
        count = NB - 8 * (i + 1)
        rest, aug = rest[8:], aug[8:]
        full = (count, NB)

        def spread(value):
            return jnp.broadcast_to(value[None], (count // 8, 8, NB)).reshape(full)

        parts = [jnp.broadcast_to(rest[:, 8 * i + b : 8 * i + b + 1], full) for b in range(8)]
        for j in range(8):
            lower = parts[j] * spread(scales[j])
            rest = rest - lower * spread(rows_t[j])
            aug = aug - lower * spread(rows_e[j])
            for b in range(j + 1, 8):
                parts[b] = parts[b] - lower * spread(links[j][b])
    return jnp.concatenate(inverse, axis=0)


def factor_kernel(s0, load, low, inv, work):
    head = s0[:PANEL]
    ids = lax.broadcasted_iota(jnp.int32, (PANEL, PANEL), 0)
    diag = ids == lax.broadcasted_iota(jnp.int32, (PANEL, PANEL), 1)
    lane = jnp.concatenate([load[b : b + 1, :] for b in range(PANEL // NB)], axis=1)
    work[...] = dot_nt(head, head) * (1.0 / 1024) + jnp.where(diag, lane, 0.0)
    low[...] = jnp.zeros_like(low)
    inv[...] = jnp.zeros_like(inv)

    def step(k, carry):
        at = pl.ds(pl.multiple_of(k * NB, NB), NB)
        inverse = factor_block(work[at, at])
        inv[at, pl.ds(pl.multiple_of((k % 2) * NB, NB), NB)] = inverse
        panel = dot_nt(work[:, at], inverse, HI)
        below = lax.broadcasted_iota(jnp.int32, (PANEL, NB), 0) >= (k + 1) * NB
        panel = jnp.where(below, panel, 0.0)
        low[:, at] = panel
        work[...] = work[...] - dot_nt(panel, panel, HI)
        return carry

    lax.fori_loop(0, PANEL // NB, step, 0)
    for q in range(2):
        a, b, c = 2 * q * NB, (2 * q + 1) * NB, (2 * q + 2) * NB
        inner = dot_nn(low[b:c, a:b], inv[a:b, :NB], HI)
        inv[b:c, :NB] = -dot_nn(inv[b:c, NB:], inner, HI)


def factorize(s0, load):
    vmem = pl.BlockSpec(memory_space=pltpu.VMEM)
    return pl.pallas_call(
        factor_kernel,
        out_shape=(
            jax.ShapeDtypeStruct((PANEL, PANEL), F32),
            jax.ShapeDtypeStruct((PANEL, 2 * NB), F32),
        ),
        in_specs=[vmem] * 2,
        out_specs=(vmem,) * 2,
        scratch_shapes=[pltpu.VMEM((PANEL, PANEL), F32)],
        name="factor_head",
    )(s0, load)


def split(value):
    high = value.astype(jnp.bfloat16)
    return high, (value - high.astype(F32)).astype(jnp.bfloat16)


def three(dot, a, b):
    return dot(a[0], b[0]) + (dot(a[0], b[1]) + dot(a[1], b[0]))


def steer_of(delays, bin_value):
    phase = (delays * bin_value) & (NFFT - 1)
    turned = phase + NFFT // 8
    quad = (turned >> 9) & 3
    angle = ((turned & 511) - 256).astype(F32) * (6.283185307179586 / NFFT)
    sq = angle * angle
    cosine = 1.0 + sq * (-0.5 + sq * (1.0 / 24 + sq * (-1.0 / 720 + sq * (1.0 / 40320))))
    sine = angle * (1.0 + sq * (-1.0 / 6 + sq * (1.0 / 120 + sq * (-1.0 / 5040 + sq * (1.0 / 362880)))))
    swap = (quad & 1) == 1
    base_c = jnp.where(swap, sine, cosine)
    base_s = jnp.where(swap, cosine, sine)
    out_c = jnp.where((quad == 1) | (quad == 2), -base_c, base_c)
    out_s = jnp.where(quad >= 2, -base_s, base_s)
    return out_c, out_s


def finish_kernel(bins, sr, sc, s0, low, inv, load, dly, td, trail, panel, white):
    row, col = lax.axis_index("row"), lax.axis_index("col")
    head = s0[:PANEL]
    mid = 2 * NB
    inv_a, inv_b = split(inv[:mid]), split(inv[mid:])
    link = split(low[mid:, :mid])

    def lanes_of(index):
        return jnp.concatenate([load[pl.ds(index * 5 + b, 1), :] for b in range(5)], axis=1)

    def solve_rows(block, lane, is_first):
        base = dot_nt(block, head) * (1.0 / 1024)
        ids = lax.broadcasted_iota(jnp.int32, base.shape, 0)
        diag = ids == lax.broadcasted_iota(jnp.int32, base.shape, 1)
        base = base + jnp.where(diag & is_first, lane[:, :PANEL], 0.0)
        left = three(dot_nt, split(base[:, :mid]), inv_a)
        left_parts = split(left)
        right = base[:, mid:] - three(dot_nt, left_parts, link)
        right = three(dot_nt, split(right), inv_b)
        right_parts = split(right)
        whole = [jnp.concatenate([p, q], axis=1) for p, q in zip(left_parts, right_parts)]
        return jnp.concatenate([left, right], axis=1), whole

    lane_r = lanes_of(row)
    own, own_parts = solve_rows(sr[...], lane_r, row == 0)
    panel[...] = own
    _, other_parts = solve_rows(sc[...], lanes_of(col), col == 0)
    shape = (640, 640)
    ids_r = lax.broadcasted_iota(jnp.int32, shape, 0)
    ids_c = lax.broadcasted_iota(jnp.int32, shape, 1)
    tile = dot_nt(sr[...], sc[...]) * (1.0 / 1024)
    tile = tile + jnp.where((ids_r == ids_c) & (row == col), lane_r, 0.0)
    update = tile - three(dot_nt, own_parts, other_parts)
    keep = (ids_r + row * 640 >= PANEL) & (ids_c + col * 640 >= PANEL)
    trail[...] = jnp.where(keep, update, 0.0)

    upper = jnp.concatenate(steer_of(td[...], bins[0]), axis=1)
    first = three(dot_nn, inv_a, split(upper[:mid]))
    second = upper[mid:] - three(dot_nn, link, split(first))
    second = three(dot_nn, inv_b, split(second))
    solved = jnp.concatenate([first, second], axis=0)
    steer = jnp.concatenate(steer_of(dly[...], bins[0]), axis=1)
    lower = steer - three(dot_nn, own_parts, split(solved))
    padded = jnp.concatenate([solved, jnp.zeros((640 - PANEL, 256), F32)], axis=0)
    ids = lax.broadcasted_iota(jnp.int32, lower.shape, 0)
    stacked = jnp.where((ids < PANEL) & (row == 0), padded, lower)
    white[0] = stacked[:, :128]
    white[1] = stacked[:, 128:]


def finish(bins, sr, sc, s0, low, inv, load, delays, td):
    vmem = pl.BlockSpec(memory_space=pltpu.VMEM)
    smem = pl.BlockSpec(memory_space=pltpu.SMEM)
    return pl.pallas_call(
        finish_kernel,
        out_shape=(
            jax.ShapeDtypeStruct((640, 640), F32),
            jax.ShapeDtypeStruct((640, PANEL), F32),
            jax.ShapeDtypeStruct((2, 640, 128), F32),
        ),
        in_specs=[smem] + [vmem] * 8,
        out_specs=(vmem,) * 3,
        name="finish_tiles",
    )(bins, sr, sc, s0, low, inv, load, delays, td)


def on_device(spectra, loading, delays, bin_index):
    load = loading.reshape(80, 128)
    sr, sc, s0, td = gather(spectra, delays)
    low, inv = factorize(s0, load)
    return finish(bin_index, sr, sc, s0, low, inv, load, delays, td)


def solution(mesh):
    return jax.shard_map(
        on_device,
        mesh=mesh,
        in_specs=(P(("row", "col"), "freq"), P("freq"), P("row", "col"), P("freq")),
        out_specs=(
            P(("freq", "row"), "col"),
            P(("freq", "row"), None),
            P(None, ("freq", "row"), "col"),
        ),
        check_vma=False,
    )
```

```python
import jax
import jax.numpy as jnp
from jax import lax
from jax.experimental import pallas as pl
from jax.experimental.pallas import tpu as pltpu
from jax.sharding import PartitionSpec as P

PANEL = 512
NFFT = 2048
NB = 128
SUB = 40
F32 = jnp.float32
HI = lax.Precision.HIGHEST
MESH = pl.DeviceIdType.MESH
TOP_BLOCKS = 13
HOLD = 14
LEAD = 30


def dot_nt(a, b, precision=None):
    return lax.dot_general(
        a, b, (((1,), (1,)), ((), ())), precision=precision, preferred_element_type=F32
    )


def dot_nn(a, b, precision=None):
    return lax.dot_general(
        a, b, (((1,), (0,)), ((), ())), precision=precision, preferred_element_type=F32
    )


def gather_kernel(
    spec, dly, load, sr, sc, s0, td, low, inv, work, loc, rings, top_mate, top_next, top_back,
    col_mate, col_next, col_back, del_mate, del_next, del_back
):
    row = lax.axis_index("row")
    col = lax.axis_index("col")
    z, core = row // 2, row % 2
    xh, y = col // 8, col % 8
    sgn = 1 - 2 * core

    def dev(z_, core_, xh_, y_):
        return {"row": z_ * 2 + core_, "col": xh_ * 8 + y_}

    mate = dev(z, 1 - core, xh, y)
    xmate = dev(z, core, 1 - xh, y)
    yplus = dev(z, core, xh, (y + 1) % 8)
    yminus = dev(z, core, xh, (y + 7) % 8)
    znext = dev((z + sgn + 8) % 8, core, xh, y)
    zprev = dev((z - sgn + 8) % 8, core, xh, y)
    peers = (mate, xmate, yplus, yminus, znext, zprev)

    barrier = pltpu.get_barrier_semaphore()
    for peer in peers:
        pl.semaphore_signal(barrier, inc=1, device_id=peer, device_id_type=MESH)

    def block_of(t):
        s, k = (t + 2) // 4, (t + 2) % 4
        d = (k % 2 + k // 2) % 2
        return ((xh + k % 2) % 2) * 8 + (y + (2 * d - 1) * s + 8) % 8, d

    def rows(ref, j):
        return ref.at[pl.ds(pl.multiple_of(j * SUB, 8), SUB), :]

    def half(ref, j, c):
        return ref.at[
            pl.ds(pl.multiple_of(j * SUB, 8), SUB), pl.ds(pl.multiple_of(c * 1024, 1024), 1024)
        ]

    def copy(src, dst, sems, index, target):
        return pltpu.make_async_remote_copy(
            src_ref=src,
            dst_ref=dst,
            send_sem=sems.at[0, index],
            recv_sem=sems.at[1, index],
            device_id=target,
            device_id_type=MESH,
        )

    def both(t, act):
        j, d = block_of(t)
        part = rows(sr, j)

        @pl.when(t == 0)
        def _():
            act(copy(part, part, rings, 1, xmate))
            act(copy(part, part, rings, 2, yplus))
            act(copy(part, part, rings, 4, yminus))

        @pl.when(t == 1)
        def _():
            act(copy(part, part, rings, 3, yminus))
            act(copy(part, part, rings, 5, yplus))

        @pl.when((t >= 2) & (t <= 11))
        def _():
            act(copy(part, part, rings, t + 4, dev(z, core, xh, (y + 1 - 2 * d + 8) % 8)))

    def ring(t):
        j, _ = block_of(t)
        part = rows(sr, j)

        @pl.when((t >= 1) & (t <= 15))
        def _():
            copy(part, part, rings, t, mate).wait_recv()

        both(t, lambda c: c.start())

    class Cast:
        def __init__(self, hold, origin, zsrc, qsrc, sems):
            self.hold, self.origin = hold, origin
            self.to_mate, self.to_next, self.back = sems
            at_src = z == zsrc
            self.head = at_src & (core == qsrc)
            self.tail = at_src & (core != qsrc)
            self.away = jnp.logical_not(at_src)
            self.far = (sgn * (z - zsrc) + 8) % 8

        def sends(self, t, ok, act):
            full_from, full_to, part_from, part_to = self.refs(t)

            @pl.when(ok & self.head)
            def _():
                act(copy(full_from, full_to, self.to_mate, t, mate))
                act(copy(part_from, part_to, self.to_next, t, znext))

            @pl.when(ok & self.tail)
            def _():
                act(copy(part_to, part_to, self.to_next, t, znext))

            @pl.when(ok & self.away)
            def _():
                act(copy(part_to, part_to, self.back, t, mate))

            @pl.when(ok & self.away & (self.far < 7))
            def _():
                act(copy(part_to, part_to, self.to_next, t, znext))

        def refs(self, t):
            j, _ = block_of(t)
            return rows(self.origin, j), rows(self.hold, j), half(self.origin, j, core), half(self.hold, j, core)

        def other(self, t):
            return half(self.hold, block_of(t)[0], 1 - core)

        def step(self, t, ok):
            _, full, _, part = self.refs(t)

            @pl.when(ok & self.tail)
            def _():
                copy(full, full, self.to_mate, t, mate).wait_recv()

            @pl.when(ok & self.away)
            def _():
                copy(part, part, self.to_next, t, mate).wait_recv()

            self.sends(t, ok, lambda c: c.start())

        def collect(self, t, ok):
            part = self.other(t)

            @pl.when(ok & self.away)
            def _():
                copy(part, part, self.back, t, mate).wait_recv()

    class DelayCast(Cast):
        def piece(self, t, c):
            return self.hold.at[pl.ds(pl.multiple_of(t * 256 + c * 128, 128), 128), :]

        def refs(self, t):
            full = self.hold.at[pl.ds(pl.multiple_of(t * 256, 256), 256), :]
            return full, full, self.piece(t, core), self.piece(t, core)

        def other(self, t):
            return self.piece(t, 1 - core)

    top = Cast(s0, sr, 0, 0, (top_mate, top_next, top_back))
    side = Cast(sc, sr, col // 2, col % 2, (col_mate, col_next, col_back))
    turns = DelayCast(td, td, 0, 0, (del_mate, del_next, del_back))

    def top_ok(t):
        return (t >= 0) & (t <= 15) & (block_of(t)[0] < TOP_BLOCKS)

    def side_ok(t):
        return (t >= 0) & (t <= 15)

    def turn_ok(t):
        return (t >= 0) & (t <= 1)

    keep_row = pltpu.make_async_copy(spec, rows(sr, col), loc.at[0])
    keep_row.start()
    keep_del = pltpu.make_async_copy(dly.at[pl.ds(0, PANEL), :], td, loc.at[1])

    @pl.when(row == 0)
    def _():
        keep_del.start()
        keep_del.wait()

    keep_row.wait()
    pl.semaphore_wait(barrier, len(peers))

    def ring_slot(n):
        late = n - HOLD

        @pl.when(row == 0)
        def _():
            ring(n)

        @pl.when((row == 1) & (late % 2 == 0))
        def _():
            ring(late // 2)

        @pl.when((row >= 2) & ((2 * n) % 5 < 2))
        def _():
            ring((2 * n) // 5)

    def lead_slot(n, carry):
        ring_slot(n)
        t = n - 2 * top.far
        top.step(t, top_ok(t))
        return carry

    def side_slot(n):
        ring_slot(n)
        t = n - LEAD - 2 * side.far
        side.step(t, side_ok(t))
        t = n - LEAD - 16 - 2 * turns.far
        turns.step(t, turn_ok(t))

    lax.fori_loop(0, LEAD, lead_slot, 0)

    def top_in(t, carry):
        top.collect(t, top_ok(t))
        return carry

    lax.fori_loop(0, 16, top_in, 0)
    keep_top = pltpu.make_async_copy(sr.at[pl.ds(0, TOP_BLOCKS * SUB), :], s0, loc.at[0])

    @pl.when(top.head)
    def _():
        keep_top.start()
        keep_top.wait()

    factor(s0, load, low, inv, work, lambda k, i: side_slot(LEAD + 8 * k + i))
    keep_col = pltpu.make_async_copy(sr, sc, loc.at[1])

    @pl.when(side.head)
    def _():
        keep_col.start()
        keep_col.wait()

    def tidy(t, carry):
        side.collect(t, t >= 0)
        both(t, lambda c: c.wait_send())
        top.sends(t, top_ok(t), lambda c: c.wait_send())
        side.sends(t, t >= 0, lambda c: c.wait_send())
        turns.collect(t, turn_ok(t))
        turns.sends(t, turn_ok(t), lambda c: c.wait_send())
        return carry

    lax.fori_loop(0, 16, tidy, 0)


def factor_block(tile, between):
    lanes = (8, NB)
    sub = lax.broadcasted_iota(jnp.int32, lanes, 0)
    col_id = lax.broadcasted_iota(jnp.int32, (NB, NB), 1)
    row_id = lax.broadcasted_iota(jnp.int32, (NB, NB), 0)
    rest = tile
    aug = jnp.where(row_id == col_id, 1.0, 0.0).astype(F32)
    inverse = []
    for i in range(NB // 8):
        top, eye = rest[:8], aug[:8]
        cols = [jnp.broadcast_to(top[:, 8 * i + b : 8 * i + b + 1], lanes) for b in range(8)]
        scales, rows_t, rows_e, links = [], [], [], []
        for j in range(8):
            scale = lax.rsqrt(jnp.broadcast_to(cols[j][j : j + 1], lanes))
            lower = cols[j] * scale
            below = jnp.where(sub > j, lower, 0.0)
            row_t = jnp.broadcast_to(top[j : j + 1], lanes) * scale
            row_e = jnp.broadcast_to(eye[j : j + 1], lanes) * scale
            top = jnp.where(sub == j, row_t, top - below * row_t)
            eye = jnp.where(sub == j, row_e, eye - below * row_e)
            link = {}
            for b in range(j + 1, 8):
                link[b] = jnp.broadcast_to(lower[b : b + 1], lanes)
                cols[b] = cols[b] - below * link[b]
            scales.append(scale)
            rows_t.append(row_t)
            rows_e.append(row_e)
            links.append(link)
        inverse.append(eye)
        if i % 2 == 1:
            between(i // 2)
        if i == NB // 8 - 1:
            break
        count = NB - 8 * (i + 1)
        rest, aug = rest[8:], aug[8:]
        full = (count, NB)

        def spread(value):
            return jnp.broadcast_to(value[None], (count // 8, 8, NB)).reshape(full)

        parts = [jnp.broadcast_to(rest[:, 8 * i + b : 8 * i + b + 1], full) for b in range(8)]
        for j in range(8):
            lower = parts[j] * spread(scales[j])
            rest = rest - lower * spread(rows_t[j])
            aug = aug - lower * spread(rows_e[j])
            for b in range(j + 1, 8):
                parts[b] = parts[b] - lower * spread(links[j][b])
    return jnp.concatenate(inverse, axis=0)


def factor(s0, load, low, inv, work, between):
    head = s0[:PANEL]
    ids = lax.broadcasted_iota(jnp.int32, (PANEL, PANEL), 0)
    diag = ids == lax.broadcasted_iota(jnp.int32, (PANEL, PANEL), 1)
    lane = jnp.concatenate([load[b : b + 1, :] for b in range(PANEL // NB)], axis=1)
    work[...] = dot_nt(head, head) * (1.0 / 1024) + jnp.where(diag, lane, 0.0)
    low[...] = jnp.zeros_like(low)
    inv[...] = jnp.zeros_like(inv)

    def step(k, carry):
        at = pl.ds(pl.multiple_of(k * NB, NB), NB)
        inverse = factor_block(work[at, at], lambda i: between(k, i))
        inv[at, pl.ds(pl.multiple_of((k % 2) * NB, NB), NB)] = inverse
        panel = dot_nt(work[:, at], inverse, HI)
        below = lax.broadcasted_iota(jnp.int32, (PANEL, NB), 0) >= (k + 1) * NB
        panel = jnp.where(below, panel, 0.0)
        low[:, at] = panel
        work[...] = work[...] - dot_nt(panel, panel, HI)
        return carry

    lax.fori_loop(0, PANEL // NB, step, 0)
    for q in range(2):
        a, b, c = 2 * q * NB, (2 * q + 1) * NB, (2 * q + 2) * NB
        inner = dot_nn(low[b:c, a:b], inv[a:b, :NB], HI)
        inv[b:c, :NB] = -dot_nn(inv[b:c, NB:], inner, HI)


def gather(spectra, delays, load):
    vmem = pl.BlockSpec(memory_space=pltpu.VMEM)
    dma = pltpu.SemaphoreType.DMA
    return pl.pallas_call(
        gather_kernel,
        out_shape=(
            jax.ShapeDtypeStruct((640, 2048), jnp.bfloat16),
            jax.ShapeDtypeStruct((640, 2048), jnp.bfloat16),
            jax.ShapeDtypeStruct((TOP_BLOCKS * SUB, 2048), jnp.bfloat16),
            jax.ShapeDtypeStruct((PANEL, 128), jnp.int32),
            jax.ShapeDtypeStruct((PANEL, PANEL), F32),
            jax.ShapeDtypeStruct((PANEL, 2 * NB), F32),
        ),
        in_specs=[vmem] * 3,
        out_specs=(vmem,) * 6,
        scratch_shapes=[pltpu.VMEM((PANEL, PANEL), F32), dma((2,))]
        + [dma((2, 16))] * 7
        + [dma((2, 2))] * 3,
        compiler_params=pltpu.CompilerParams(
            collective_id=0, has_side_effects=True, vmem_limit_bytes=20 << 20
        ),
        name="gather_and_factor",
    )(spectra, delays, load)


def split(value):
    high = value.astype(jnp.bfloat16)
    return high, (value - high.astype(F32)).astype(jnp.bfloat16)


def three(dot, a, b):
    return dot(a[0], b[0]) + (dot(a[0], b[1]) + dot(a[1], b[0]))


def steer_of(delays, bin_value):
    phase = (delays * bin_value) & (NFFT - 1)
    turned = phase + NFFT // 8
    quad = (turned >> 9) & 3
    angle = ((turned & 511) - 256).astype(F32) * (6.283185307179586 / NFFT)
    sq = angle * angle
    cosine = 1.0 + sq * (-0.5 + sq * (1.0 / 24 + sq * (-1.0 / 720 + sq * (1.0 / 40320))))
    sine = angle * (1.0 + sq * (-1.0 / 6 + sq * (1.0 / 120 + sq * (-1.0 / 5040 + sq * (1.0 / 362880)))))
    swap = (quad & 1) == 1
    base_c = jnp.where(swap, sine, cosine)
    base_s = jnp.where(swap, cosine, sine)
    out_c = jnp.where((quad == 1) | (quad == 2), -base_c, base_c)
    out_s = jnp.where(quad >= 2, -base_s, base_s)
    return out_c, out_s


def finish_kernel(bins, sr, sc, s0, low, inv, load, dly, td, trail, panel, white):
    row, col = lax.axis_index("row"), lax.axis_index("col")
    head = s0[:PANEL]
    mid = 2 * NB
    inv_a, inv_b = split(inv[:mid]), split(inv[mid:])
    link = split(low[mid:, :mid])

    def lanes_of(index):
        return jnp.concatenate([load[pl.ds(index * 5 + b, 1), :] for b in range(5)], axis=1)

    def solve_rows(block, lane, is_first):
        base = dot_nt(block, head) * (1.0 / 1024)
        ids = lax.broadcasted_iota(jnp.int32, base.shape, 0)
        diag = ids == lax.broadcasted_iota(jnp.int32, base.shape, 1)
        base = base + jnp.where(diag & is_first, lane[:, :PANEL], 0.0)
        left = three(dot_nt, split(base[:, :mid]), inv_a)
        left_parts = split(left)
        right = base[:, mid:] - three(dot_nt, left_parts, link)
        right = three(dot_nt, split(right), inv_b)
        right_parts = split(right)
        whole = [jnp.concatenate([p, q], axis=1) for p, q in zip(left_parts, right_parts)]
        return jnp.concatenate([left, right], axis=1), whole

    lane_r = lanes_of(row)
    own, own_parts = solve_rows(sr[...], lane_r, row == 0)
    panel[...] = own
    _, other_parts = solve_rows(sc[...], lanes_of(col), col == 0)
    shape = (640, 640)
    ids_r = lax.broadcasted_iota(jnp.int32, shape, 0)
    ids_c = lax.broadcasted_iota(jnp.int32, shape, 1)
    tile = dot_nt(sr[...], sc[...]) * (1.0 / 1024)
    tile = tile + jnp.where((ids_r == ids_c) & (row == col), lane_r, 0.0)
    update = tile - three(dot_nt, own_parts, other_parts)
    keep = (ids_r + row * 640 >= PANEL) & (ids_c + col * 640 >= PANEL)
    trail[...] = jnp.where(keep, update, 0.0)

    upper = jnp.concatenate(steer_of(td[...], bins[0]), axis=1)
    first = three(dot_nn, inv_a, split(upper[:mid]))
    second = upper[mid:] - three(dot_nn, link, split(first))
    second = three(dot_nn, inv_b, split(second))
    solved = jnp.concatenate([first, second], axis=0)
    steer = jnp.concatenate(steer_of(dly[...], bins[0]), axis=1)
    lower = steer - three(dot_nn, own_parts, split(solved))
    padded = jnp.concatenate([solved, jnp.zeros((640 - PANEL, 256), F32)], axis=0)
    ids = lax.broadcasted_iota(jnp.int32, lower.shape, 0)
    stacked = jnp.where((ids < PANEL) & (row == 0), padded, lower)
    white[0] = stacked[:, :128]
    white[1] = stacked[:, 128:]


def finish(bins, sr, sc, s0, low, inv, load, delays, td):
    vmem = pl.BlockSpec(memory_space=pltpu.VMEM)
    smem = pl.BlockSpec(memory_space=pltpu.SMEM)
    return pl.pallas_call(
        finish_kernel,
        out_shape=(
            jax.ShapeDtypeStruct((640, 640), F32),
            jax.ShapeDtypeStruct((640, PANEL), F32),
            jax.ShapeDtypeStruct((2, 640, 128), F32),
        ),
        in_specs=[smem] + [vmem] * 8,
        out_specs=(vmem,) * 3,
        compiler_params=pltpu.CompilerParams(vmem_limit_bytes=36 << 20),
        name="finish_tiles",
    )(bins, sr, sc, s0, low, inv, load, delays, td)


def on_device(spectra, loading, delays, bin_index):
    load = loading.reshape(80, 128)
    sr, sc, s0, td, low, inv = gather(spectra, delays, load)
    return finish(bin_index, sr, sc, s0, low, inv, load, delays, td)


def solution(mesh):
    return jax.shard_map(
        on_device,
        mesh=mesh,
        in_specs=(P(("row", "col"), "freq"), P("freq"), P("row", "col"), P("freq")),
        out_specs=(
            P(("freq", "row"), "col"),
            P(("freq", "row"), None),
            P(None, ("freq", "row"), "col"),
        ),
        check_vma=False,
    )
```

```python
import jax
import jax.numpy as jnp
from jax import lax
from jax.experimental import pallas as pl
from jax.experimental.pallas import tpu as pltpu
from jax.sharding import PartitionSpec as P

PANEL = 512
NFFT = 2048
NB = 128
SUB = 40
F32 = jnp.float32
HI = lax.Precision.HIGHEST
MESH = pl.DeviceIdType.MESH
TOP_BLOCKS = 13
HOLD = 14
LEAD = 30


def dot_nt(a, b, precision=None):
    return lax.dot_general(
        a, b, (((1,), (1,)), ((), ())), precision=precision, preferred_element_type=F32
    )


def dot_nn(a, b, precision=None):
    return lax.dot_general(
        a, b, (((1,), (0,)), ((), ())), precision=precision, preferred_element_type=F32
    )


def gather_kernel(
    spec, dly, load, sr, sc, s0, td, link, inv, low, work, ld, loc, rings, top_mate, top_next, top_back,
    col_mate, col_plus, col_minus, col_back, del_mate, del_next, del_back, res
):
    row = lax.axis_index("row")
    col = lax.axis_index("col")
    z, core = row // 2, row % 2
    xh, y = col // 8, col % 8
    sgn = 1 - 2 * core

    def dev(z_, core_, xh_, y_):
        return {"row": z_ * 2 + core_, "col": xh_ * 8 + y_}

    mate = dev(z, 1 - core, xh, y)
    xmate = dev(z, core, 1 - xh, y)
    yplus = dev(z, core, xh, (y + 1) % 8)
    yminus = dev(z, core, xh, (y + 7) % 8)
    zplus = dev((z + 1) % 8, core, xh, y)
    zminus = dev((z + 7) % 8, core, xh, y)
    znext = dev((z + sgn + 8) % 8, core, xh, y)
    peers = (mate, xmate, yplus, yminus, zplus, zminus)

    keep_row = pltpu.make_async_copy(spec, sr.at[pl.ds(pl.multiple_of(col * SUB, 8), SUB), :], loc.at[0])
    keep_row.start()
    keep_del = pltpu.make_async_copy(dly.at[pl.ds(0, PANEL), :], td, loc.at[1])
    keep_load = pltpu.make_async_copy(load, ld, loc.at[2])
    keep_load.start()

    @pl.when(row == 0)
    def _():
        keep_del.start()

    barrier = pltpu.get_barrier_semaphore()
    for peer in peers:
        pl.semaphore_signal(barrier, inc=1, device_id=peer, device_id_type=MESH)

    def block_of(t):
        s, k = (t + 2) // 4, (t + 2) % 4
        d = (k % 2 + k // 2) % 2
        return ((xh + k % 2) % 2) * 8 + (y + (2 * d - 1) * s + 8) % 8, d

    def rows(ref, j):
        return ref.at[pl.ds(pl.multiple_of(j * SUB, 8), SUB), :]

    def half(ref, j, c):
        return ref.at[
            pl.ds(pl.multiple_of(j * SUB, 8), SUB), pl.ds(pl.multiple_of(c * 1024, 1024), 1024)
        ]

    def copy(src, dst, sems, index, target):
        return pltpu.make_async_remote_copy(
            src_ref=src,
            dst_ref=dst,
            send_sem=sems.at[0, index],
            recv_sem=sems.at[1, index],
            device_id=target,
            device_id_type=MESH,
        )

    def both(t, act):
        j, d = block_of(t)
        part = rows(sr, j)

        @pl.when(t == 0)
        def _():
            act(copy(part, part, rings, 1, xmate))
            act(copy(part, part, rings, 2, yplus))
            act(copy(part, part, rings, 4, yminus))

        @pl.when(t == 1)
        def _():
            act(copy(part, part, rings, 3, yminus))
            act(copy(part, part, rings, 5, yplus))

        @pl.when((t >= 2) & (t <= 11))
        def _():
            act(copy(part, part, rings, t + 4, dev(z, core, xh, (y + 1 - 2 * d + 8) % 8)))

    def ring(t):
        j, _ = block_of(t)
        part = rows(sr, j)

        @pl.when((t >= 1) & (t <= 15))
        def _():
            copy(part, part, rings, t, mate).wait_recv()

        both(t, lambda c: c.start())

        @pl.when((t >= 0) & (t <= 15) & (row == col))
        def _():
            copy(part, rows(sc, j), col_mate, t, mate).start()

    class Cast:
        def __init__(self, hold, origin, zsrc, qsrc, sems):
            self.hold, self.origin = hold, origin
            self.to_mate, self.to_next, self.back = sems
            at_src = z == zsrc
            self.head = at_src & (core == qsrc)
            self.tail = at_src & (core != qsrc)
            self.away = jnp.logical_not(at_src)
            self.far = (sgn * (z - zsrc) + 8) % 8

        def sends(self, t, ok, act):
            full_from, full_to, part_from, part_to = self.refs(t)

            @pl.when(ok & self.head)
            def _():
                act(copy(full_from, full_to, self.to_mate, t, mate))
                act(copy(part_from, part_to, self.to_next, t, znext))

            @pl.when(ok & self.tail)
            def _():
                act(copy(part_to, part_to, self.to_next, t, znext))

            @pl.when(ok & self.away)
            def _():
                act(copy(part_to, part_to, self.back, t, mate))

            @pl.when(ok & self.away & (self.far < 7))
            def _():
                act(copy(part_to, part_to, self.to_next, t, znext))

        def refs(self, t):
            j, _ = block_of(t)
            return rows(self.origin, j), rows(self.hold, j), half(self.origin, j, core), half(self.hold, j, core)

        def other(self, t):
            return half(self.hold, block_of(t)[0], 1 - core)

        def step(self, t, ok):
            _, full, _, part = self.refs(t)

            @pl.when(ok & self.tail)
            def _():
                copy(full, full, self.to_mate, t, mate).wait_recv()

            @pl.when(ok & self.away)
            def _():
                copy(part, part, self.to_next, t, mate).wait_recv()

            self.sends(t, ok, lambda c: c.start())

        def collect(self, t, ok):
            part = self.other(t)

            @pl.when(ok & self.away)
            def _():
                copy(part, part, self.back, t, mate).wait_recv()

    class DelayCast(Cast):
        def piece(self, t, c):
            return self.hold.at[pl.ds(pl.multiple_of(t * 256 + c * 128, 128), 128), :]

        def refs(self, t):
            full = self.hold.at[pl.ds(pl.multiple_of(t * 256, 256), 256), :]
            return full, full, self.piece(t, core), self.piece(t, core)

        def other(self, t):
            return self.piece(t, 1 - core)

    top = Cast(s0, sr, 0, 0, (top_mate, top_next, top_back))
    turns = DelayCast(td, td, 0, 0, (del_mate, del_next, del_back))

    zsrc, from_zero = col // 2, col % 2 == 0
    at_src = z == zsrc
    caster = at_src & (core == 1)
    guest = jnp.logical_not(at_src) & (core == 1)
    far_plus = (z - zsrc + 8) % 8
    far_minus = (zsrc - z + 8) % 8

    def side_sends(t, ok, way, act):
        j, _ = block_of(t)
        sems, target, far = ((col_plus, zplus, far_plus), (col_minus, zminus, far_minus))[way]
        part = half(sc, j, way)

        @pl.when(ok & caster & from_zero)
        def _():
            act(copy(part, part, sems, t, target))

        @pl.when(ok & caster & jnp.logical_not(from_zero))
        def _():
            act(copy(half(sr, j, way), part, sems, t, target))

        @pl.when(ok & guest & (far < 7))
        def _():
            act(copy(part, part, sems, t, target))

        @pl.when(ok & guest)
        def _():
            act(copy(part, part, col_back, 2 * t + way, mate))

    def side_step(m):
        full = rows(sc, block_of(m)[0])

        @pl.when(caster & from_zero & (m <= 15))
        def _():
            copy(full, full, col_mate, m, mate).wait_recv()

        for way, (sems, far) in enumerate(((col_plus, far_plus), (col_minus, far_minus))):
            t = m - 2 * far
            ok = (t >= 0) & (t <= 15)
            part = half(sc, block_of(t)[0], way)

            @pl.when(ok & guest)
            def _():
                copy(part, part, sems, t, mate).wait_recv()

            side_sends(t, ok, way, lambda c: c.start())

    def top_ok(t):
        return (t >= 0) & (t <= 15) & (block_of(t)[0] < TOP_BLOCKS)

    def turn_ok(t):
        return (t >= 0) & (t <= 1)

    @pl.when(row == 0)
    def _():
        keep_del.wait()

    keep_load.wait()
    keep_row.wait()
    pl.semaphore_wait(barrier, len(peers))

    def ring_slot(n):
        late = n - HOLD

        @pl.when(row == 0)
        def _():
            ring(n)

        @pl.when((row == 1) & (late % 2 == 0))
        def _():
            ring(late // 2)

        @pl.when((row >= 2) & ((2 * n) % 5 < 2))
        def _():
            ring((2 * n) // 5)

    def lead_slot(n, carry):
        ring_slot(n)
        t = n - 2 * top.far
        top.step(t, top_ok(t))
        turns.step(t, turn_ok(t))
        return carry

    lax.fori_loop(0, LEAD, lead_slot, 0)

    def top_in(t, carry):
        top.collect(t, top_ok(t))
        return carry

    lax.fori_loop(0, 16, top_in, 0)
    keep_top = pltpu.make_async_copy(sr.at[pl.ds(0, TOP_BLOCKS * SUB), :], s0, loc.at[0])

    @pl.when(top.head)
    def _():
        keep_top.start()
        keep_top.wait()

    upper, under = pl.ds(0, 2 * NB), pl.ds(2 * NB, 2 * NB)
    results = [
        copy(link, link, res, 0, mate),
        copy(inv.at[upper, :], inv.at[upper, :], res, 1, mate),
        copy(inv.at[under, :], inv.at[under, :], res, 2, mate),
    ]

    def col_in(t, carry):
        j, _ = block_of(t)
        full = rows(sc, j)

        @pl.when(at_src & jnp.logical_not(from_zero))
        def _():
            copy(full, full, col_mate, t, mate).wait_recv()

        @pl.when(jnp.logical_not(at_src))
        def _():
            for way in range(2):
                part = half(sc, j, way)
                copy(part, part, col_back, 2 * t + way, mate).wait_recv()

        return carry

    @pl.when(core == 0)
    def _():
        factor(
            s0, ld, low, link, inv, work,
            lambda k, i: ring_slot(LEAD + 8 * k + i),
            lambda: [c.start() for c in results[:2]],
        )
        lax.fori_loop(0, 16, col_in, 0)
        results[2].start()
        for c in results:
            c.wait_send()

    @pl.when(core == 1)
    def _():
        def side_slot(m, carry):
            ring_slot(LEAD + m)
            side_step(m)
            return carry

        lax.fori_loop(0, 30, side_slot, 0)
        for c in results:
            c.wait_recv()

    keep_col = pltpu.make_async_copy(sr, sc, loc.at[1])

    @pl.when(row == col)
    def _():
        keep_col.start()
        keep_col.wait()

    def tidy(t, carry):
        j, _ = block_of(t)
        both(t, lambda c: c.wait_send())
        top.sends(t, top_ok(t), lambda c: c.wait_send())
        for way in range(2):
            side_sends(t, t >= 0, way, lambda c: c.wait_send())
        turns.collect(t, turn_ok(t))
        turns.sends(t, turn_ok(t), lambda c: c.wait_send())

        @pl.when(row == col)
        def _():
            copy(rows(sr, j), rows(sc, j), col_mate, t, mate).wait_send()

        return carry

    lax.fori_loop(0, 16, tidy, 0)


def factor_block(tile, between):
    lanes = (8, NB)
    sub = lax.broadcasted_iota(jnp.int32, lanes, 0)
    col_id = lax.broadcasted_iota(jnp.int32, (NB, NB), 1)
    row_id = lax.broadcasted_iota(jnp.int32, (NB, NB), 0)
    rest = tile
    aug = jnp.where(row_id == col_id, 1.0, 0.0).astype(F32)
    inverse = []
    for i in range(NB // 8):
        top, eye = rest[:8], aug[:8]
        cols = [jnp.broadcast_to(top[:, 8 * i + b : 8 * i + b + 1], lanes) for b in range(8)]
        scales, rows_t, rows_e, links = [], [], [], []
        for j in range(8):
            scale = lax.rsqrt(jnp.broadcast_to(cols[j][j : j + 1], lanes))
            lower = cols[j] * scale
            below = jnp.where(sub > j, lower, 0.0)
            row_t = jnp.broadcast_to(top[j : j + 1], lanes) * scale
            row_e = jnp.broadcast_to(eye[j : j + 1], lanes) * scale
            top = jnp.where(sub == j, row_t, top - below * row_t)
            eye = jnp.where(sub == j, row_e, eye - below * row_e)
            link = {}
            for b in range(j + 1, 8):
                link[b] = jnp.broadcast_to(lower[b : b + 1], lanes)
                cols[b] = cols[b] - below * link[b]
            scales.append(scale)
            rows_t.append(row_t)
            rows_e.append(row_e)
            links.append(link)
        inverse.append(eye)
        if i % 2 == 1:
            between(i // 2)
        if i == NB // 8 - 1:
            break
        count = NB - 8 * (i + 1)
        rest, aug = rest[8:], aug[8:]
        full = (count, NB)

        def spread(value):
            return jnp.broadcast_to(value[None], (count // 8, 8, NB)).reshape(full)

        parts = [jnp.broadcast_to(rest[:, 8 * i + b : 8 * i + b + 1], full) for b in range(8)]
        for j in range(8):
            lower = parts[j] * spread(scales[j])
            rest = rest - lower * spread(rows_t[j])
            aug = aug - lower * spread(rows_e[j])
            for b in range(j + 1, 8):
                parts[b] = parts[b] - lower * spread(links[j][b])
    return jnp.concatenate(inverse, axis=0)


def factor(s0, load, low, link, inv, work, between, halfway):
    head = s0[:PANEL]
    ids = lax.broadcasted_iota(jnp.int32, (PANEL, PANEL), 0)
    diag = ids == lax.broadcasted_iota(jnp.int32, (PANEL, PANEL), 1)
    lane = jnp.concatenate([load[b : b + 1, :] for b in range(PANEL // NB)], axis=1)
    work[...] = dot_nt(head, head) * (1.0 / 1024) + jnp.where(diag, lane, 0.0)
    inv[...] = jnp.zeros_like(inv)

    def join(q):
        a, b, c = 2 * q * NB, (2 * q + 1) * NB, (2 * q + 2) * NB
        inner = dot_nn(low[b:c, a:b], inv[a:b, :NB], HI)
        inv[b:c, :NB] = -dot_nn(inv[b:c, NB:], inner, HI)

    def step(k, carry):
        at = pl.ds(pl.multiple_of(k * NB, NB), NB)
        inverse = factor_block(work[at, at], lambda i: between(k, i))
        inv[at, pl.ds(pl.multiple_of((k % 2) * NB, NB), NB)] = inverse
        panel = dot_nt(work[:, at], inverse, HI)
        below = lax.broadcasted_iota(jnp.int32, (PANEL, NB), 0) >= (k + 1) * NB
        panel = jnp.where(below, panel, 0.0)
        low[:, at] = panel
        work[...] = work[...] - dot_nt(panel, panel, HI)

        @pl.when(k == 1)
        def _():
            join(0)
            link[...] = low[2 * NB :, : 2 * NB]

        @pl.when(k == 2)
        def _():
            halfway()

        return carry

    lax.fori_loop(0, PANEL // NB, step, 0)
    join(1)


def gather(spectra, delays, load):
    vmem = pl.BlockSpec(memory_space=pltpu.VMEM)
    outside = pl.BlockSpec(memory_space=pltpu.HBM)
    dma = pltpu.SemaphoreType.DMA
    return pl.pallas_call(
        gather_kernel,
        out_shape=(
            jax.ShapeDtypeStruct((640, 2048), jnp.bfloat16),
            jax.ShapeDtypeStruct((640, 2048), jnp.bfloat16),
            jax.ShapeDtypeStruct((TOP_BLOCKS * SUB, 2048), jnp.bfloat16),
            jax.ShapeDtypeStruct((PANEL, 128), jnp.int32),
            jax.ShapeDtypeStruct((2 * NB, 2 * NB), F32),
            jax.ShapeDtypeStruct((PANEL, 2 * NB), F32),
        ),
        in_specs=[outside] * 3,
        out_specs=(vmem,) * 6,
        scratch_shapes=[pltpu.VMEM((PANEL, PANEL), F32)] * 2
        + [pltpu.VMEM((80, 128), F32), dma((3,))]
        + [dma((2, 16))] * 7
        + [dma((2, 32))]
        + [dma((2, 2))] * 3
        + [dma((2, 3))],
        compiler_params=pltpu.CompilerParams(
            collective_id=0, has_side_effects=True, vmem_limit_bytes=20 << 20
        ),
        name="gather_and_factor",
    )(spectra, delays, load)


def split(value):
    high = value.astype(jnp.bfloat16)
    return high, (value - high.astype(F32)).astype(jnp.bfloat16)


def three(dot, a, b):
    return dot(a[0], b[0]) + (dot(a[0], b[1]) + dot(a[1], b[0]))


def steer_of(delays, bin_value):
    phase = (delays * bin_value) & (NFFT - 1)
    turned = phase + NFFT // 8
    quad = (turned >> 9) & 3
    angle = ((turned & 511) - 256).astype(F32) * (6.283185307179586 / NFFT)
    sq = angle * angle
    cosine = 1.0 + sq * (-0.5 + sq * (1.0 / 24 + sq * (-1.0 / 720 + sq * (1.0 / 40320))))
    sine = angle * (1.0 + sq * (-1.0 / 6 + sq * (1.0 / 120 + sq * (-1.0 / 5040 + sq * (1.0 / 362880)))))
    swap = (quad & 1) == 1
    base_c = jnp.where(swap, sine, cosine)
    base_s = jnp.where(swap, cosine, sine)
    out_c = jnp.where((quad == 1) | (quad == 2), -base_c, base_c)
    out_s = jnp.where(quad >= 2, -base_s, base_s)
    return out_c, out_s


def finish_kernel(bins, sr, sc, s0, low, inv, load_far, dly_far, td, trail, panel, white, load, dly, sems):
    fetch = [
        pltpu.make_async_copy(load_far, load, sems.at[0]),
        pltpu.make_async_copy(dly_far, dly, sems.at[1]),
    ]
    for c in fetch:
        c.start()
    row, col = lax.axis_index("row"), lax.axis_index("col")
    head = s0[:PANEL]
    mid = 2 * NB
    inv_a, inv_b = split(inv[:mid]), split(inv[mid:])
    link = split(low[...])
    for c in fetch:
        c.wait()

    def lanes_of(index):
        return jnp.concatenate([load[pl.ds(index * 5 + b, 1), :] for b in range(5)], axis=1)

    def solve_rows(block, lane, is_first):
        base = dot_nt(block, head) * (1.0 / 1024)
        ids = lax.broadcasted_iota(jnp.int32, base.shape, 0)
        diag = ids == lax.broadcasted_iota(jnp.int32, base.shape, 1)
        base = base + jnp.where(diag & is_first, lane[:, :PANEL], 0.0)
        left = three(dot_nt, split(base[:, :mid]), inv_a)
        left_parts = split(left)
        right = base[:, mid:] - three(dot_nt, left_parts, link)
        right = three(dot_nt, split(right), inv_b)
        right_parts = split(right)
        whole = [jnp.concatenate([p, q], axis=1) for p, q in zip(left_parts, right_parts)]
        return jnp.concatenate([left, right], axis=1), whole

    lane_r = lanes_of(row)
    own, own_parts = solve_rows(sr[...], lane_r, row == 0)
    panel[...] = own
    _, other_parts = solve_rows(sc[...], lanes_of(col), col == 0)
    shape = (640, 640)
    ids_r = lax.broadcasted_iota(jnp.int32, shape, 0)
    ids_c = lax.broadcasted_iota(jnp.int32, shape, 1)
    tile = dot_nt(sr[...], sc[...]) * (1.0 / 1024)
    tile = tile + jnp.where((ids_r == ids_c) & (row == col), lane_r, 0.0)
    update = tile - three(dot_nt, own_parts, other_parts)
    keep = (ids_r + row * 640 >= PANEL) & (ids_c + col * 640 >= PANEL)
    trail[...] = jnp.where(keep, update, 0.0)

    upper = jnp.concatenate(steer_of(td[...], bins[0]), axis=1)
    first = three(dot_nn, inv_a, split(upper[:mid]))
    second = upper[mid:] - three(dot_nn, link, split(first))
    second = three(dot_nn, inv_b, split(second))
    solved = jnp.concatenate([first, second], axis=0)
    steer = jnp.concatenate(steer_of(dly[...], bins[0]), axis=1)
    lower = steer - three(dot_nn, own_parts, split(solved))
    padded = jnp.concatenate([solved, jnp.zeros((640 - PANEL, 256), F32)], axis=0)
    ids = lax.broadcasted_iota(jnp.int32, lower.shape, 0)
    stacked = jnp.where((ids < PANEL) & (row == 0), padded, lower)
    white[0] = stacked[:, :128]
    white[1] = stacked[:, 128:]


def finish(bins, sr, sc, s0, low, inv, load, delays, td):
    vmem = pl.BlockSpec(memory_space=pltpu.VMEM)
    smem = pl.BlockSpec(memory_space=pltpu.SMEM)
    outside = pl.BlockSpec(memory_space=pltpu.HBM)
    return pl.pallas_call(
        finish_kernel,
        out_shape=(
            jax.ShapeDtypeStruct((640, 640), F32),
            jax.ShapeDtypeStruct((640, PANEL), F32),
            jax.ShapeDtypeStruct((2, 640, 128), F32),
        ),
        in_specs=[smem] + [vmem] * 5 + [outside] * 2 + [vmem],
        out_specs=(vmem,) * 3,
        scratch_shapes=[
            pltpu.VMEM((80, 128), F32), pltpu.VMEM((640, 128), jnp.int32), pltpu.SemaphoreType.DMA((2,)),
        ],
        compiler_params=pltpu.CompilerParams(vmem_limit_bytes=36 << 20),
        name="finish_tiles",
    )(bins, sr, sc, s0, low, inv, load, delays, td)


def on_device(spectra, loading, delays, bin_index):
    load = loading.reshape(80, 128)
    sr, sc, s0, td, low, inv = gather(spectra, delays, load)
    return finish(bin_index, sr, sc, s0, low, inv, load, delays, td)


def solution(mesh):
    return jax.shard_map(
        on_device,
        mesh=mesh,
        in_specs=(P(("row", "col"), "freq"), P("freq"), P("row", "col"), P("freq")),
        out_specs=(
            P(("freq", "row"), "col"),
            P(("freq", "row"), None),
            P(None, ("freq", "row"), "col"),
        ),
        check_vma=False,
    )
```

```python
import jax
import jax.numpy as jnp
from jax import lax
from jax.experimental import pallas as pl
from jax.experimental.pallas import tpu as pltpu
from jax.sharding import PartitionSpec as P

PANEL = 512
NFFT = 2048
NB = 128
SUB = 40
F32 = jnp.float32
HI = lax.Precision.HIGHEST
MESH = pl.DeviceIdType.MESH
TOP_BLOCKS = 13
HOLD = 12
LEAD = 24
SIDE = 17


def dot_nt(a, b, precision=None):
    return lax.dot_general(
        a, b, (((1,), (1,)), ((), ())), precision=precision, preferred_element_type=F32
    )


def dot_nn(a, b, precision=None):
    return lax.dot_general(
        a, b, (((1,), (0,)), ((), ())), precision=precision, preferred_element_type=F32
    )


def gather_kernel(
    spec, dly, load, sr, sc, s0, td, link, inv, low, work, ld, loc, rings, top_mate, top_next, top_back,
    col_mate, col_plus, col_minus, col_back, del_mate, del_next, del_back, res
):
    row = lax.axis_index("row")
    col = lax.axis_index("col")
    z, core = row // 2, row % 2
    xh, y = col // 8, col % 8
    sgn = 1 - 2 * core

    def dev(z_, core_, xh_, y_):
        return {"row": z_ * 2 + core_, "col": xh_ * 8 + y_}

    mate = dev(z, 1 - core, xh, y)
    xmate = dev(z, core, 1 - xh, y)
    yplus = dev(z, core, xh, (y + 1) % 8)
    yminus = dev(z, core, xh, (y + 7) % 8)
    zplus = dev((z + 1) % 8, core, xh, y)
    zminus = dev((z + 7) % 8, core, xh, y)
    znext = dev((z + sgn + 8) % 8, core, xh, y)
    peers = (mate, xmate, yplus, yminus, zplus, zminus)

    keep_row = pltpu.make_async_copy(spec, sr.at[pl.ds(pl.multiple_of(col * SUB, 8), SUB), :], loc.at[0])
    keep_row.start()
    keep_del = pltpu.make_async_copy(dly.at[pl.ds(0, PANEL), :], td, loc.at[1])
    keep_load = pltpu.make_async_copy(load, ld, loc.at[2])
    keep_load.start()

    @pl.when(row == 0)
    def _():
        keep_del.start()

    barrier = pltpu.get_barrier_semaphore()
    for peer in peers:
        pl.semaphore_signal(barrier, inc=1, device_id=peer, device_id_type=MESH)

    def block_of(t):
        s, k = (t + 2) // 4, (t + 2) % 4
        d = (k % 2 + k // 2) % 2
        return ((xh + k % 2) % 2) * 8 + (y + (2 * d - 1) * s + 8) % 8, d

    def rows(ref, j):
        return ref.at[pl.ds(pl.multiple_of(j * SUB, 8), SUB), :]

    def half(ref, j, c):
        return ref.at[
            pl.ds(pl.multiple_of(j * SUB, 8), SUB), pl.ds(pl.multiple_of(c * 1024, 1024), 1024)
        ]

    def copy(src, dst, sems, index, target):
        return pltpu.make_async_remote_copy(
            src_ref=src,
            dst_ref=dst,
            send_sem=sems.at[0, index],
            recv_sem=sems.at[1, index],
            device_id=target,
            device_id_type=MESH,
        )

    def both(t, act):
        j, d = block_of(t)
        part = rows(sr, j)

        @pl.when(t == 0)
        def _():
            act(copy(part, part, rings, 1, xmate))
            act(copy(part, part, rings, 2, yplus))
            act(copy(part, part, rings, 4, yminus))

        @pl.when(t == 1)
        def _():
            act(copy(part, part, rings, 3, yminus))
            act(copy(part, part, rings, 5, yplus))

        @pl.when((t >= 2) & (t <= 11))
        def _():
            act(copy(part, part, rings, t + 4, dev(z, core, xh, (y + 1 - 2 * d + 8) % 8)))

    def ring(t):
        j, _ = block_of(t)
        part = rows(sr, j)

        @pl.when((t >= 1) & (t <= 15))
        def _():
            copy(part, part, rings, t, mate).wait_recv()

        both(t, lambda c: c.start())

        @pl.when((t >= 0) & (t <= 15) & (row == col))
        def _():
            copy(part, rows(sc, j), col_mate, t, mate).start()

    class Cast:
        def __init__(self, hold, origin, zsrc, qsrc, sems):
            self.hold, self.origin = hold, origin
            self.to_mate, self.to_next, self.back = sems
            at_src = z == zsrc
            self.head = at_src & (core == qsrc)
            self.tail = at_src & (core != qsrc)
            self.away = jnp.logical_not(at_src)
            self.far = (sgn * (z - zsrc) + 8) % 8

        def sends(self, t, ok, act):
            full_from, full_to, part_from, part_to = self.refs(t)

            @pl.when(ok & self.head)
            def _():
                act(copy(full_from, full_to, self.to_mate, t, mate))
                act(copy(part_from, part_to, self.to_next, t, znext))

            @pl.when(ok & self.tail)
            def _():
                act(copy(part_to, part_to, self.to_next, t, znext))

            @pl.when(ok & self.away)
            def _():
                act(copy(part_to, part_to, self.back, t, mate))

            @pl.when(ok & self.away & (self.far < 7))
            def _():
                act(copy(part_to, part_to, self.to_next, t, znext))

        def refs(self, t):
            j, _ = block_of(t)
            return rows(self.origin, j), rows(self.hold, j), half(self.origin, j, core), half(self.hold, j, core)

        def other(self, t):
            return half(self.hold, block_of(t)[0], 1 - core)

        def step(self, t, ok):
            _, full, _, part = self.refs(t)

            @pl.when(ok & self.tail)
            def _():
                copy(full, full, self.to_mate, t, mate).wait_recv()

            @pl.when(ok & self.away)
            def _():
                copy(part, part, self.to_next, t, mate).wait_recv()

            self.sends(t, ok, lambda c: c.start())

        def collect(self, t, ok):
            part = self.other(t)

            @pl.when(ok & self.away)
            def _():
                copy(part, part, self.back, t, mate).wait_recv()

    class DelayCast(Cast):
        def piece(self, t, c):
            return self.hold.at[pl.ds(pl.multiple_of(t * 256 + c * 128, 128), 128), :]

        def refs(self, t):
            full = self.hold.at[pl.ds(pl.multiple_of(t * 256, 256), 256), :]
            return full, full, self.piece(t, core), self.piece(t, core)

        def other(self, t):
            return self.piece(t, 1 - core)

    class HeadCast(Cast):
        def setup(self):
            limit = 4 - core
            self.member = self.away & (self.far <= limit)
            self.onward = self.away & (self.far < limit)
            self.guest = self.away & (self.far > limit)

        def sends(self, t, ok, act):
            j, _ = block_of(t)
            origin, part = rows(self.origin, j), rows(self.hold, j)

            @pl.when(ok & self.head)
            def _():
                act(copy(origin, part, self.to_next, t, znext))
                act(copy(origin, part, self.to_mate, t, mate))

            @pl.when(ok & (self.tail | self.onward))
            def _():
                act(copy(part, part, self.to_next, t, znext))

            @pl.when(ok & self.member)
            def _():
                act(copy(part, part, self.back, t, mate))

        def step(self, t, ok):
            part = rows(self.hold, block_of(t)[0])

            @pl.when(ok & self.tail)
            def _():
                copy(part, part, self.to_mate, t, mate).wait_recv()

            @pl.when(ok & self.member)
            def _():
                copy(part, part, self.to_next, t, mate).wait_recv()

            self.sends(t, ok, lambda c: c.start())

        def collect(self, t, ok):
            part = rows(self.hold, block_of(t)[0])

            @pl.when(ok & self.guest)
            def _():
                copy(part, part, self.back, t, mate).wait_recv()

    top = HeadCast(s0, sr, 0, 0, (top_mate, top_next, top_back))
    top.setup()
    turns = DelayCast(td, td, 0, 0, (del_mate, del_next, del_back))

    zsrc, from_zero = col // 2, col % 2 == 0
    at_src = z == zsrc
    caster = at_src & (core == 1)
    guest = jnp.logical_not(at_src) & (core == 1)
    far_plus = (z - zsrc + 8) % 8
    far_minus = (zsrc - z + 8) % 8

    def side_sends(t, ok, way, act):
        j, _ = block_of(t)
        sems, target, far = ((col_plus, zplus, far_plus), (col_minus, zminus, far_minus))[way]
        part = half(sc, j, way)

        @pl.when(ok & caster & from_zero)
        def _():
            act(copy(part, part, sems, t, target))

        @pl.when(ok & caster & jnp.logical_not(from_zero))
        def _():
            act(copy(half(sr, j, way), part, sems, t, target))

        @pl.when(ok & guest & (far < 7))
        def _():
            act(copy(part, part, sems, t, target))

        @pl.when(ok & guest)
        def _():
            act(copy(part, part, col_back, 2 * t + way, mate))

    def side_step(m):
        full = rows(sc, block_of(m)[0])

        @pl.when(caster & from_zero & (m >= 0) & (m <= 15))
        def _():
            copy(full, full, col_mate, m, mate).wait_recv()

        for way, (sems, far) in enumerate(((col_plus, far_plus), (col_minus, far_minus))):
            t = m - 2 * far
            ok = (t >= 0) & (t <= 15)
            part = half(sc, block_of(t)[0], way)

            @pl.when(ok & guest)
            def _():
                copy(part, part, sems, t, mate).wait_recv()

            side_sends(t, ok, way, lambda c: c.start())

    def top_ok(t):
        return (t >= 0) & (t <= 15) & (block_of(t)[0] < TOP_BLOCKS)

    def turn_ok(t):
        return (t >= 0) & (t <= 1)

    @pl.when(row == 0)
    def _():
        keep_del.wait()

    keep_load.wait()
    keep_row.wait()
    pl.semaphore_wait(barrier, len(peers))

    def ring_slot(n):
        late = n - HOLD

        @pl.when(row == 0)
        def _():
            ring(n)

        @pl.when((row == 1) & ((2 * late) % 3 < 2))
        def _():
            ring((2 * late) // 3)

        @pl.when((row >= 2) & ((3 * n) % 5 < 3))
        def _():
            ring((3 * n) // 5)

    slow = 3 * (col == 1).astype(jnp.int32)

    def lead_slot(n, carry):
        ring_slot(n)
        t = n - 2 * top.far
        top.step(t, top_ok(t))
        t = n - 2 * turns.far
        turns.step(t, turn_ok(t))

        @pl.when((core == 1) & (n >= SIDE))
        def _():
            side_step(n - SIDE - slow)

        return carry

    lax.fori_loop(0, LEAD, lead_slot, 0)

    def top_in(t, carry):
        top.collect(t, top_ok(t))
        return carry

    @pl.when(core == 0)
    def _():
        lax.fori_loop(0, 16, top_in, 0)

    keep_top = pltpu.make_async_copy(sr.at[pl.ds(0, TOP_BLOCKS * SUB), :], s0, loc.at[0])

    @pl.when(top.head)
    def _():
        keep_top.start()
        keep_top.wait()

    upper, under = pl.ds(0, 2 * NB), pl.ds(2 * NB, 2 * NB)
    results = [
        copy(link, link, res, 0, mate),
        copy(inv.at[upper, :], inv.at[upper, :], res, 1, mate),
        copy(inv.at[under, :], inv.at[under, :], res, 2, mate),
    ]

    def col_in(t, carry):
        j, _ = block_of(t)
        full = rows(sc, j)

        @pl.when(at_src & jnp.logical_not(from_zero))
        def _():
            copy(full, full, col_mate, t, mate).wait_recv()

        @pl.when(jnp.logical_not(at_src))
        def _():
            for way in range(2):
                part = half(sc, j, way)
                copy(part, part, col_back, 2 * t + way, mate).wait_recv()

        return carry

    def drain(t, carry):
        j, _ = block_of(t)
        both(t, lambda c: c.wait_send())
        top.sends(t, top_ok(t), lambda c: c.wait_send())

        @pl.when(turn_ok(t))
        def _():
            turns.collect(t, t >= 0)
            turns.sends(t, t >= 0, lambda c: c.wait_send())

        @pl.when(row == col)
        def _():
            copy(rows(sr, j), rows(sc, j), col_mate, t, mate).wait_send()

        return carry

    @pl.when(core == 0)
    def _():
        factor(
            s0, ld, low, link, inv, work,
            lambda k, i: ring_slot(LEAD + 8 * k + i),
            lambda: [c.start() for c in results[:2]],
        )
        lax.fori_loop(0, 16, drain, 0)
        results[2].start()
        lax.fori_loop(0, 16, col_in, 0)
        for c in results:
            c.wait_send()

    @pl.when(core == 1)
    def _():
        def side_slot(m, carry):
            ring_slot(m)
            side_step(m - SIDE - slow)
            return carry

        lax.fori_loop(LEAD, SIDE + 33, side_slot, 0)
        lax.fori_loop(0, 16, drain, 0)
        lax.fori_loop(0, 16, top_in, 0)
        for c in results:
            c.wait_recv()

    keep_col = pltpu.make_async_copy(sr, sc, loc.at[1])

    @pl.when(row == col)
    def _():
        keep_col.start()
        keep_col.wait()

    @pl.when(core == 1)
    def _():
        def tidy(t, carry):
            for way in range(2):
                side_sends(t, t >= 0, way, lambda c: c.wait_send())
            return carry

        lax.fori_loop(0, 16, tidy, 0)


def factor_block(tile, between):
    lanes = (8, NB)
    sub = lax.broadcasted_iota(jnp.int32, lanes, 0)
    col_id = lax.broadcasted_iota(jnp.int32, (NB, NB), 1)
    row_id = lax.broadcasted_iota(jnp.int32, (NB, NB), 0)
    rest = tile
    aug = jnp.where(row_id == col_id, 1.0, 0.0).astype(F32)
    inverse = []
    for i in range(NB // 8):
        top, eye = rest[:8], aug[:8]
        cols = [jnp.broadcast_to(top[:, 8 * i + b : 8 * i + b + 1], lanes) for b in range(8)]
        scales, rows_t, rows_e, links = [], [], [], []
        for j in range(8):
            scale = lax.rsqrt(jnp.broadcast_to(cols[j][j : j + 1], lanes))
            lower = cols[j] * scale
            below = jnp.where(sub > j, lower, 0.0)
            row_t = jnp.broadcast_to(top[j : j + 1], lanes) * scale
            row_e = jnp.broadcast_to(eye[j : j + 1], lanes) * scale
            top = jnp.where(sub == j, row_t, top - below * row_t)
            eye = jnp.where(sub == j, row_e, eye - below * row_e)
            link = {}
            for b in range(j + 1, 8):
                link[b] = jnp.broadcast_to(lower[b : b + 1], lanes)
                cols[b] = cols[b] - below * link[b]
            scales.append(scale)
            rows_t.append(row_t)
            rows_e.append(row_e)
            links.append(link)
        inverse.append(eye)
        if i % 2 == 1:
            between(i // 2)
        if i == NB // 8 - 1:
            break
        count = NB - 8 * (i + 1)
        rest, aug = rest[8:], aug[8:]
        full = (count, NB)

        def spread(value):
            return jnp.broadcast_to(value[None], (count // 8, 8, NB)).reshape(full)

        parts = [jnp.broadcast_to(rest[:, 8 * i + b : 8 * i + b + 1], full) for b in range(8)]
        for j in range(8):
            lower = parts[j] * spread(scales[j])
            rest = rest - lower * spread(rows_t[j])
            aug = aug - lower * spread(rows_e[j])
            for b in range(j + 1, 8):
                parts[b] = parts[b] - lower * spread(links[j][b])
    return jnp.concatenate(inverse, axis=0)


def factor(s0, load, low, link, inv, work, between, halfway):
    head = s0[:PANEL]
    ids = lax.broadcasted_iota(jnp.int32, (PANEL, PANEL), 0)
    diag = ids == lax.broadcasted_iota(jnp.int32, (PANEL, PANEL), 1)
    lane = jnp.concatenate([load[b : b + 1, :] for b in range(PANEL // NB)], axis=1)
    work[...] = dot_nt(head, head) * (1.0 / 1024) + jnp.where(diag, lane, 0.0)
    inv[...] = jnp.zeros_like(inv)

    def join(q):
        a, b, c = 2 * q * NB, (2 * q + 1) * NB, (2 * q + 2) * NB
        inner = dot_nn(low[b:c, a:b], inv[a:b, :NB], HI)
        inv[b:c, :NB] = -dot_nn(inv[b:c, NB:], inner, HI)

    def step(k, carry):
        at = pl.ds(pl.multiple_of(k * NB, NB), NB)
        inverse = factor_block(work[at, at], lambda i: between(k, i))
        inv[at, pl.ds(pl.multiple_of((k % 2) * NB, NB), NB)] = inverse
        panel = dot_nt(work[:, at], inverse, HI)
        below = lax.broadcasted_iota(jnp.int32, (PANEL, NB), 0) >= (k + 1) * NB
        panel = jnp.where(below, panel, 0.0)
        low[:, at] = panel
        work[...] = work[...] - dot_nt(panel, panel, HI)

        @pl.when(k == 1)
        def _():
            join(0)
            link[...] = low[2 * NB :, : 2 * NB]

        @pl.when(k == 2)
        def _():
            halfway()

        return carry

    lax.fori_loop(0, PANEL // NB, step, 0)
    join(1)


def gather(spectra, delays, load):
    vmem = pl.BlockSpec(memory_space=pltpu.VMEM)
    outside = pl.BlockSpec(memory_space=pltpu.HBM)
    dma = pltpu.SemaphoreType.DMA
    return pl.pallas_call(
        gather_kernel,
        out_shape=(
            jax.ShapeDtypeStruct((640, 2048), jnp.bfloat16),
            jax.ShapeDtypeStruct((640, 2048), jnp.bfloat16),
            jax.ShapeDtypeStruct((TOP_BLOCKS * SUB, 2048), jnp.bfloat16),
            jax.ShapeDtypeStruct((PANEL, 128), jnp.int32),
            jax.ShapeDtypeStruct((2 * NB, 2 * NB), F32),
            jax.ShapeDtypeStruct((PANEL, 2 * NB), F32),
        ),
        in_specs=[outside] * 3,
        out_specs=(vmem,) * 6,
        scratch_shapes=[pltpu.VMEM((PANEL, PANEL), F32)] * 2
        + [pltpu.VMEM((80, 128), F32), dma((3,))]
        + [dma((2, 16))] * 7
        + [dma((2, 32))]
        + [dma((2, 2))] * 3
        + [dma((2, 3))],
        compiler_params=pltpu.CompilerParams(
            collective_id=0, has_side_effects=True, vmem_limit_bytes=20 << 20
        ),
        name="gather_and_factor",
    )(spectra, delays, load)


def split(value):
    high = value.astype(jnp.bfloat16)
    return high, (value - high.astype(F32)).astype(jnp.bfloat16)


def three(dot, a, b):
    return dot(a[0], b[0]) + (dot(a[0], b[1]) + dot(a[1], b[0]))


def steer_of(delays, bin_value):
    phase = (delays * bin_value) & (NFFT - 1)
    turned = phase + NFFT // 8
    quad = (turned >> 9) & 3
    angle = ((turned & 511) - 256).astype(F32) * (6.283185307179586 / NFFT)
    sq = angle * angle
    cosine = 1.0 + sq * (-0.5 + sq * (1.0 / 24 + sq * (-1.0 / 720 + sq * (1.0 / 40320))))
    sine = angle * (1.0 + sq * (-1.0 / 6 + sq * (1.0 / 120 + sq * (-1.0 / 5040 + sq * (1.0 / 362880)))))
    swap = (quad & 1) == 1
    base_c = jnp.where(swap, sine, cosine)
    base_s = jnp.where(swap, cosine, sine)
    out_c = jnp.where((quad == 1) | (quad == 2), -base_c, base_c)
    out_s = jnp.where(quad >= 2, -base_s, base_s)
    return out_c, out_s


def finish_kernel(bins, sr, sc, s0, low, inv, load_far, dly_far, td, trail, panel, white, load, dly, sems):
    fetch = [
        pltpu.make_async_copy(load_far, load, sems.at[0]),
        pltpu.make_async_copy(dly_far, dly, sems.at[1]),
    ]
    for c in fetch:
        c.start()
    row, col = lax.axis_index("row"), lax.axis_index("col")
    head = s0[:PANEL]
    mid = 2 * NB
    inv_a, inv_b = split(inv[:mid]), split(inv[mid:])
    link = split(low[...])
    for c in fetch:
        c.wait()

    def lanes_of(index):
        return jnp.concatenate([load[pl.ds(index * 5 + b, 1), :] for b in range(5)], axis=1)

    def solve_rows(block, lane, is_first):
        base = dot_nt(block, head) * (1.0 / 1024)
        ids = lax.broadcasted_iota(jnp.int32, base.shape, 0)
        diag = ids == lax.broadcasted_iota(jnp.int32, base.shape, 1)
        base = base + jnp.where(diag & is_first, lane[:, :PANEL], 0.0)
        left = three(dot_nt, split(base[:, :mid]), inv_a)
        left_parts = split(left)
        right = base[:, mid:] - three(dot_nt, left_parts, link)
        right = three(dot_nt, split(right), inv_b)
        right_parts = split(right)
        whole = [jnp.concatenate([p, q], axis=1) for p, q in zip(left_parts, right_parts)]
        return jnp.concatenate([left, right], axis=1), whole

    lane_r = lanes_of(row)
    own, own_parts = solve_rows(sr[...], lane_r, row == 0)
    panel[...] = own
    _, other_parts = solve_rows(sc[...], lanes_of(col), col == 0)
    shape = (640, 640)
    ids_r = lax.broadcasted_iota(jnp.int32, shape, 0)
    ids_c = lax.broadcasted_iota(jnp.int32, shape, 1)
    tile = dot_nt(sr[...], sc[...]) * (1.0 / 1024)
    tile = tile + jnp.where((ids_r == ids_c) & (row == col), lane_r, 0.0)
    update = tile - three(dot_nt, own_parts, other_parts)
    keep = (ids_r + row * 640 >= PANEL) & (ids_c + col * 640 >= PANEL)
    trail[...] = jnp.where(keep, update, 0.0)

    upper = jnp.concatenate(steer_of(td[...], bins[0]), axis=1)
    first = three(dot_nn, inv_a, split(upper[:mid]))
    second = upper[mid:] - three(dot_nn, link, split(first))
    second = three(dot_nn, inv_b, split(second))
    solved = jnp.concatenate([first, second], axis=0)
    steer = jnp.concatenate(steer_of(dly[...], bins[0]), axis=1)
    lower = steer - three(dot_nn, own_parts, split(solved))
    padded = jnp.concatenate([solved, jnp.zeros((640 - PANEL, 256), F32)], axis=0)
    ids = lax.broadcasted_iota(jnp.int32, lower.shape, 0)
    stacked = jnp.where((ids < PANEL) & (row == 0), padded, lower)
    white[0] = stacked[:, :128]
    white[1] = stacked[:, 128:]


def finish(bins, sr, sc, s0, low, inv, load, delays, td):
    vmem = pl.BlockSpec(memory_space=pltpu.VMEM)
    smem = pl.BlockSpec(memory_space=pltpu.SMEM)
    outside = pl.BlockSpec(memory_space=pltpu.HBM)
    return pl.pallas_call(
        finish_kernel,
        out_shape=(
            jax.ShapeDtypeStruct((640, 640), F32),
            jax.ShapeDtypeStruct((640, PANEL), F32),
            jax.ShapeDtypeStruct((2, 640, 128), F32),
        ),
        in_specs=[smem] + [vmem] * 5 + [outside] * 2 + [vmem],
        out_specs=(vmem,) * 3,
        scratch_shapes=[
            pltpu.VMEM((80, 128), F32), pltpu.VMEM((640, 128), jnp.int32), pltpu.SemaphoreType.DMA((2,)),
        ],
        compiler_params=pltpu.CompilerParams(vmem_limit_bytes=36 << 20),
        name="finish_tiles",
    )(bins, sr, sc, s0, low, inv, load, delays, td)


def on_device(spectra, loading, delays, bin_index):
    load = pltpu.with_memory_space_constraint(loading.reshape(80, 128), pltpu.HBM)
    spectra = pltpu.with_memory_space_constraint(spectra, pltpu.HBM)
    delays = pltpu.with_memory_space_constraint(delays, pltpu.HBM)
    sr, sc, s0, td, low, inv = gather(spectra, delays, load)
    return finish(bin_index, sr, sc, s0, low, inv, load, delays, td)


def solution(mesh):
    return jax.shard_map(
        on_device,
        mesh=mesh,
        in_specs=(P(("row", "col"), "freq"), P("freq"), P("row", "col"), P("freq")),
        out_specs=(
            P(("freq", "row"), "col"),
            P(("freq", "row"), None),
            P(None, ("freq", "row"), "col"),
        ),
        check_vma=False,
    )
```

```python
import jax
import jax.numpy as jnp
from jax import lax
from jax.experimental import pallas as pl
from jax.experimental.pallas import tpu as pltpu
from jax.sharding import PartitionSpec as P

PANEL = 512
NFFT = 2048
NB = 128
SUB = 40
F32 = jnp.float32
HI = lax.Precision.HIGHEST
MESH = pl.DeviceIdType.MESH
TOP_BLOCKS = 13
HOLD = 12
LEAD = 24
SIDE = 17


def dot_nt(a, b, precision=None):
    return lax.dot_general(
        a, b, (((1,), (1,)), ((), ())), precision=precision, preferred_element_type=F32
    )


def dot_nn(a, b, precision=None):
    return lax.dot_general(
        a, b, (((1,), (0,)), ((), ())), precision=precision, preferred_element_type=F32
    )


def gather_kernel(
    spec, dly, load, sr, sc, s0, td, link, inv, low, work, ld, loc, rings, top_mate, top_next, top_back,
    col_mate, col_plus, col_minus, col_back, del_mate, del_next, del_back, res
):
    row = lax.axis_index("row")
    col = lax.axis_index("col")
    z, core = row // 2, row % 2
    xh, y = col // 8, col % 8
    sgn = 1 - 2 * core

    def dev(z_, core_, xh_, y_):
        return {"row": z_ * 2 + core_, "col": xh_ * 8 + y_}

    mate = dev(z, 1 - core, xh, y)
    xmate = dev(z, core, 1 - xh, y)
    yplus = dev(z, core, xh, (y + 1) % 8)
    yminus = dev(z, core, xh, (y + 7) % 8)
    zplus = dev((z + 1) % 8, core, xh, y)
    zminus = dev((z + 7) % 8, core, xh, y)
    znext = dev((z + sgn + 8) % 8, core, xh, y)
    peers = (mate, xmate, yplus, yminus, zplus, zminus)

    keep_row = pltpu.make_async_copy(spec, sr.at[pl.ds(pl.multiple_of(col * SUB, 8), SUB), :], loc.at[0])
    keep_row.start()
    keep_del = pltpu.make_async_copy(dly.at[pl.ds(0, PANEL), :], td, loc.at[1])
    keep_load = pltpu.make_async_copy(load, ld, loc.at[2])
    keep_load.start()

    @pl.when(row == 0)
    def _():
        keep_del.start()

    barrier = pltpu.get_barrier_semaphore()
    for peer in peers:
        pl.semaphore_signal(barrier, inc=1, device_id=peer, device_id_type=MESH)

    def block_of(t):
        s, k = (t + 2) // 4, (t + 2) % 4
        d = (k % 2 + k // 2) % 2
        return ((xh + k % 2) % 2) * 8 + (y + (2 * d - 1) * s + 8) % 8, d

    def rows(ref, j):
        return ref.at[pl.ds(pl.multiple_of(j * SUB, 8), SUB), :]

    def half(ref, j, c):
        return ref.at[
            pl.ds(pl.multiple_of(j * SUB, 8), SUB), pl.ds(pl.multiple_of(c * 1024, 1024), 1024)
        ]

    def copy(src, dst, sems, index, target):
        return pltpu.make_async_remote_copy(
            src_ref=src,
            dst_ref=dst,
            send_sem=sems.at[0, index],
            recv_sem=sems.at[1, index],
            device_id=target,
            device_id_type=MESH,
        )

    def both(t, act):
        j, d = block_of(t)
        part = rows(sr, j)

        @pl.when(t == 0)
        def _():
            act(copy(part, part, rings, 1, xmate))
            act(copy(part, part, rings, 2, yplus))
            act(copy(part, part, rings, 4, yminus))

        @pl.when(t == 1)
        def _():
            act(copy(part, part, rings, 3, yminus))
            act(copy(part, part, rings, 5, yplus))

        @pl.when((t >= 2) & (t <= 11))
        def _():
            act(copy(part, part, rings, t + 4, dev(z, core, xh, (y + 1 - 2 * d + 8) % 8)))

    def ring(t):
        j, _ = block_of(t)
        part = rows(sr, j)

        @pl.when((t >= 1) & (t <= 15))
        def _():
            copy(part, part, rings, t, mate).wait_recv()

        both(t, lambda c: c.start())

        @pl.when((t >= 0) & (t <= 15) & (row == col))
        def _():
            copy(part, rows(sc, j), col_mate, t, mate).start()

    class Cast:
        def __init__(self, hold, origin, zsrc, qsrc, sems):
            self.hold, self.origin = hold, origin
            self.to_mate, self.to_next, self.back = sems
            at_src = z == zsrc
            self.head = at_src & (core == qsrc)
            self.tail = at_src & (core != qsrc)
            self.away = jnp.logical_not(at_src)
            self.far = (sgn * (z - zsrc) + 8) % 8

        def sends(self, t, ok, act):
            full_from, full_to, part_from, part_to = self.refs(t)

            @pl.when(ok & self.head)
            def _():
                act(copy(full_from, full_to, self.to_mate, t, mate))
                act(copy(part_from, part_to, self.to_next, t, znext))

            @pl.when(ok & self.tail)
            def _():
                act(copy(part_to, part_to, self.to_next, t, znext))

            @pl.when(ok & self.away)
            def _():
                act(copy(part_to, part_to, self.back, t, mate))

            @pl.when(ok & self.away & (self.far < 7))
            def _():
                act(copy(part_to, part_to, self.to_next, t, znext))

        def refs(self, t):
            j, _ = block_of(t)
            return rows(self.origin, j), rows(self.hold, j), half(self.origin, j, core), half(self.hold, j, core)

        def other(self, t):
            return half(self.hold, block_of(t)[0], 1 - core)

        def step(self, t, ok):
            _, full, _, part = self.refs(t)

            @pl.when(ok & self.tail)
            def _():
                copy(full, full, self.to_mate, t, mate).wait_recv()

            @pl.when(ok & self.away)
            def _():
                copy(part, part, self.to_next, t, mate).wait_recv()

            self.sends(t, ok, lambda c: c.start())

        def collect(self, t, ok):
            part = self.other(t)

            @pl.when(ok & self.away)
            def _():
                copy(part, part, self.back, t, mate).wait_recv()

    class DelayCast(Cast):
        def piece(self, t, c):
            return self.hold.at[pl.ds(pl.multiple_of(t * 256 + c * 128, 128), 128), :]

        def refs(self, t):
            full = self.hold.at[pl.ds(pl.multiple_of(t * 256, 256), 256), :]
            return full, full, self.piece(t, core), self.piece(t, core)

        def other(self, t):
            return self.piece(t, 1 - core)

    class HeadCast(Cast):
        def setup(self):
            limit = 4 - core
            self.member = self.away & (self.far <= limit)
            self.onward = self.away & (self.far < limit)
            self.guest = self.away & (self.far > limit)

        def sends(self, t, ok, act):
            j, _ = block_of(t)
            origin, part = rows(self.origin, j), rows(self.hold, j)

            @pl.when(ok & self.head)
            def _():
                act(copy(origin, part, self.to_next, t, znext))
                act(copy(origin, part, self.to_mate, t, mate))

            @pl.when(ok & (self.tail | self.onward))
            def _():
                act(copy(part, part, self.to_next, t, znext))

            @pl.when(ok & self.member)
            def _():
                act(copy(part, part, self.back, t, mate))

        def step(self, t, ok):
            part = rows(self.hold, block_of(t)[0])

            @pl.when(ok & self.tail)
            def _():
                copy(part, part, self.to_mate, t, mate).wait_recv()

            @pl.when(ok & self.member)
            def _():
                copy(part, part, self.to_next, t, mate).wait_recv()

            self.sends(t, ok, lambda c: c.start())

        def collect(self, t, ok):
            part = rows(self.hold, block_of(t)[0])

            @pl.when(ok & self.guest)
            def _():
                copy(part, part, self.back, t, mate).wait_recv()

    top = HeadCast(s0, sr, 0, 0, (top_mate, top_next, top_back))
    top.setup()
    turns = DelayCast(td, td, 0, 0, (del_mate, del_next, del_back))

    zsrc, from_zero = col // 2, col % 2 == 0
    at_src = z == zsrc
    caster = at_src & (core == 1)
    guest = jnp.logical_not(at_src) & (core == 1)
    far_plus = (z - zsrc + 8) % 8
    far_minus = (zsrc - z + 8) % 8

    def side_sends(t, ok, way, act):
        j, _ = block_of(t)
        sems, target, far = ((col_plus, zplus, far_plus), (col_minus, zminus, far_minus))[way]
        part = half(sc, j, way)

        @pl.when(ok & caster & from_zero)
        def _():
            act(copy(part, part, sems, t, target))

        @pl.when(ok & caster & jnp.logical_not(from_zero))
        def _():
            act(copy(half(sr, j, way), part, sems, t, target))

        @pl.when(ok & guest & (far < 7))
        def _():
            act(copy(part, part, sems, t, target))

        @pl.when(ok & guest)
        def _():
            act(copy(part, part, col_back, 2 * t + way, mate))

    def side_step(m):
        full = rows(sc, block_of(m)[0])

        @pl.when(caster & from_zero & (m >= 0) & (m <= 15))
        def _():
            copy(full, full, col_mate, m, mate).wait_recv()

        for way, (sems, far) in enumerate(((col_plus, far_plus), (col_minus, far_minus))):
            t = m - 2 * far
            ok = (t >= 0) & (t <= 15)
            part = half(sc, block_of(t)[0], way)

            @pl.when(ok & guest)
            def _():
                copy(part, part, sems, t, mate).wait_recv()

            side_sends(t, ok, way, lambda c: c.start())

    def top_ok(t):
        return (t >= 0) & (t <= 15) & (block_of(t)[0] < TOP_BLOCKS)

    def turn_ok(t):
        return (t >= 0) & (t <= 1)

    @pl.when(row == 0)
    def _():
        keep_del.wait()

    keep_load.wait()
    keep_row.wait()
    pl.semaphore_wait(barrier, len(peers))

    def ring_slot(n):
        late = n - HOLD

        @pl.when(row == 0)
        def _():
            ring(n)

        @pl.when((row == 1) & ((2 * late) % 3 < 2))
        def _():
            ring((2 * late) // 3)

        @pl.when((row >= 2) & ((3 * n) % 5 < 3))
        def _():
            ring((3 * n) // 5)

    held = (zsrc >= 1) & (zsrc <= 3)
    side_at = SIDE + 3 * (col == 1).astype(jnp.int32) + (LEAD - SIDE) * held.astype(jnp.int32)

    def lead_slot(n, carry):
        ring_slot(n)
        t = n - 2 * top.far
        top.step(t, top_ok(t))
        t = n - 2 * turns.far
        turns.step(t, turn_ok(t))

        @pl.when((core == 1) & (n >= SIDE))
        def _():
            side_step(n - side_at)

        return carry

    lax.fori_loop(0, LEAD, lead_slot, 0)

    def top_in(t, carry):
        top.collect(t, top_ok(t))
        return carry

    @pl.when(core == 0)
    def _():
        lax.fori_loop(0, 16, top_in, 0)

    keep_top = pltpu.make_async_copy(sr.at[pl.ds(0, TOP_BLOCKS * SUB), :], s0, loc.at[0])

    @pl.when(top.head)
    def _():
        keep_top.start()
        keep_top.wait()

    upper, under = pl.ds(0, 2 * NB), pl.ds(2 * NB, 2 * NB)
    results = [
        copy(link, link, res, 0, mate),
        copy(inv.at[upper, :], inv.at[upper, :], res, 1, mate),
        copy(inv.at[under, :], inv.at[under, :], res, 2, mate),
    ]

    def col_in(t, carry):
        j, _ = block_of(t)
        full = rows(sc, j)

        @pl.when(at_src & jnp.logical_not(from_zero))
        def _():
            copy(full, full, col_mate, t, mate).wait_recv()

        @pl.when(jnp.logical_not(at_src))
        def _():
            for way in range(2):
                part = half(sc, j, way)
                copy(part, part, col_back, 2 * t + way, mate).wait_recv()

        return carry

    def drain(t, carry):
        j, _ = block_of(t)
        both(t, lambda c: c.wait_send())
        top.sends(t, top_ok(t), lambda c: c.wait_send())

        @pl.when(turn_ok(t))
        def _():
            turns.collect(t, t >= 0)
            turns.sends(t, t >= 0, lambda c: c.wait_send())

        @pl.when(row == col)
        def _():
            copy(rows(sr, j), rows(sc, j), col_mate, t, mate).wait_send()

        return carry

    @pl.when(core == 0)
    def _():
        factor(
            s0, ld, low, link, inv, work,
            lambda k, i: ring_slot(LEAD + 8 * k + i),
            lambda: [c.start() for c in results[:2]],
        )
        lax.fori_loop(0, 16, drain, 0)
        results[2].start()
        lax.fori_loop(0, 16, col_in, 0)
        for c in results:
            c.wait_send()

    @pl.when(core == 1)
    def _():
        def side_slot(m, carry):
            ring_slot(m)
            side_step(m - side_at)
            return carry

        @pl.when(caster & held)
        def _():
            lax.fori_loop(0, 16, top_in, 0)

        lax.fori_loop(LEAD, LEAD + 31, side_slot, 0)
        lax.fori_loop(0, 16, drain, 0)

        @pl.when(jnp.logical_not(caster & held))
        def _():
            lax.fori_loop(0, 16, top_in, 0)

        for c in results:
            c.wait_recv()

    keep_col = pltpu.make_async_copy(sr, sc, loc.at[1])

    @pl.when(row == col)
    def _():
        keep_col.start()
        keep_col.wait()

    @pl.when(core == 1)
    def _():
        def tidy(t, carry):
            for way in range(2):
                side_sends(t, t >= 0, way, lambda c: c.wait_send())
            return carry

        lax.fori_loop(0, 16, tidy, 0)


def factor_block(tile, between):
    lanes = (8, NB)
    sub = lax.broadcasted_iota(jnp.int32, lanes, 0)
    col_id = lax.broadcasted_iota(jnp.int32, (NB, NB), 1)
    row_id = lax.broadcasted_iota(jnp.int32, (NB, NB), 0)
    rest = tile
    aug = jnp.where(row_id == col_id, 1.0, 0.0).astype(F32)
    inverse = []
    for i in range(NB // 8):
        top, eye = rest[:8], aug[:8]
        cols = [jnp.broadcast_to(top[:, 8 * i + b : 8 * i + b + 1], lanes) for b in range(8)]
        scales, rows_t, rows_e, links = [], [], [], []
        for j in range(8):
            scale = lax.rsqrt(jnp.broadcast_to(cols[j][j : j + 1], lanes))
            lower = cols[j] * scale
            below = jnp.where(sub > j, lower, 0.0)
            row_t = jnp.broadcast_to(top[j : j + 1], lanes) * scale
            row_e = jnp.broadcast_to(eye[j : j + 1], lanes) * scale
            top = jnp.where(sub == j, row_t, top - below * row_t)
            eye = jnp.where(sub == j, row_e, eye - below * row_e)
            link = {}
            for b in range(j + 1, 8):
                link[b] = jnp.broadcast_to(lower[b : b + 1], lanes)
                cols[b] = cols[b] - below * link[b]
            scales.append(scale)
            rows_t.append(row_t)
            rows_e.append(row_e)
            links.append(link)
        inverse.append(eye)
        if i % 2 == 1:
            between(i // 2)
        if i == NB // 8 - 1:
            break
        count = NB - 8 * (i + 1)
        rest, aug = rest[8:], aug[8:]
        full = (count, NB)

        def spread(value):
            return jnp.broadcast_to(value[None], (count // 8, 8, NB)).reshape(full)

        parts = [jnp.broadcast_to(rest[:, 8 * i + b : 8 * i + b + 1], full) for b in range(8)]
        for j in range(8):
            lower = parts[j] * spread(scales[j])
            rest = rest - lower * spread(rows_t[j])
            aug = aug - lower * spread(rows_e[j])
            for b in range(j + 1, 8):
                parts[b] = parts[b] - lower * spread(links[j][b])
    return jnp.concatenate(inverse, axis=0)


def factor(s0, load, low, link, inv, work, between, halfway):
    head = s0[:PANEL]
    ids = lax.broadcasted_iota(jnp.int32, (PANEL, PANEL), 0)
    diag = ids == lax.broadcasted_iota(jnp.int32, (PANEL, PANEL), 1)
    lane = jnp.concatenate([load[b : b + 1, :] for b in range(PANEL // NB)], axis=1)
    work[...] = dot_nt(head, head) * (1.0 / 1024) + jnp.where(diag, lane, 0.0)
    inv[...] = jnp.zeros_like(inv)

    def join(q):
        a, b, c = 2 * q * NB, (2 * q + 1) * NB, (2 * q + 2) * NB
        inner = dot_nn(low[b:c, a:b], inv[a:b, :NB], HI)
        inv[b:c, :NB] = -dot_nn(inv[b:c, NB:], inner, HI)

    def step(k, carry):
        at = pl.ds(pl.multiple_of(k * NB, NB), NB)
        inverse = factor_block(work[at, at], lambda i: between(k, i))
        inv[at, pl.ds(pl.multiple_of((k % 2) * NB, NB), NB)] = inverse
        for now in range(PANEL // NB - 1):
            here, rest = slice(now * NB, (now + 1) * NB), slice((now + 1) * NB, PANEL)

            @pl.when(k == now)
            def _():
                panel = dot_nt(work[rest, here], inverse, HI)
                low[rest, here] = panel
                work[rest, rest] = work[rest, rest] - dot_nt(panel, panel, HI)

        @pl.when(k == 1)
        def _():
            join(0)
            link[...] = low[2 * NB :, : 2 * NB]

        @pl.when(k == 2)
        def _():
            halfway()

        return carry

    lax.fori_loop(0, PANEL // NB, step, 0)
    join(1)


def gather(spectra, delays, load):
    vmem = pl.BlockSpec(memory_space=pltpu.VMEM)
    outside = pl.BlockSpec(memory_space=pltpu.HBM)
    dma = pltpu.SemaphoreType.DMA
    return pl.pallas_call(
        gather_kernel,
        out_shape=(
            jax.ShapeDtypeStruct((640, 2048), jnp.bfloat16),
            jax.ShapeDtypeStruct((640, 2048), jnp.bfloat16),
            jax.ShapeDtypeStruct((TOP_BLOCKS * SUB, 2048), jnp.bfloat16),
            jax.ShapeDtypeStruct((PANEL, 128), jnp.int32),
            jax.ShapeDtypeStruct((2 * NB, 2 * NB), F32),
            jax.ShapeDtypeStruct((PANEL, 2 * NB), F32),
        ),
        in_specs=[outside] * 3,
        out_specs=(vmem,) * 6,
        scratch_shapes=[pltpu.VMEM((PANEL, PANEL), F32)] * 2
        + [pltpu.VMEM((80, 128), F32), dma((3,))]
        + [dma((2, 16))] * 7
        + [dma((2, 32))]
        + [dma((2, 2))] * 3
        + [dma((2, 3))],
        compiler_params=pltpu.CompilerParams(
            collective_id=0, has_side_effects=True, vmem_limit_bytes=20 << 20
        ),
        name="gather_and_factor",
    )(spectra, delays, load)


def split(value):
    high = value.astype(jnp.bfloat16)
    return high, (value - high.astype(F32)).astype(jnp.bfloat16)


def three(dot, a, b):
    return dot(a[0], b[0]) + (dot(a[0], b[1]) + dot(a[1], b[0]))


def steer_of(delays, bin_value):
    phase = (delays * bin_value) & (NFFT - 1)
    turned = phase + NFFT // 8
    quad = (turned >> 9) & 3
    angle = ((turned & 511) - 256).astype(F32) * (6.283185307179586 / NFFT)
    sq = angle * angle
    cosine = 1.0 + sq * (-0.5 + sq * (1.0 / 24 + sq * (-1.0 / 720 + sq * (1.0 / 40320))))
    sine = angle * (1.0 + sq * (-1.0 / 6 + sq * (1.0 / 120 + sq * (-1.0 / 5040 + sq * (1.0 / 362880)))))
    swap = (quad & 1) == 1
    base_c = jnp.where(swap, sine, cosine)
    base_s = jnp.where(swap, cosine, sine)
    out_c = jnp.where((quad == 1) | (quad == 2), -base_c, base_c)
    out_s = jnp.where(quad >= 2, -base_s, base_s)
    return out_c, out_s


def finish_kernel(bins, sr, sc, s0, low, inv, load_far, dly_far, td, trail, panel, white, load, dly, sems):
    fetch = [
        pltpu.make_async_copy(load_far, load, sems.at[0]),
        pltpu.make_async_copy(dly_far, dly, sems.at[1]),
    ]
    for c in fetch:
        c.start()
    row, col = lax.axis_index("row"), lax.axis_index("col")
    head = s0[:PANEL]
    mid = 2 * NB
    inv_a, inv_b = split(inv[:mid]), split(inv[mid:])
    link = split(low[...])
    fetch[0].wait()

    def lanes_of(index):
        return jnp.concatenate([load[pl.ds(index * 5 + b, 1), :] for b in range(5)], axis=1)

    def solve_rows(block, lane, is_first):
        base = dot_nt(block, head) * (1.0 / 1024)
        ids = lax.broadcasted_iota(jnp.int32, base.shape, 0)
        diag = ids == lax.broadcasted_iota(jnp.int32, base.shape, 1)
        base = base + jnp.where(diag & is_first, lane[:, :PANEL], 0.0)
        left = three(dot_nt, split(base[:, :mid]), inv_a)
        left_parts = split(left)
        right = base[:, mid:] - three(dot_nt, left_parts, link)
        right = three(dot_nt, split(right), inv_b)
        right_parts = split(right)
        whole = [jnp.concatenate([p, q], axis=1) for p, q in zip(left_parts, right_parts)]
        return jnp.concatenate([left, right], axis=1), whole

    lane_r = lanes_of(row)
    own, own_parts = solve_rows(sr[...], lane_r, row == 0)
    panel[...] = own
    _, other_parts = solve_rows(sc[...], lanes_of(col), col == 0)
    shape = (640, 640)
    ids_r = lax.broadcasted_iota(jnp.int32, shape, 0)
    ids_c = lax.broadcasted_iota(jnp.int32, shape, 1)
    tile = dot_nt(sr[...], sc[...]) * (1.0 / 1024)
    tile = tile + jnp.where((ids_r == ids_c) & (row == col), lane_r, 0.0)
    update = tile - three(dot_nt, own_parts, other_parts)
    keep = (ids_r + row * 640 >= PANEL) & (ids_c + col * 640 >= PANEL)
    trail[...] = jnp.where(keep, update, 0.0)

    upper = jnp.concatenate(steer_of(td[...], bins[0]), axis=1)
    first = three(dot_nn, inv_a, split(upper[:mid]))
    second = upper[mid:] - three(dot_nn, link, split(first))
    second = three(dot_nn, inv_b, split(second))
    solved = jnp.concatenate([first, second], axis=0)
    fetch[1].wait()
    steer = jnp.concatenate(steer_of(dly[...], bins[0]), axis=1)
    lower = steer - three(dot_nn, own_parts, split(solved))
    padded = jnp.concatenate([solved, jnp.zeros((640 - PANEL, 256), F32)], axis=0)
    ids = lax.broadcasted_iota(jnp.int32, lower.shape, 0)
    stacked = jnp.where((ids < PANEL) & (row == 0), padded, lower)
    white[0] = stacked[:, :128]
    white[1] = stacked[:, 128:]


def finish(bins, sr, sc, s0, low, inv, load, delays, td):
    vmem = pl.BlockSpec(memory_space=pltpu.VMEM)
    smem = pl.BlockSpec(memory_space=pltpu.SMEM)
    outside = pl.BlockSpec(memory_space=pltpu.HBM)
    return pl.pallas_call(
        finish_kernel,
        out_shape=(
            jax.ShapeDtypeStruct((640, 640), F32),
            jax.ShapeDtypeStruct((640, PANEL), F32),
            jax.ShapeDtypeStruct((2, 640, 128), F32),
        ),
        in_specs=[smem] + [vmem] * 5 + [outside] * 2 + [vmem],
        out_specs=(vmem,) * 3,
        scratch_shapes=[
            pltpu.VMEM((80, 128), F32), pltpu.VMEM((640, 128), jnp.int32), pltpu.SemaphoreType.DMA((2,)),
        ],
        compiler_params=pltpu.CompilerParams(vmem_limit_bytes=36 << 20),
        name="finish_tiles",
    )(bins, sr, sc, s0, low, inv, load, delays, td)


def on_device(spectra, loading, delays, bin_index):
    load = pltpu.with_memory_space_constraint(loading.reshape(80, 128), pltpu.HBM)
    spectra = pltpu.with_memory_space_constraint(spectra, pltpu.HBM)
    delays = pltpu.with_memory_space_constraint(delays, pltpu.HBM)
    sr, sc, s0, td, low, inv = gather(spectra, delays, load)
    return finish(bin_index, sr, sc, s0, low, inv, load, delays, td)


def solution(mesh):
    return jax.shard_map(
        on_device,
        mesh=mesh,
        in_specs=(P(("row", "col"), "freq"), P("freq"), P("row", "col"), P("freq")),
        out_specs=(
            P(("freq", "row"), "col"),
            P(("freq", "row"), None),
            P(None, ("freq", "row"), "col"),
        ),
        check_vma=False,
    )
```

```python
import jax
import jax.numpy as jnp
from jax import lax
from jax.experimental import pallas as pl
from jax.experimental.pallas import tpu as pltpu
from jax.sharding import PartitionSpec as P

PANEL = 512
NFFT = 2048
NB = 128
SUB = 40
F32 = jnp.float32
HI = lax.Precision.HIGHEST
MESH = pl.DeviceIdType.MESH
TOP_BLOCKS = 13
HOLD = 12
LEAD = 24
SIDE = 17


def dot_nt(a, b, precision=None):
    return lax.dot_general(
        a, b, (((1,), (1,)), ((), ())), precision=precision, preferred_element_type=F32
    )


def dot_nn(a, b, precision=None):
    return lax.dot_general(
        a, b, (((1,), (0,)), ((), ())), precision=precision, preferred_element_type=F32
    )


def gather_kernel(
    spec, dly, load, sr, sc, s0, td, link, inv, ld, low, work, loc, rings, top_mate, top_next, top_back,
    col_mate, col_plus, col_minus, col_back, del_mate, del_next, del_back, res
):
    row = lax.axis_index("row")
    col = lax.axis_index("col")
    z, core = row // 2, row % 2
    xh, y = col // 8, col % 8
    sgn = 1 - 2 * core

    def dev(z_, core_, xh_, y_):
        return {"row": z_ * 2 + core_, "col": xh_ * 8 + y_}

    mate = dev(z, 1 - core, xh, y)
    xmate = dev(z, core, 1 - xh, y)
    yplus = dev(z, core, xh, (y + 1) % 8)
    yminus = dev(z, core, xh, (y + 7) % 8)
    zplus = dev((z + 1) % 8, core, xh, y)
    zminus = dev((z + 7) % 8, core, xh, y)
    znext = dev((z + sgn + 8) % 8, core, xh, y)
    peers = (mate, xmate, yplus, yminus, zplus, zminus)

    keep_row = pltpu.make_async_copy(spec, sr.at[pl.ds(pl.multiple_of(col * SUB, 8), SUB), :], loc.at[0])
    keep_row.start()
    keep_del = pltpu.make_async_copy(dly.at[pl.ds(0, PANEL), :], td, loc.at[1])
    keep_load = pltpu.make_async_copy(load, ld, loc.at[2])
    keep_load.start()

    @pl.when(row == 0)
    def _():
        keep_del.start()

    barrier = pltpu.get_barrier_semaphore()
    for peer in peers:
        pl.semaphore_signal(barrier, inc=1, device_id=peer, device_id_type=MESH)

    def block_of(t):
        s, k = (t + 2) // 4, (t + 2) % 4
        d = (k % 2 + k // 2) % 2
        return ((xh + k % 2) % 2) * 8 + (y + (2 * d - 1) * s + 8) % 8, d

    def rows(ref, j):
        return ref.at[pl.ds(pl.multiple_of(j * SUB, 8), SUB), :]

    def half(ref, j, c):
        return ref.at[
            pl.ds(pl.multiple_of(j * SUB, 8), SUB), pl.ds(pl.multiple_of(c * 1024, 1024), 1024)
        ]

    def copy(src, dst, sems, index, target):
        return pltpu.make_async_remote_copy(
            src_ref=src,
            dst_ref=dst,
            send_sem=sems.at[0, index],
            recv_sem=sems.at[1, index],
            device_id=target,
            device_id_type=MESH,
        )

    def both(t, q, act):
        j, d = block_of(t)
        part = half(sr, j, q)

        @pl.when(t == 0)
        def _():
            act(copy(part, part, rings, 2 + q, xmate))
            act(copy(part, part, rings, 4 + q, yplus))
            act(copy(part, part, rings, 8 + q, yminus))

        @pl.when(t == 1)
        def _():
            act(copy(part, part, rings, 6 + q, yminus))
            act(copy(part, part, rings, 10 + q, yplus))

        @pl.when((t >= 2) & (t <= 11))
        def _():
            act(copy(part, part, rings, 2 * t + 8 + q, dev(z, core, xh, (y + 1 - 2 * d + 8) % 8)))

    def ring(t):
        j, _ = block_of(t)
        for q in range(2):
            @pl.when((t >= 1) & (t <= 15))
            def _():
                copy(half(sr, j, q), half(sr, j, q), rings, 2 * t + q, mate).wait_recv()

            both(t, q, lambda c: c.start())

        part = rows(sr, j)

        @pl.when((t >= 0) & (t <= 15) & (row == col))
        def _():
            copy(part, rows(sc, j), col_mate, t, mate).start()

    class Cast:
        def __init__(self, hold, origin, zsrc, qsrc, sems):
            self.hold, self.origin = hold, origin
            self.to_mate, self.to_next, self.back = sems
            at_src = z == zsrc
            self.head = at_src & (core == qsrc)
            self.tail = at_src & (core != qsrc)
            self.away = jnp.logical_not(at_src)
            self.far = (sgn * (z - zsrc) + 8) % 8

        def sends(self, t, ok, act):
            full_from, full_to, part_from, part_to = self.refs(t)

            @pl.when(ok & self.head)
            def _():
                act(copy(full_from, full_to, self.to_mate, t, mate))
                act(copy(part_from, part_to, self.to_next, t, znext))

            @pl.when(ok & self.tail)
            def _():
                act(copy(part_to, part_to, self.to_next, t, znext))

            @pl.when(ok & self.away)
            def _():
                act(copy(part_to, part_to, self.back, t, mate))

            @pl.when(ok & self.away & (self.far < 7))
            def _():
                act(copy(part_to, part_to, self.to_next, t, znext))

        def refs(self, t):
            j, _ = block_of(t)
            return rows(self.origin, j), rows(self.hold, j), half(self.origin, j, core), half(self.hold, j, core)

        def other(self, t):
            return half(self.hold, block_of(t)[0], 1 - core)

        def step(self, t, ok):
            _, full, _, part = self.refs(t)

            @pl.when(ok & self.tail)
            def _():
                copy(full, full, self.to_mate, t, mate).wait_recv()

            @pl.when(ok & self.away)
            def _():
                copy(part, part, self.to_next, t, mate).wait_recv()

            self.sends(t, ok, lambda c: c.start())

        def collect(self, t, ok):
            part = self.other(t)

            @pl.when(ok & self.away)
            def _():
                copy(part, part, self.back, t, mate).wait_recv()

    class DelayCast(Cast):
        def piece(self, t, c):
            return self.hold.at[pl.ds(pl.multiple_of(t * 256 + c * 128, 128), 128), :]

        def refs(self, t):
            full = self.hold.at[pl.ds(pl.multiple_of(t * 256, 256), 256), :]
            return full, full, self.piece(t, core), self.piece(t, core)

        def other(self, t):
            return self.piece(t, 1 - core)

    class HeadCast(Cast):
        def setup(self):
            limit = 4 - core
            self.member = self.away & (self.far <= limit)
            self.onward = self.away & (self.far < limit)
            self.guest = self.away & (self.far > limit)

        def sends(self, t, ok, act, q):
            j, _ = block_of(t)
            origin, part = half(self.origin, j, q), half(self.hold, j, q)
            at = 2 * t + q

            @pl.when(ok & self.head)
            def _():
                act(copy(origin, part, self.to_next, at, znext))
                act(copy(origin, part, self.to_mate, at, mate))

            @pl.when(ok & (self.tail | self.onward))
            def _():
                act(copy(part, part, self.to_next, at, znext))

            @pl.when(ok & self.member)
            def _():
                act(copy(part, part, self.back, at, mate))

        def step(self, t, ok):
            for q in range(2):
                part, at = half(self.hold, block_of(t)[0], q), 2 * t + q

                @pl.when(ok & self.tail)
                def _():
                    copy(part, part, self.to_mate, at, mate).wait_recv()

                @pl.when(ok & self.member)
                def _():
                    copy(part, part, self.to_next, at, mate).wait_recv()

                self.sends(t, ok, lambda c: c.start(), q)

        def collect(self, t, ok):
            for q in range(2):
                part = half(self.hold, block_of(t)[0], q)

                @pl.when(ok & self.guest)
                def _():
                    copy(part, part, self.back, 2 * t + q, mate).wait_recv()

    top = HeadCast(s0, sr, 0, 0, (top_mate, top_next, top_back))
    top.setup()
    turns = DelayCast(td, td, 0, 0, (del_mate, del_next, del_back))

    zsrc, from_zero = col // 2, col % 2 == 0
    at_src = z == zsrc
    caster = at_src & (core == 1)
    guest = jnp.logical_not(at_src) & (core == 1)
    far_plus = (z - zsrc + 8) % 8
    far_minus = (zsrc - z + 8) % 8

    def side_sends(t, ok, way, act):
        j, _ = block_of(t)
        sems, target, far = ((col_plus, zplus, far_plus), (col_minus, zminus, far_minus))[way]
        part = half(sc, j, way)

        @pl.when(ok & caster & from_zero)
        def _():
            act(copy(part, part, sems, t, target))

        @pl.when(ok & caster & jnp.logical_not(from_zero))
        def _():
            act(copy(half(sr, j, way), part, sems, t, target))

        @pl.when(ok & guest & (far < 7))
        def _():
            act(copy(part, part, sems, t, target))

        @pl.when(ok & guest)
        def _():
            act(copy(part, part, col_back, 2 * t + way, mate))

    held = ((zsrc >= 1) & (zsrc <= 3)).astype(jnp.int32)
    minus_at = SIDE + 3 * (col == 1).astype(jnp.int32)
    plus_at = minus_at + 2 * zsrc * held

    def side_step(n):
        m = n - minus_at
        full = rows(sc, block_of(m)[0])

        @pl.when(caster & from_zero & (m >= 0) & (m <= 15))
        def _():
            copy(full, full, col_mate, m, mate).wait_recv()

        ways = ((col_plus, far_plus, plus_at), (col_minus, far_minus, minus_at))
        for way, (sems, far, start) in enumerate(ways):
            t = n - start - 2 * far
            ok = (t >= 0) & (t <= 15)
            part = half(sc, block_of(t)[0], way)

            @pl.when(ok & guest)
            def _():
                copy(part, part, sems, t, mate).wait_recv()

            side_sends(t, ok, way, lambda c: c.start())

    def side_slot(n):
        t = n - 2 * z - 1
        top.collect(t, top_ok(t))
        side_step(n)

    def top_ok(t):
        return (t >= 0) & (t <= 15) & (block_of(t)[0] < TOP_BLOCKS)

    def turn_ok(t):
        return (t >= 0) & (t <= 1)

    @pl.when(row == 0)
    def _():
        keep_del.wait()

    keep_load.wait()
    keep_row.wait()
    pl.semaphore_wait(barrier, len(peers))

    def ring_slot(n):
        late = n - HOLD

        @pl.when(row == 0)
        def _():
            ring(n)

        @pl.when((row == 1) & ((2 * late) % 3 < 2))
        def _():
            ring((2 * late) // 3)

        @pl.when((row >= 2) & ((3 * n) % 5 < 3))
        def _():
            ring((3 * n) // 5)

    def lead_slot(n, carry):
        ring_slot(n)
        t = n - 2 * top.far
        top.step(t, top_ok(t))
        t = n - 2 * turns.far
        turns.step(t, turn_ok(t))

        @pl.when(core == 1)
        def _():
            side_slot(n)

        return carry

    lax.fori_loop(0, LEAD, lead_slot, 0)

    def top_in(t, carry):
        top.collect(t, top_ok(t))
        return carry

    @pl.when(core == 0)
    def _():
        lax.fori_loop(0, 16, top_in, 0)

    keep_top = pltpu.make_async_copy(sr.at[pl.ds(0, TOP_BLOCKS * SUB), :], s0, loc.at[0])

    @pl.when(top.head)
    def _():
        keep_top.start()
        keep_top.wait()

    upper, under = pl.ds(0, 2 * NB), pl.ds(2 * NB, 2 * NB)
    results = [
        copy(link, link, res, 0, mate),
        copy(inv.at[upper, :], inv.at[upper, :], res, 1, mate),
        copy(inv.at[under, :], inv.at[under, :], res, 2, mate),
    ]

    def col_in(t, carry):
        j, _ = block_of(t)
        full = rows(sc, j)

        @pl.when(at_src & jnp.logical_not(from_zero))
        def _():
            copy(full, full, col_mate, t, mate).wait_recv()

        @pl.when(jnp.logical_not(at_src))
        def _():
            for way in range(2):
                part = half(sc, j, way)
                copy(part, part, col_back, 2 * t + way, mate).wait_recv()

        return carry

    def drain(t, carry):
        j, _ = block_of(t)
        for q in range(2):
            both(t, q, lambda c: c.wait_send())
            top.sends(t, top_ok(t), lambda c: c.wait_send(), q)


        @pl.when(turn_ok(t))
        def _():
            turns.collect(t, t >= 0)
            turns.sends(t, t >= 0, lambda c: c.wait_send())

        @pl.when(row == col)
        def _():
            copy(rows(sr, j), rows(sc, j), col_mate, t, mate).wait_send()

        return carry

    @pl.when(core == 0)
    def _():
        factor(
            s0, ld, low, link, inv, work,
            lambda k, i: ring_slot(LEAD + 8 * k + i),
            lambda: [c.start() for c in results[:2]],
        )
        lax.fori_loop(0, 16, drain, 0)
        results[2].start()
        lax.fori_loop(0, 16, col_in, 0)
        for c in results:
            c.wait_send()

    @pl.when(core == 1)
    def _():
        def later_slot(n, carry):
            ring_slot(n)
            side_slot(n)
            return carry

        lax.fori_loop(LEAD, LEAD + 31, later_slot, 0)
        lax.fori_loop(0, 16, drain, 0)
        for c in results:
            c.wait_recv()

    keep_col = pltpu.make_async_copy(sr, sc, loc.at[1])

    @pl.when(row == col)
    def _():
        keep_col.start()
        keep_col.wait()

    @pl.when(core == 1)
    def _():
        def tidy(t, carry):
            for way in range(2):
                side_sends(t, t >= 0, way, lambda c: c.wait_send())
            return carry

        lax.fori_loop(0, 16, tidy, 0)


def factor_block(tile, between):
    lanes = (8, NB)
    sub = lax.broadcasted_iota(jnp.int32, lanes, 0)
    col_id = lax.broadcasted_iota(jnp.int32, (NB, NB), 1)
    row_id = lax.broadcasted_iota(jnp.int32, (NB, NB), 0)
    rest = tile
    aug = jnp.where(row_id == col_id, 1.0, 0.0).astype(F32)
    inverse = []
    for i in range(NB // 8):
        top, eye = rest[:8], aug[:8]
        cols = [jnp.broadcast_to(top[:, 8 * i + b : 8 * i + b + 1], lanes) for b in range(8)]
        scales, rows_t, rows_e, links = [], [], [], []
        for j in range(8):
            scale = lax.rsqrt(jnp.broadcast_to(cols[j][j : j + 1], lanes))
            lower = cols[j] * scale
            below = jnp.where(sub > j, lower, 0.0)
            row_t = jnp.broadcast_to(top[j : j + 1], lanes) * scale
            row_e = jnp.broadcast_to(eye[j : j + 1], lanes) * scale
            top = jnp.where(sub == j, row_t, top - below * row_t)
            eye = jnp.where(sub == j, row_e, eye - below * row_e)
            link = {}
            for b in range(j + 1, 8):
                link[b] = jnp.broadcast_to(lower[b : b + 1], lanes)
                cols[b] = cols[b] - below * link[b]
            scales.append(scale)
            rows_t.append(row_t)
            rows_e.append(row_e)
            links.append(link)
        inverse.append(eye)
        if i % 2 == 1:
            between(i // 2)
        if i == NB // 8 - 1:
            break
        count = NB - 8 * (i + 1)
        rest, aug = rest[8:], aug[8:]
        full = (count, NB)

        def spread(value):
            return jnp.broadcast_to(value[None], (count // 8, 8, NB)).reshape(full)

        parts = [jnp.broadcast_to(rest[:, 8 * i + b : 8 * i + b + 1], full) for b in range(8)]
        for j in range(8):
            lower = parts[j] * spread(scales[j])
            rest = rest - lower * spread(rows_t[j])
            aug = aug - lower * spread(rows_e[j])
            for b in range(j + 1, 8):
                parts[b] = parts[b] - lower * spread(links[j][b])
    return jnp.concatenate(inverse, axis=0)


def factor(s0, load, low, link, inv, work, between, halfway):
    head = s0[:PANEL]
    ids = lax.broadcasted_iota(jnp.int32, (PANEL, PANEL), 0)
    diag = ids == lax.broadcasted_iota(jnp.int32, (PANEL, PANEL), 1)
    lane = jnp.concatenate([load[b : b + 1, :] for b in range(PANEL // NB)], axis=1)
    work[...] = dot_nt(head, head) * (1.0 / 1024) + jnp.where(diag, lane, 0.0)
    inv[...] = jnp.zeros_like(inv)

    def join(q):
        a, b, c = 2 * q * NB, (2 * q + 1) * NB, (2 * q + 2) * NB
        inner = dot_nn(low[b:c, a:b], inv[a:b, :NB], HI)
        inv[b:c, :NB] = -dot_nn(inv[b:c, NB:], inner, HI)

    def step(k, carry):
        at = pl.ds(pl.multiple_of(k * NB, NB), NB)
        inverse = factor_block(work[at, at], lambda i: between(k, i))
        inv[at, pl.ds(pl.multiple_of((k % 2) * NB, NB), NB)] = inverse
        for now in range(PANEL // NB - 1):
            here, rest = slice(now * NB, (now + 1) * NB), slice((now + 1) * NB, PANEL)

            @pl.when(k == now)
            def _():
                panel = dot_nt(work[rest, here], inverse, HI)
                low[rest, here] = panel
                work[rest, rest] = work[rest, rest] - dot_nt(panel, panel, HI)

        @pl.when(k == 1)
        def _():
            join(0)
            link[...] = low[2 * NB :, : 2 * NB]

        @pl.when(k == 2)
        def _():
            halfway()

        return carry

    lax.fori_loop(0, PANEL // NB, step, 0)
    join(1)


def gather(spectra, delays, load):
    vmem = pl.BlockSpec(memory_space=pltpu.VMEM)
    outside = pl.BlockSpec(memory_space=pltpu.HBM)
    dma = pltpu.SemaphoreType.DMA
    return pl.pallas_call(
        gather_kernel,
        out_shape=(
            jax.ShapeDtypeStruct((640, 2048), jnp.bfloat16),
            jax.ShapeDtypeStruct((640, 2048), jnp.bfloat16),
            jax.ShapeDtypeStruct((TOP_BLOCKS * SUB, 2048), jnp.bfloat16),
            jax.ShapeDtypeStruct((PANEL, 128), jnp.int32),
            jax.ShapeDtypeStruct((2 * NB, 2 * NB), F32),
            jax.ShapeDtypeStruct((PANEL, 2 * NB), F32),
            jax.ShapeDtypeStruct((80, 128), F32),
        ),
        in_specs=[outside] * 3,
        out_specs=(vmem,) * 7,
        scratch_shapes=[pltpu.VMEM((PANEL, PANEL), F32)] * 2
        + [dma((3,))]
        + [dma((2, 32))] * 4
        + [dma((2, 16))] * 3
        + [dma((2, 32))]
        + [dma((2, 2))] * 3
        + [dma((2, 3))],
        compiler_params=pltpu.CompilerParams(
            collective_id=0, has_side_effects=True, vmem_limit_bytes=20 << 20
        ),
        name="gather_and_factor",
    )(spectra, delays, load)


def split(value):
    high = value.astype(jnp.bfloat16)
    return high, (value - high.astype(F32)).astype(jnp.bfloat16)


def three(dot, a, b):
    return dot(a[0], b[0]) + (dot(a[0], b[1]) + dot(a[1], b[0]))


def steer_of(delays, bin_value):
    phase = (delays * bin_value) & (NFFT - 1)
    turned = phase + NFFT // 8
    quad = (turned >> 9) & 3
    angle = ((turned & 511) - 256).astype(F32) * (6.283185307179586 / NFFT)
    sq = angle * angle
    cosine = 1.0 + sq * (-0.5 + sq * (1.0 / 24 + sq * (-1.0 / 720 + sq * (1.0 / 40320))))
    sine = angle * (1.0 + sq * (-1.0 / 6 + sq * (1.0 / 120 + sq * (-1.0 / 5040 + sq * (1.0 / 362880)))))
    swap = (quad & 1) == 1
    base_c = jnp.where(swap, sine, cosine)
    base_s = jnp.where(swap, cosine, sine)
    out_c = jnp.where((quad == 1) | (quad == 2), -base_c, base_c)
    out_s = jnp.where(quad >= 2, -base_s, base_s)
    return out_c, out_s


def finish_kernel(bins, sr, sc, s0, low, inv, load, td, dly_far, trail, panel, white, dly, sem):
    fetch = pltpu.make_async_copy(dly_far, dly, sem)
    fetch.start()
    row, col = lax.axis_index("row"), lax.axis_index("col")
    head = s0[:PANEL]
    mid = 2 * NB
    inv_a, inv_b = split(inv[:mid]), split(inv[mid:])
    link = split(low[...])

    def lanes_of(index):
        return jnp.concatenate([load[pl.ds(index * 5 + b, 1), :] for b in range(5)], axis=1)

    def solve_rows(block, lane, is_first):
        base = dot_nt(block, head) * (1.0 / 1024)
        ids = lax.broadcasted_iota(jnp.int32, base.shape, 0)
        diag = ids == lax.broadcasted_iota(jnp.int32, base.shape, 1)
        base = base + jnp.where(diag & is_first, lane[:, :PANEL], 0.0)
        left = three(dot_nt, split(base[:, :mid]), inv_a)
        left_parts = split(left)
        right = base[:, mid:] - three(dot_nt, left_parts, link)
        right = three(dot_nt, split(right), inv_b)
        right_parts = split(right)
        whole = [jnp.concatenate([p, q], axis=1) for p, q in zip(left_parts, right_parts)]
        return jnp.concatenate([left, right], axis=1), whole

    lane_r = lanes_of(row)
    own, own_parts = solve_rows(sr[...], lane_r, row == 0)
    panel[...] = own
    _, other_parts = solve_rows(sc[...], lanes_of(col), col == 0)
    shape = (640, 640)
    ids_r = lax.broadcasted_iota(jnp.int32, shape, 0)
    ids_c = lax.broadcasted_iota(jnp.int32, shape, 1)
    tile = dot_nt(sr[...], sc[...]) * (1.0 / 1024)
    tile = tile + jnp.where((ids_r == ids_c) & (row == col), lane_r, 0.0)
    update = tile - three(dot_nt, own_parts, other_parts)
    keep = (ids_r + row * 640 >= PANEL) & (ids_c + col * 640 >= PANEL)
    trail[...] = jnp.where(keep, update, 0.0)

    upper = jnp.concatenate(steer_of(td[...], bins[0]), axis=1)
    first = three(dot_nn, inv_a, split(upper[:mid]))
    second = upper[mid:] - three(dot_nn, link, split(first))
    second = three(dot_nn, inv_b, split(second))
    solved = jnp.concatenate([first, second], axis=0)
    fetch.wait()
    steer = jnp.concatenate(steer_of(dly[...], bins[0]), axis=1)
    lower = steer - three(dot_nn, own_parts, split(solved))
    padded = jnp.concatenate([solved, jnp.zeros((640 - PANEL, 256), F32)], axis=0)
    ids = lax.broadcasted_iota(jnp.int32, lower.shape, 0)
    stacked = jnp.where((ids < PANEL) & (row == 0), padded, lower)
    white[0] = stacked[:, :128]
    white[1] = stacked[:, 128:]


def finish(bins, sr, sc, s0, low, inv, load, td, delays):
    vmem = pl.BlockSpec(memory_space=pltpu.VMEM)
    smem = pl.BlockSpec(memory_space=pltpu.SMEM)
    outside = pl.BlockSpec(memory_space=pltpu.HBM)
    return pl.pallas_call(
        finish_kernel,
        out_shape=(
            jax.ShapeDtypeStruct((640, 640), F32),
            jax.ShapeDtypeStruct((640, PANEL), F32),
            jax.ShapeDtypeStruct((2, 640, 128), F32),
        ),
        in_specs=[smem] + [vmem] * 7 + [outside],
        out_specs=(vmem,) * 3,
        scratch_shapes=[pltpu.VMEM((640, 128), jnp.int32), pltpu.SemaphoreType.DMA(())],
        compiler_params=pltpu.CompilerParams(vmem_limit_bytes=36 << 20),
        name="finish_tiles",
    )(bins, sr, sc, s0, low, inv, load, td, delays)


def on_device(spectra, loading, delays, bin_index):
    load = pltpu.with_memory_space_constraint(loading.reshape(80, 128), pltpu.HBM)
    spectra = pltpu.with_memory_space_constraint(spectra, pltpu.HBM)
    delays = pltpu.with_memory_space_constraint(delays, pltpu.HBM)
    sr, sc, s0, td, low, inv, lanes = gather(spectra, delays, load)
    return finish(bin_index, sr, sc, s0, low, inv, lanes, td, delays)


def solution(mesh):
    return jax.shard_map(
        on_device,
        mesh=mesh,
        in_specs=(P(("row", "col"), "freq"), P("freq"), P("row", "col"), P("freq")),
        out_specs=(
            P(("freq", "row"), "col"),
            P(("freq", "row"), None),
            P(None, ("freq", "row"), "col"),
        ),
        check_vma=False,
    )
```

```python
import jax
import jax.numpy as jnp
from jax import lax
from jax.experimental import pallas as pl
from jax.experimental.pallas import tpu as pltpu
from jax.sharding import PartitionSpec as P

PANEL = 512
NFFT = 2048
NB = 128
SUB = 40
F32 = jnp.float32
HI = lax.Precision.HIGHEST
MESH = pl.DeviceIdType.MESH
TOP_BLOCKS = 13
HOLD = 12
LEAD = 24
SIDE = 17


def dot_nt(a, b, precision=None):
    return lax.dot_general(
        a, b, (((1,), (1,)), ((), ())), precision=precision, preferred_element_type=F32
    )


def dot_nn(a, b, precision=None):
    return lax.dot_general(
        a, b, (((1,), (0,)), ((), ())), precision=precision, preferred_element_type=F32
    )


def gather_kernel(
    spec, dly, load, sr, sc, s0, td, link, inv, ld, low, work, loc, rings, top_mate, top_next, top_back,
    col_mate, col_plus, col_minus, col_back, del_mate, del_next, del_back, res
):
    row = lax.axis_index("row")
    col = lax.axis_index("col")
    z, core = row // 2, row % 2
    xh, y = col // 8, col % 8
    sgn = 1 - 2 * core

    def dev(z_, core_, xh_, y_):
        return {"row": z_ * 2 + core_, "col": xh_ * 8 + y_}

    mate = dev(z, 1 - core, xh, y)
    xmate = dev(z, core, 1 - xh, y)
    yplus = dev(z, core, xh, (y + 1) % 8)
    yminus = dev(z, core, xh, (y + 7) % 8)
    zplus = dev((z + 1) % 8, core, xh, y)
    zminus = dev((z + 7) % 8, core, xh, y)
    znext = dev((z + sgn + 8) % 8, core, xh, y)
    peers = (mate, xmate, yplus, yminus, zplus, zminus)

    keep_row = pltpu.make_async_copy(spec, sr.at[pl.ds(pl.multiple_of(col * SUB, 8), SUB), :], loc.at[0])
    keep_row.start()
    keep_del = pltpu.make_async_copy(dly.at[pl.ds(0, PANEL), :], td, loc.at[1])
    keep_load = pltpu.make_async_copy(load, ld, loc.at[2])
    keep_load.start()

    @pl.when(row == 0)
    def _():
        keep_del.start()

    barrier = pltpu.get_barrier_semaphore()
    for peer in peers:
        pl.semaphore_signal(barrier, inc=1, device_id=peer, device_id_type=MESH)

    def block_of(t):
        s, k = (t + 2) // 4, (t + 2) % 4
        d = (k % 2 + k // 2) % 2
        return ((xh + k % 2) % 2) * 8 + (y + (2 * d - 1) * s + 8) % 8, d

    def rows(ref, j):
        return ref.at[pl.ds(pl.multiple_of(j * SUB, 8), SUB), :]

    def half(ref, j, c):
        return ref.at[
            pl.ds(pl.multiple_of(j * SUB, 8), SUB), pl.ds(pl.multiple_of(c * 1024, 1024), 1024)
        ]

    def copy(src, dst, sems, index, target):
        return pltpu.make_async_remote_copy(
            src_ref=src,
            dst_ref=dst,
            send_sem=sems.at[0, index],
            recv_sem=sems.at[1, index],
            device_id=target,
            device_id_type=MESH,
        )

    def both(t, q, act):
        j, d = block_of(t)
        part = half(sr, j, q)

        @pl.when(t == 0)
        def _():
            act(copy(part, part, rings, 2 + q, xmate))
            act(copy(part, part, rings, 4 + q, yplus))
            act(copy(part, part, rings, 8 + q, yminus))

        @pl.when(t == 1)
        def _():
            act(copy(part, part, rings, 6 + q, yminus))
            act(copy(part, part, rings, 10 + q, yplus))

        @pl.when((t >= 2) & (t <= 11))
        def _():
            act(copy(part, part, rings, 2 * t + 8 + q, dev(z, core, xh, (y + 1 - 2 * d + 8) % 8)))

    def ring(t):
        j, _ = block_of(t)
        for q in range(2):
            @pl.when((t >= 1) & (t <= 15))
            def _():
                copy(half(sr, j, q), half(sr, j, q), rings, 2 * t + q, mate).wait_recv()

            both(t, q, lambda c: c.start())

        part = rows(sr, j)

        @pl.when((t >= 0) & (t <= 15) & (row == col))
        def _():
            copy(part, rows(sc, j), col_mate, t, mate).start()

    class Cast:
        def __init__(self, hold, origin, zsrc, qsrc, sems):
            self.hold, self.origin = hold, origin
            self.to_mate, self.to_next, self.back = sems
            at_src = z == zsrc
            self.head = at_src & (core == qsrc)
            self.tail = at_src & (core != qsrc)
            self.away = jnp.logical_not(at_src)
            self.far = (sgn * (z - zsrc) + 8) % 8

        def sends(self, t, ok, act):
            full_from, full_to, part_from, part_to = self.refs(t)

            @pl.when(ok & self.head)
            def _():
                act(copy(full_from, full_to, self.to_mate, t, mate))
                act(copy(part_from, part_to, self.to_next, t, znext))

            @pl.when(ok & self.tail)
            def _():
                act(copy(part_to, part_to, self.to_next, t, znext))

            @pl.when(ok & self.away)
            def _():
                act(copy(part_to, part_to, self.back, t, mate))

            @pl.when(ok & self.away & (self.far < 7))
            def _():
                act(copy(part_to, part_to, self.to_next, t, znext))

        def refs(self, t):
            j, _ = block_of(t)
            return rows(self.origin, j), rows(self.hold, j), half(self.origin, j, core), half(self.hold, j, core)

        def other(self, t):
            return half(self.hold, block_of(t)[0], 1 - core)

        def step(self, t, ok):
            _, full, _, part = self.refs(t)

            @pl.when(ok & self.tail)
            def _():
                copy(full, full, self.to_mate, t, mate).wait_recv()

            @pl.when(ok & self.away)
            def _():
                copy(part, part, self.to_next, t, mate).wait_recv()

            self.sends(t, ok, lambda c: c.start())

        def collect(self, t, ok):
            part = self.other(t)

            @pl.when(ok & self.away)
            def _():
                copy(part, part, self.back, t, mate).wait_recv()

    class DelayCast(Cast):
        def piece(self, t, c):
            return self.hold.at[pl.ds(pl.multiple_of(t * 256 + c * 128, 128), 128), :]

        def refs(self, t):
            full = self.hold.at[pl.ds(pl.multiple_of(t * 256, 256), 256), :]
            return full, full, self.piece(t, core), self.piece(t, core)

        def other(self, t):
            return self.piece(t, 1 - core)

    class HeadCast(Cast):
        def setup(self):
            limit = 4 - core
            self.member = self.away & (self.far <= limit)
            self.onward = self.away & (self.far < limit)
            self.guest = self.away & (self.far > limit)

        def sends(self, t, ok, act, q):
            j, _ = block_of(t)
            origin, part = half(self.origin, j, q), half(self.hold, j, q)
            at = 2 * t + q

            @pl.when(ok & self.head)
            def _():
                act(copy(origin, part, self.to_next, at, znext))
                act(copy(origin, part, self.to_mate, at, mate))

            @pl.when(ok & (self.tail | self.onward))
            def _():
                act(copy(part, part, self.to_next, at, znext))

            @pl.when(ok & self.member)
            def _():
                act(copy(part, part, self.back, at, mate))

        def step(self, t, ok):
            for q in range(2):
                part, at = half(self.hold, block_of(t)[0], q), 2 * t + q

                @pl.when(ok & self.tail)
                def _():
                    copy(part, part, self.to_mate, at, mate).wait_recv()

                @pl.when(ok & self.member)
                def _():
                    copy(part, part, self.to_next, at, mate).wait_recv()

                self.sends(t, ok, lambda c: c.start(), q)

        def collect(self, t, ok):
            for q in range(2):
                part = half(self.hold, block_of(t)[0], q)

                @pl.when(ok & self.guest)
                def _():
                    copy(part, part, self.back, 2 * t + q, mate).wait_recv()

    top = HeadCast(s0, sr, 0, 0, (top_mate, top_next, top_back))
    top.setup()
    turns = DelayCast(td, td, 0, 0, (del_mate, del_next, del_back))

    zsrc, from_zero = col // 2, col % 2 == 0
    at_src = z == zsrc
    caster = at_src & (core == 1)
    guest = jnp.logical_not(at_src) & (core == 1)
    far_plus = (z - zsrc + 8) % 8
    far_minus = (zsrc - z + 8) % 8

    def side_sends(t, ok, way, act):
        j, _ = block_of(t)
        sems, target, far = ((col_plus, zplus, far_plus), (col_minus, zminus, far_minus))[way]
        part = half(sc, j, way)

        @pl.when(ok & caster & from_zero)
        def _():
            act(copy(part, part, sems, t, target))

        @pl.when(ok & caster & jnp.logical_not(from_zero))
        def _():
            act(copy(half(sr, j, way), part, sems, t, target))

        @pl.when(ok & guest & (far < 7))
        def _():
            act(copy(part, part, sems, t, target))

        @pl.when(ok & guest)
        def _():
            act(copy(part, part, col_back, 2 * t + way, mate))

    held = ((zsrc >= 1) & (zsrc <= 3)).astype(jnp.int32)
    minus_at = SIDE + 3 * (col == 1).astype(jnp.int32)
    plus_at = minus_at + 2 * zsrc * held

    def side_step(n):
        m = n - minus_at
        full = rows(sc, block_of(m)[0])

        @pl.when(caster & from_zero & (m >= 0) & (m <= 15))
        def _():
            copy(full, full, col_mate, m, mate).wait_recv()

        ways = ((col_plus, far_plus, plus_at), (col_minus, far_minus, minus_at))
        for way, (sems, far, start) in enumerate(ways):
            t = n - start - 2 * far
            ok = (t >= 0) & (t <= 15)
            part = half(sc, block_of(t)[0], way)

            @pl.when(ok & guest)
            def _():
                copy(part, part, sems, t, mate).wait_recv()

            side_sends(t, ok, way, lambda c: c.start())

    def top_in(t, carry):
        top.collect(t, top_ok(t))
        return carry

    def side_slot(n):
        @pl.when(caster & (held == 1) & (n == plus_at))
        def _():
            lax.fori_loop(0, 16, top_in, 0)

        side_step(n)

    def top_ok(t):
        return (t >= 0) & (t <= 15) & (block_of(t)[0] < TOP_BLOCKS)

    def turn_ok(t):
        return (t >= 0) & (t <= 1)

    @pl.when(row == 0)
    def _():
        keep_del.wait()

    keep_load.wait()
    keep_row.wait()
    pl.semaphore_wait(barrier, len(peers))

    def ring_slot(n):
        late = n - HOLD

        @pl.when(row == 0)
        def _():
            ring(n)

        @pl.when((row == 1) & ((2 * late) % 3 < 2))
        def _():
            ring((2 * late) // 3)

        @pl.when((row >= 2) & ((3 * n) % 5 < 3))
        def _():
            ring((3 * n) // 5)

    def lead_slot(n, carry):
        ring_slot(n)
        t = n - 2 * top.far
        top.step(t, top_ok(t))
        t = n - 2 * turns.far
        turns.step(t, turn_ok(t))

        @pl.when(core == 1)
        def _():
            side_slot(n)

        return carry

    lax.fori_loop(0, LEAD, lead_slot, 0)

    @pl.when(core == 0)
    def _():
        lax.fori_loop(0, 16, top_in, 0)

    keep_top = pltpu.make_async_copy(sr.at[pl.ds(0, TOP_BLOCKS * SUB), :], s0, loc.at[0])

    @pl.when(top.head)
    def _():
        keep_top.start()
        keep_top.wait()

    upper, under = pl.ds(0, 2 * NB), pl.ds(2 * NB, 2 * NB)
    results = [
        copy(link, link, res, 0, mate),
        copy(inv.at[upper, :], inv.at[upper, :], res, 1, mate),
        copy(inv.at[under, :], inv.at[under, :], res, 2, mate),
    ]

    def col_in(t, carry):
        j, _ = block_of(t)
        full = rows(sc, j)

        @pl.when(at_src & jnp.logical_not(from_zero))
        def _():
            copy(full, full, col_mate, t, mate).wait_recv()

        @pl.when(jnp.logical_not(at_src))
        def _():
            for way in range(2):
                part = half(sc, j, way)
                copy(part, part, col_back, 2 * t + way, mate).wait_recv()

        return carry

    def drain(t, carry):
        j, _ = block_of(t)
        for q in range(2):
            both(t, q, lambda c: c.wait_send())
            top.sends(t, top_ok(t), lambda c: c.wait_send(), q)


        @pl.when(turn_ok(t))
        def _():
            turns.collect(t, t >= 0)
            turns.sends(t, t >= 0, lambda c: c.wait_send())

        @pl.when(row == col)
        def _():
            copy(rows(sr, j), rows(sc, j), col_mate, t, mate).wait_send()

        return carry

    @pl.when(core == 0)
    def _():
        factor(
            s0, ld, low, link, inv, work,
            lambda k, i: ring_slot(LEAD + 8 * k + i),
            lambda: [c.start() for c in results[:2]],
        )
        lax.fori_loop(0, 16, drain, 0)
        results[2].start()
        lax.fori_loop(0, 16, col_in, 0)
        for c in results:
            c.wait_send()

    @pl.when(core == 1)
    def _():
        def later_slot(n, carry):
            ring_slot(n)
            side_slot(n)
            return carry

        lax.fori_loop(LEAD, LEAD + 31, later_slot, 0)
        lax.fori_loop(0, 16, drain, 0)

        @pl.when(jnp.logical_not(caster & (held == 1)))
        def _():
            lax.fori_loop(0, 16, top_in, 0)

        for c in results:
            c.wait_recv()

    keep_col = pltpu.make_async_copy(sr, sc, loc.at[1])

    @pl.when(row == col)
    def _():
        keep_col.start()
        keep_col.wait()

    @pl.when(core == 1)
    def _():
        def tidy(t, carry):
            for way in range(2):
                side_sends(t, t >= 0, way, lambda c: c.wait_send())
            return carry

        lax.fori_loop(0, 16, tidy, 0)


def factor_block(tile, between):
    lanes = (8, NB)
    sub = lax.broadcasted_iota(jnp.int32, lanes, 0)
    col_id = lax.broadcasted_iota(jnp.int32, (NB, NB), 1)
    row_id = lax.broadcasted_iota(jnp.int32, (NB, NB), 0)
    rest = tile
    aug = jnp.where(row_id == col_id, 1.0, 0.0).astype(F32)
    inverse = []
    for i in range(NB // 8):
        top, eye = rest[:8], aug[:8]
        cols = [jnp.broadcast_to(top[:, 8 * i + b : 8 * i + b + 1], lanes) for b in range(8)]
        scales, rows_t, rows_e, links = [], [], [], []
        for j in range(8):
            scale = lax.rsqrt(jnp.broadcast_to(cols[j][j : j + 1], lanes))
            lower = cols[j] * scale
            below = jnp.where(sub > j, lower, 0.0)
            row_t = jnp.broadcast_to(top[j : j + 1], lanes) * scale
            row_e = jnp.broadcast_to(eye[j : j + 1], lanes) * scale
            top = jnp.where(sub == j, row_t, top - below * row_t)
            eye = jnp.where(sub == j, row_e, eye - below * row_e)
            link = {}
            for b in range(j + 1, 8):
                link[b] = jnp.broadcast_to(lower[b : b + 1], lanes)
                cols[b] = cols[b] - below * link[b]
            scales.append(scale)
            rows_t.append(row_t)
            rows_e.append(row_e)
            links.append(link)
        inverse.append(eye)
        if i % 2 == 1:
            between(i // 2)
        if i == NB // 8 - 1:
            break
        count = NB - 8 * (i + 1)
        rest, aug = rest[8:], aug[8:]
        full = (count, NB)

        def spread(value):
            return jnp.broadcast_to(value[None], (count // 8, 8, NB)).reshape(full)

        parts = [jnp.broadcast_to(rest[:, 8 * i + b : 8 * i + b + 1], full) for b in range(8)]
        for j in range(8):
            lower = parts[j] * spread(scales[j])
            rest = rest - lower * spread(rows_t[j])
            aug = aug - lower * spread(rows_e[j])
            for b in range(j + 1, 8):
                parts[b] = parts[b] - lower * spread(links[j][b])
    return jnp.concatenate(inverse, axis=0)


def factor(s0, load, low, link, inv, work, between, halfway):
    head = s0[:PANEL]
    ids = lax.broadcasted_iota(jnp.int32, (PANEL, PANEL), 0)
    diag = ids == lax.broadcasted_iota(jnp.int32, (PANEL, PANEL), 1)
    lane = jnp.concatenate([load[b : b + 1, :] for b in range(PANEL // NB)], axis=1)
    work[...] = dot_nt(head, head) * (1.0 / 1024) + jnp.where(diag, lane, 0.0)
    inv[...] = jnp.zeros_like(inv)

    def join(q):
        a, b, c = 2 * q * NB, (2 * q + 1) * NB, (2 * q + 2) * NB
        inner = dot_nn(low[b:c, a:b], inv[a:b, :NB], HI)
        inv[b:c, :NB] = -dot_nn(inv[b:c, NB:], inner, HI)

    def step(k, carry):
        at = pl.ds(pl.multiple_of(k * NB, NB), NB)
        inverse = factor_block(work[at, at], lambda i: between(k, i))
        inv[at, pl.ds(pl.multiple_of((k % 2) * NB, NB), NB)] = inverse
        for now in range(PANEL // NB - 1):
            here, rest = slice(now * NB, (now + 1) * NB), slice((now + 1) * NB, PANEL)

            @pl.when(k == now)
            def _():
                panel = dot_nt(work[rest, here], inverse, HI)
                low[rest, here] = panel
                work[rest, rest] = work[rest, rest] - dot_nt(panel, panel, HI)

        @pl.when(k == 1)
        def _():
            join(0)
            link[...] = low[2 * NB :, : 2 * NB]

        @pl.when(k == 2)
        def _():
            halfway()

        return carry

    lax.fori_loop(0, PANEL // NB, step, 0)
    join(1)


def gather(spectra, delays, load):
    vmem = pl.BlockSpec(memory_space=pltpu.VMEM)
    outside = pl.BlockSpec(memory_space=pltpu.HBM)
    dma = pltpu.SemaphoreType.DMA
    return pl.pallas_call(
        gather_kernel,
        out_shape=(
            jax.ShapeDtypeStruct((640, 2048), jnp.bfloat16),
            jax.ShapeDtypeStruct((640, 2048), jnp.bfloat16),
            jax.ShapeDtypeStruct((TOP_BLOCKS * SUB, 2048), jnp.bfloat16),
            jax.ShapeDtypeStruct((PANEL, 128), jnp.int32),
            jax.ShapeDtypeStruct((2 * NB, 2 * NB), F32),
            jax.ShapeDtypeStruct((PANEL, 2 * NB), F32),
            jax.ShapeDtypeStruct((80, 128), F32),
        ),
        in_specs=[outside] * 3,
        out_specs=(vmem,) * 7,
        scratch_shapes=[pltpu.VMEM((PANEL, PANEL), F32)] * 2
        + [dma((3,))]
        + [dma((2, 32))] * 4
        + [dma((2, 16))] * 3
        + [dma((2, 32))]
        + [dma((2, 2))] * 3
        + [dma((2, 3))],
        compiler_params=pltpu.CompilerParams(
            collective_id=0, has_side_effects=True, vmem_limit_bytes=20 << 20
        ),
        name="gather_and_factor",
    )(spectra, delays, load)


def split(value):
    high = value.astype(jnp.bfloat16)
    return high, (value - high.astype(F32)).astype(jnp.bfloat16)


def three(dot, a, b):
    return dot(a[0], b[0]) + (dot(a[0], b[1]) + dot(a[1], b[0]))


def steer_of(delays, bin_value):
    phase = (delays * bin_value) & (NFFT - 1)
    turned = phase + NFFT // 8
    quad = (turned >> 9) & 3
    angle = ((turned & 511) - 256).astype(F32) * (6.283185307179586 / NFFT)
    sq = angle * angle
    cosine = 1.0 + sq * (-0.5 + sq * (1.0 / 24 + sq * (-1.0 / 720 + sq * (1.0 / 40320))))
    sine = angle * (1.0 + sq * (-1.0 / 6 + sq * (1.0 / 120 + sq * (-1.0 / 5040 + sq * (1.0 / 362880)))))
    swap = (quad & 1) == 1
    base_c = jnp.where(swap, sine, cosine)
    base_s = jnp.where(swap, cosine, sine)
    out_c = jnp.where((quad == 1) | (quad == 2), -base_c, base_c)
    out_s = jnp.where(quad >= 2, -base_s, base_s)
    return out_c, out_s


def finish_kernel(bins, sr, sc, s0, low, inv, load, td, dly_far, trail, panel, white, dly, sem):
    fetch = pltpu.make_async_copy(dly_far, dly, sem)
    fetch.start()
    row, col = lax.axis_index("row"), lax.axis_index("col")
    head = s0[:PANEL]
    mid = 2 * NB
    inv_a, inv_b = split(inv[:mid]), split(inv[mid:])
    link = split(low[...])

    def lanes_of(index):
        return jnp.concatenate([load[pl.ds(index * 5 + b, 1), :] for b in range(5)], axis=1)

    def solve_rows(block, lane, is_first):
        base = dot_nt(block, head) * (1.0 / 1024)
        ids = lax.broadcasted_iota(jnp.int32, base.shape, 0)
        diag = ids == lax.broadcasted_iota(jnp.int32, base.shape, 1)
        base = base + jnp.where(diag & is_first, lane[:, :PANEL], 0.0)
        left = three(dot_nt, split(base[:, :mid]), inv_a)
        left_parts = split(left)
        right = base[:, mid:] - three(dot_nt, left_parts, link)
        right = three(dot_nt, split(right), inv_b)
        right_parts = split(right)
        whole = [jnp.concatenate([p, q], axis=1) for p, q in zip(left_parts, right_parts)]
        return jnp.concatenate([left, right], axis=1), whole

    lane_r = lanes_of(row)
    own, own_parts = solve_rows(sr[...], lane_r, row == 0)
    panel[...] = own
    _, other_parts = solve_rows(sc[...], lanes_of(col), col == 0)
    shape = (640, 640)
    ids_r = lax.broadcasted_iota(jnp.int32, shape, 0)
    ids_c = lax.broadcasted_iota(jnp.int32, shape, 1)
    tile = dot_nt(sr[...], sc[...]) * (1.0 / 1024)
    tile = tile + jnp.where((ids_r == ids_c) & (row == col), lane_r, 0.0)
    update = tile - three(dot_nt, own_parts, other_parts)
    keep = (ids_r + row * 640 >= PANEL) & (ids_c + col * 640 >= PANEL)
    trail[...] = jnp.where(keep, update, 0.0)

    upper = jnp.concatenate(steer_of(td[...], bins[0]), axis=1)
    first = three(dot_nn, inv_a, split(upper[:mid]))
    second = upper[mid:] - three(dot_nn, link, split(first))
    second = three(dot_nn, inv_b, split(second))
    solved = jnp.concatenate([first, second], axis=0)
    fetch.wait()
    steer = jnp.concatenate(steer_of(dly[...], bins[0]), axis=1)
    lower = steer - three(dot_nn, own_parts, split(solved))
    padded = jnp.concatenate([solved, jnp.zeros((640 - PANEL, 256), F32)], axis=0)
    ids = lax.broadcasted_iota(jnp.int32, lower.shape, 0)
    stacked = jnp.where((ids < PANEL) & (row == 0), padded, lower)
    white[0] = stacked[:, :128]
    white[1] = stacked[:, 128:]


def finish(bins, sr, sc, s0, low, inv, load, td, delays):
    vmem = pl.BlockSpec(memory_space=pltpu.VMEM)
    smem = pl.BlockSpec(memory_space=pltpu.SMEM)
    outside = pl.BlockSpec(memory_space=pltpu.HBM)
    return pl.pallas_call(
        finish_kernel,
        out_shape=(
            jax.ShapeDtypeStruct((640, 640), F32),
            jax.ShapeDtypeStruct((640, PANEL), F32),
            jax.ShapeDtypeStruct((2, 640, 128), F32),
        ),
        in_specs=[smem] + [vmem] * 7 + [outside],
        out_specs=(vmem,) * 3,
        scratch_shapes=[pltpu.VMEM((640, 128), jnp.int32), pltpu.SemaphoreType.DMA(())],
        compiler_params=pltpu.CompilerParams(vmem_limit_bytes=36 << 20),
        name="finish_tiles",
    )(bins, sr, sc, s0, low, inv, load, td, delays)


def on_device(spectra, loading, delays, bin_index):
    load = pltpu.with_memory_space_constraint(loading.reshape(80, 128), pltpu.HBM)
    spectra = pltpu.with_memory_space_constraint(spectra, pltpu.HBM)
    delays = pltpu.with_memory_space_constraint(delays, pltpu.HBM)
    sr, sc, s0, td, low, inv, lanes = gather(spectra, delays, load)
    return finish(bin_index, sr, sc, s0, low, inv, lanes, td, delays)


def solution(mesh):
    return jax.shard_map(
        on_device,
        mesh=mesh,
        in_specs=(P(("row", "col"), "freq"), P("freq"), P("row", "col"), P("freq")),
        out_specs=(
            P(("freq", "row"), "col"),
            P(("freq", "row"), None),
            P(None, ("freq", "row"), "col"),
        ),
        check_vma=False,
    )
```

```python
import jax
import jax.numpy as jnp
from jax import lax
from jax.experimental import pallas as pl
from jax.experimental.pallas import tpu as pltpu
from jax.sharding import PartitionSpec as P

PANEL = 512
NFFT = 2048
NB = 128
SUB = 40
F32 = jnp.float32
HI = lax.Precision.HIGHEST
MESH = pl.DeviceIdType.MESH
TOP_BLOCKS = 13
HOLD = 12
LEAD = 24
SIDE = 17


def dot_nt(a, b, precision=None):
    return lax.dot_general(
        a, b, (((1,), (1,)), ((), ())), precision=precision, preferred_element_type=F32
    )


def dot_nn(a, b, precision=None):
    return lax.dot_general(
        a, b, (((1,), (0,)), ((), ())), precision=precision, preferred_element_type=F32
    )


def gather_kernel(
    spec, dly, load, sr, sc, s0, td, link, inv, ld, low, work, loc, rings, top_mate, top_next, top_back,
    col_mate, col_plus, col_minus, col_back, del_mate, del_next, del_back, res
):
    row = lax.axis_index("row")
    col = lax.axis_index("col")
    z, core = row // 2, row % 2
    xh, y = col // 8, col % 8
    sgn = 1 - 2 * core

    def dev(z_, core_, xh_, y_):
        return {"row": z_ * 2 + core_, "col": xh_ * 8 + y_}

    mate = dev(z, 1 - core, xh, y)
    xmate = dev(z, core, 1 - xh, y)
    yplus = dev(z, core, xh, (y + 1) % 8)
    yminus = dev(z, core, xh, (y + 7) % 8)
    zplus = dev((z + 1) % 8, core, xh, y)
    zminus = dev((z + 7) % 8, core, xh, y)
    znext = dev((z + sgn + 8) % 8, core, xh, y)
    peers = (mate, xmate, yplus, yminus, zplus, zminus)

    keep_row = pltpu.make_async_copy(spec, sr.at[pl.ds(pl.multiple_of(col * SUB, 8), SUB), :], loc.at[0])
    keep_row.start()
    keep_del = pltpu.make_async_copy(dly.at[pl.ds(0, PANEL), :], td, loc.at[1])
    keep_load = pltpu.make_async_copy(load, ld, loc.at[2])
    keep_load.start()

    @pl.when(row == 0)
    def _():
        keep_del.start()

    barrier = pltpu.get_barrier_semaphore()
    for peer in peers:
        pl.semaphore_signal(barrier, inc=1, device_id=peer, device_id_type=MESH)

    def block_of(t):
        s, k = (t + 2) // 4, (t + 2) % 4
        d = (k % 2 + k // 2) % 2
        return ((xh + k % 2) % 2) * 8 + (y + (2 * d - 1) * s + 8) % 8, d

    def rows(ref, j):
        return ref.at[pl.ds(pl.multiple_of(j * SUB, 8), SUB), :]

    def half(ref, j, c):
        return ref.at[
            pl.ds(pl.multiple_of(j * SUB, 8), SUB), pl.ds(pl.multiple_of(c * 1024, 1024), 1024)
        ]

    def copy(src, dst, sems, index, target):
        return pltpu.make_async_remote_copy(
            src_ref=src,
            dst_ref=dst,
            send_sem=sems.at[0, index],
            recv_sem=sems.at[1, index],
            device_id=target,
            device_id_type=MESH,
        )

    def both(t, q, act):
        j, d = block_of(t)
        part = half(sr, j, q)

        @pl.when(t == 0)
        def _():
            act(copy(part, part, rings, 2 + q, xmate))
            act(copy(part, part, rings, 4 + q, yplus))
            act(copy(part, part, rings, 8 + q, yminus))

        @pl.when(t == 1)
        def _():
            act(copy(part, part, rings, 6 + q, yminus))
            act(copy(part, part, rings, 10 + q, yplus))

        @pl.when((t >= 2) & (t <= 11))
        def _():
            act(copy(part, part, rings, 2 * t + 8 + q, dev(z, core, xh, (y + 1 - 2 * d + 8) % 8)))

    def ring(t):
        j, _ = block_of(t)
        for q in range(2):
            @pl.when((t >= 1) & (t <= 15))
            def _():
                copy(half(sr, j, q), half(sr, j, q), rings, 2 * t + q, mate).wait_recv()

            both(t, q, lambda c: c.start())

        part = rows(sr, j)

        @pl.when((t >= 0) & (t <= 15) & (row == col))
        def _():
            copy(part, rows(sc, j), col_mate, t, mate).start()

    class Cast:
        def __init__(self, hold, origin, zsrc, qsrc, sems):
            self.hold, self.origin = hold, origin
            self.to_mate, self.to_next, self.back = sems
            at_src = z == zsrc
            self.head = at_src & (core == qsrc)
            self.tail = at_src & (core != qsrc)
            self.away = jnp.logical_not(at_src)
            self.far = (sgn * (z - zsrc) + 8) % 8

        def sends(self, t, ok, act):
            full_from, full_to, part_from, part_to = self.refs(t)

            @pl.when(ok & self.head)
            def _():
                act(copy(full_from, full_to, self.to_mate, t, mate))
                act(copy(part_from, part_to, self.to_next, t, znext))

            @pl.when(ok & self.tail)
            def _():
                act(copy(part_to, part_to, self.to_next, t, znext))

            @pl.when(ok & self.away)
            def _():
                act(copy(part_to, part_to, self.back, t, mate))

            @pl.when(ok & self.away & (self.far < 7))
            def _():
                act(copy(part_to, part_to, self.to_next, t, znext))

        def refs(self, t):
            j, _ = block_of(t)
            return rows(self.origin, j), rows(self.hold, j), half(self.origin, j, core), half(self.hold, j, core)

        def other(self, t):
            return half(self.hold, block_of(t)[0], 1 - core)

        def step(self, t, ok):
            _, full, _, part = self.refs(t)

            @pl.when(ok & self.tail)
            def _():
                copy(full, full, self.to_mate, t, mate).wait_recv()

            @pl.when(ok & self.away)
            def _():
                copy(part, part, self.to_next, t, mate).wait_recv()

            self.sends(t, ok, lambda c: c.start())

        def collect(self, t, ok):
            part = self.other(t)

            @pl.when(ok & self.away)
            def _():
                copy(part, part, self.back, t, mate).wait_recv()

    class DelayCast(Cast):
        def piece(self, t, c):
            return self.hold.at[pl.ds(pl.multiple_of(t * 256 + c * 128, 128), 128), :]

        def refs(self, t):
            full = self.hold.at[pl.ds(pl.multiple_of(t * 256, 256), 256), :]
            return full, full, self.piece(t, core), self.piece(t, core)

        def other(self, t):
            return self.piece(t, 1 - core)

    class HeadCast(Cast):
        def setup(self):
            limit = 4 - core
            self.member = self.away & (self.far <= limit)
            self.onward = self.away & (self.far < limit)
            self.guest = self.away & (self.far > limit)

        def sends(self, t, ok, act, q):
            j, _ = block_of(t)
            origin, part = half(self.origin, j, q), half(self.hold, j, q)
            at = 2 * t + q

            @pl.when(ok & self.head)
            def _():
                act(copy(origin, part, self.to_next, at, znext))
                act(copy(origin, part, self.to_mate, at, mate))

            @pl.when(ok & (self.tail | self.onward))
            def _():
                act(copy(part, part, self.to_next, at, znext))

            @pl.when(ok & self.member)
            def _():
                act(copy(part, part, self.back, at, mate))

        def step(self, t, ok):
            for q in range(2):
                part, at = half(self.hold, block_of(t)[0], q), 2 * t + q

                @pl.when(ok & self.tail)
                def _():
                    copy(part, part, self.to_mate, at, mate).wait_recv()

                @pl.when(ok & self.member)
                def _():
                    copy(part, part, self.to_next, at, mate).wait_recv()

                self.sends(t, ok, lambda c: c.start(), q)

        def collect(self, t, ok):
            for q in range(2):
                part = half(self.hold, block_of(t)[0], q)

                @pl.when(ok & self.guest)
                def _():
                    copy(part, part, self.back, 2 * t + q, mate).wait_recv()

    top = HeadCast(s0, sr, 0, 0, (top_mate, top_next, top_back))
    top.setup()
    turns = DelayCast(td, td, 0, 0, (del_mate, del_next, del_back))

    zsrc, from_zero = col // 2, col % 2 == 0
    at_src = z == zsrc
    caster = at_src & (core == 1)
    guest = jnp.logical_not(at_src) & (core == 1)
    far_plus = (z - zsrc + 8) % 8
    far_minus = (zsrc - z + 8) % 8

    def side_sends(t, ok, way, act):
        j, _ = block_of(t)
        sems, target, far = ((col_plus, zplus, far_plus), (col_minus, zminus, far_minus))[way]
        part = half(sc, j, way)

        @pl.when(ok & caster & from_zero)
        def _():
            act(copy(part, part, sems, t, target))

        @pl.when(ok & caster & jnp.logical_not(from_zero))
        def _():
            act(copy(half(sr, j, way), part, sems, t, target))

        @pl.when(ok & guest & (far < 7))
        def _():
            act(copy(part, part, sems, t, target))

        @pl.when(ok & guest)
        def _():
            act(copy(part, part, col_back, 2 * t + way, mate))

    held = ((zsrc >= 1) & (zsrc <= 3)).astype(jnp.int32)
    minus_at = SIDE
    plus_at = minus_at + 2 * zsrc * held

    def side_step(n):
        m = n - minus_at
        full = rows(sc, block_of(m)[0])

        @pl.when(caster & from_zero & (m >= 0) & (m <= 15))
        def _():
            copy(full, full, col_mate, m, mate).wait_recv()

        ways = ((col_plus, far_plus, plus_at), (col_minus, far_minus, minus_at))
        for way, (sems, far, start) in enumerate(ways):
            t = n - start - 2 * far
            ok = (t >= 0) & (t <= 15)
            part = half(sc, block_of(t)[0], way)

            @pl.when(ok & guest)
            def _():
                copy(part, part, sems, t, mate).wait_recv()

            side_sends(t, ok, way, lambda c: c.start())

    def top_in(t, carry):
        top.collect(t, top_ok(t))
        return carry

    def side_slot(n):
        @pl.when(caster & (held == 1) & (n == plus_at))
        def _():
            lax.fori_loop(0, 16, top_in, 0)

        side_step(n)

    def top_ok(t):
        return (t >= 0) & (t <= 15) & (block_of(t)[0] < TOP_BLOCKS)

    def turn_ok(t):
        return (t >= 0) & (t <= 1)

    @pl.when(row == 0)
    def _():
        keep_del.wait()

    keep_load.wait()
    keep_row.wait()
    pl.semaphore_wait(barrier, len(peers))

    def ring_slot(n):
        late = n - HOLD

        @pl.when(row == 0)
        def _():
            ring(n)

        @pl.when(row == 1)
        def _():
            ring(late)

        @pl.when((row >= 2) & ((3 * n) % 5 < 3))
        def _():
            ring((3 * n) // 5)

    def lead_slot(n, carry):
        ring_slot(n)
        t = n - 2 * top.far
        top.step(t, top_ok(t))
        t = n - 2 * turns.far
        turns.step(t, turn_ok(t))

        @pl.when(core == 1)
        def _():
            side_slot(n)

        return carry

    lax.fori_loop(0, LEAD, lead_slot, 0)

    @pl.when(core == 0)
    def _():
        lax.fori_loop(0, 16, top_in, 0)

    keep_top = pltpu.make_async_copy(sr.at[pl.ds(0, TOP_BLOCKS * SUB), :], s0, loc.at[0])

    @pl.when(top.head)
    def _():
        keep_top.start()
        keep_top.wait()

    upper, under = pl.ds(0, 2 * NB), pl.ds(2 * NB, 2 * NB)
    results = [
        copy(link, link, res, 0, mate),
        copy(inv.at[upper, :], inv.at[upper, :], res, 1, mate),
        copy(inv.at[under, :], inv.at[under, :], res, 2, mate),
    ]

    def col_in(t, carry):
        j, _ = block_of(t)
        full = rows(sc, j)

        @pl.when(at_src & jnp.logical_not(from_zero))
        def _():
            copy(full, full, col_mate, t, mate).wait_recv()

        @pl.when(jnp.logical_not(at_src))
        def _():
            for way in range(2):
                part = half(sc, j, way)
                copy(part, part, col_back, 2 * t + way, mate).wait_recv()

        return carry

    def drain(t, carry):
        j, _ = block_of(t)
        for q in range(2):
            both(t, q, lambda c: c.wait_send())
            top.sends(t, top_ok(t), lambda c: c.wait_send(), q)


        @pl.when(turn_ok(t))
        def _():
            turns.collect(t, t >= 0)
            turns.sends(t, t >= 0, lambda c: c.wait_send())

        @pl.when(row == col)
        def _():
            copy(rows(sr, j), rows(sc, j), col_mate, t, mate).wait_send()

        return carry

    @pl.when(core == 0)
    def _():
        factor(
            s0, ld, low, link, inv, work,
            lambda k, i: ring_slot(LEAD + 8 * k + i),
            lambda: [c.start() for c in results[:2]],
        )
        lax.fori_loop(0, 16, drain, 0)
        results[2].start()
        lax.fori_loop(0, 16, col_in, 0)
        for c in results:
            c.wait_send()

    @pl.when(core == 1)
    def _():
        def later_slot(n, carry):
            ring_slot(n)
            side_slot(n)

            @pl.when((n >= LEAD + 8) & (n < LEAD + 24))
            def _():
                t = n - LEAD - 8
                drain(t, 0)

                @pl.when(jnp.logical_not(caster & (held == 1)))
                def _():
                    top.collect(t, top_ok(t))

            return carry

        lax.fori_loop(LEAD, LEAD + 31, later_slot, 0)
        for c in results:
            c.wait_recv()

    keep_col = pltpu.make_async_copy(sr, sc, loc.at[1])

    @pl.when(row == col)
    def _():
        keep_col.start()
        keep_col.wait()

    @pl.when(core == 1)
    def _():
        def tidy(t, carry):
            for way in range(2):
                side_sends(t, t >= 0, way, lambda c: c.wait_send())
            return carry

        lax.fori_loop(0, 16, tidy, 0)


def factor_block(tile, between):
    lanes = (8, NB)
    sub = lax.broadcasted_iota(jnp.int32, lanes, 0)
    col_id = lax.broadcasted_iota(jnp.int32, (NB, NB), 1)
    row_id = lax.broadcasted_iota(jnp.int32, (NB, NB), 0)
    rest = tile
    aug = jnp.where(row_id == col_id, 1.0, 0.0).astype(F32)
    inverse = []
    for i in range(NB // 8):
        top, eye = rest[:8], aug[:8]
        cols = [jnp.broadcast_to(top[:, 8 * i + b : 8 * i + b + 1], lanes) for b in range(8)]
        scales, rows_t, rows_e, links = [], [], [], []
        for j in range(8):
            scale = lax.rsqrt(jnp.broadcast_to(cols[j][j : j + 1], lanes))
            lower = cols[j] * scale
            below = jnp.where(sub > j, lower, 0.0)
            row_t = jnp.broadcast_to(top[j : j + 1], lanes) * scale
            row_e = jnp.broadcast_to(eye[j : j + 1], lanes) * scale
            top = jnp.where(sub == j, row_t, top - below * row_t)
            eye = jnp.where(sub == j, row_e, eye - below * row_e)
            link = {}
            for b in range(j + 1, 8):
                link[b] = jnp.broadcast_to(lower[b : b + 1], lanes)
                cols[b] = cols[b] - below * link[b]
            scales.append(scale)
            rows_t.append(row_t)
            rows_e.append(row_e)
            links.append(link)
        inverse.append(eye)
        if i % 2 == 1:
            between(i // 2)
        if i == NB // 8 - 1:
            break
        count = NB - 8 * (i + 1)
        rest, aug = rest[8:], aug[8:]
        full = (count, NB)

        def spread(value):
            return jnp.broadcast_to(value[None], (count // 8, 8, NB)).reshape(full)

        parts = [jnp.broadcast_to(rest[:, 8 * i + b : 8 * i + b + 1], full) for b in range(8)]
        for j in range(8):
            lower = parts[j] * spread(scales[j])
            rest = rest - lower * spread(rows_t[j])
            aug = aug - lower * spread(rows_e[j])
            for b in range(j + 1, 8):
                parts[b] = parts[b] - lower * spread(links[j][b])
    return jnp.concatenate(inverse, axis=0)


def factor(s0, load, low, link, inv, work, between, halfway):
    head = s0[:PANEL]
    ids = lax.broadcasted_iota(jnp.int32, (PANEL, PANEL), 0)
    diag = ids == lax.broadcasted_iota(jnp.int32, (PANEL, PANEL), 1)
    lane = jnp.concatenate([load[b : b + 1, :] for b in range(PANEL // NB)], axis=1)
    work[...] = dot_nt(head, head) * (1.0 / 1024) + jnp.where(diag, lane, 0.0)
    inv[...] = jnp.zeros_like(inv)

    def join(q):
        a, b, c = 2 * q * NB, (2 * q + 1) * NB, (2 * q + 2) * NB
        inner = dot_nn(low[b:c, a:b], inv[a:b, :NB], HI)
        inv[b:c, :NB] = -dot_nn(inv[b:c, NB:], inner, HI)

    def step(k, carry):
        at = pl.ds(pl.multiple_of(k * NB, NB), NB)
        inverse = factor_block(work[at, at], lambda i: between(k, i))
        inv[at, pl.ds(pl.multiple_of((k % 2) * NB, NB), NB)] = inverse
        for now in range(PANEL // NB - 1):
            here, rest = slice(now * NB, (now + 1) * NB), slice((now + 1) * NB, PANEL)

            @pl.when(k == now)
            def _():
                panel = dot_nt(work[rest, here], inverse, HI)
                low[rest, here] = panel
                work[rest, rest] = work[rest, rest] - dot_nt(panel, panel, HI)

        @pl.when(k == 1)
        def _():
            join(0)
            link[...] = low[2 * NB :, : 2 * NB]

        @pl.when(k == 2)
        def _():
            halfway()

        return carry

    lax.fori_loop(0, PANEL // NB, step, 0)
    join(1)


def gather(spectra, delays, load):
    vmem = pl.BlockSpec(memory_space=pltpu.VMEM)
    outside = pl.BlockSpec(memory_space=pltpu.HBM)
    dma = pltpu.SemaphoreType.DMA
    return pl.pallas_call(
        gather_kernel,
        out_shape=(
            jax.ShapeDtypeStruct((640, 2048), jnp.bfloat16),
            jax.ShapeDtypeStruct((640, 2048), jnp.bfloat16),
            jax.ShapeDtypeStruct((TOP_BLOCKS * SUB, 2048), jnp.bfloat16),
            jax.ShapeDtypeStruct((PANEL, 128), jnp.int32),
            jax.ShapeDtypeStruct((2 * NB, 2 * NB), F32),
            jax.ShapeDtypeStruct((PANEL, 2 * NB), F32),
            jax.ShapeDtypeStruct((80, 128), F32),
        ),
        in_specs=[outside] * 3,
        out_specs=(vmem,) * 7,
        scratch_shapes=[pltpu.VMEM((PANEL, PANEL), F32)] * 2
        + [dma((3,))]
        + [dma((2, 32))] * 4
        + [dma((2, 16))] * 3
        + [dma((2, 32))]
        + [dma((2, 2))] * 3
        + [dma((2, 3))],
        compiler_params=pltpu.CompilerParams(
            collective_id=0, has_side_effects=True, vmem_limit_bytes=20 << 20
        ),
        name="gather_and_factor",
    )(spectra, delays, load)


def split(value):
    high = value.astype(jnp.bfloat16)
    return high, (value - high.astype(F32)).astype(jnp.bfloat16)


def three(dot, a, b):
    return dot(a[0], b[0]) + (dot(a[0], b[1]) + dot(a[1], b[0]))


def steer_of(delays, bin_value):
    phase = (delays * bin_value) & (NFFT - 1)
    turned = phase + NFFT // 8
    quad = (turned >> 9) & 3
    angle = ((turned & 511) - 256).astype(F32) * (6.283185307179586 / NFFT)
    sq = angle * angle
    cosine = 1.0 + sq * (-0.5 + sq * (1.0 / 24 + sq * (-1.0 / 720 + sq * (1.0 / 40320))))
    sine = angle * (1.0 + sq * (-1.0 / 6 + sq * (1.0 / 120 + sq * (-1.0 / 5040 + sq * (1.0 / 362880)))))
    swap = (quad & 1) == 1
    base_c = jnp.where(swap, sine, cosine)
    base_s = jnp.where(swap, cosine, sine)
    out_c = jnp.where((quad == 1) | (quad == 2), -base_c, base_c)
    out_s = jnp.where(quad >= 2, -base_s, base_s)
    return out_c, out_s


def finish_kernel(bins, sr, sc, s0, low, inv, load, td, dly_far, trail, panel, white, dly, sem):
    fetch = pltpu.make_async_copy(dly_far, dly, sem)
    fetch.start()
    row, col = lax.axis_index("row"), lax.axis_index("col")
    head = s0[:PANEL]
    mid = 2 * NB
    inv_a, inv_b = split(inv[:mid]), split(inv[mid:])
    link = split(low[...])

    def lanes_of(index):
        return jnp.concatenate([load[pl.ds(index * 5 + b, 1), :] for b in range(5)], axis=1)

    def solve_rows(block, lane, is_first):
        base = dot_nt(block, head) * (1.0 / 1024)
        ids = lax.broadcasted_iota(jnp.int32, base.shape, 0)
        diag = ids == lax.broadcasted_iota(jnp.int32, base.shape, 1)
        base = base + jnp.where(diag & is_first, lane[:, :PANEL], 0.0)
        left = three(dot_nt, split(base[:, :mid]), inv_a)
        left_parts = split(left)
        right = base[:, mid:] - three(dot_nt, left_parts, link)
        right = three(dot_nt, split(right), inv_b)
        right_parts = split(right)
        whole = [jnp.concatenate([p, q], axis=1) for p, q in zip(left_parts, right_parts)]
        return jnp.concatenate([left, right], axis=1), whole

    lane_r = lanes_of(row)
    own, own_parts = solve_rows(sr[...], lane_r, row == 0)
    panel[...] = own
    _, other_parts = solve_rows(sc[...], lanes_of(col), col == 0)
    shape = (640, 640)
    ids_r = lax.broadcasted_iota(jnp.int32, shape, 0)
    ids_c = lax.broadcasted_iota(jnp.int32, shape, 1)
    tile = dot_nt(sr[...], sc[...]) * (1.0 / 1024)
    tile = tile + jnp.where((ids_r == ids_c) & (row == col), lane_r, 0.0)
    update = tile - three(dot_nt, own_parts, other_parts)
    keep = (ids_r + row * 640 >= PANEL) & (ids_c + col * 640 >= PANEL)
    trail[...] = jnp.where(keep, update, 0.0)

    upper = jnp.concatenate(steer_of(td[...], bins[0]), axis=1)
    first = three(dot_nn, inv_a, split(upper[:mid]))
    second = upper[mid:] - three(dot_nn, link, split(first))
    second = three(dot_nn, inv_b, split(second))
    solved = jnp.concatenate([first, second], axis=0)
    fetch.wait()
    steer = jnp.concatenate(steer_of(dly[...], bins[0]), axis=1)
    lower = steer - three(dot_nn, own_parts, split(solved))
    padded = jnp.concatenate([solved, jnp.zeros((640 - PANEL, 256), F32)], axis=0)
    ids = lax.broadcasted_iota(jnp.int32, lower.shape, 0)
    stacked = jnp.where((ids < PANEL) & (row == 0), padded, lower)
    white[0] = stacked[:, :128]
    white[1] = stacked[:, 128:]


def finish(bins, sr, sc, s0, low, inv, load, td, delays):
    vmem = pl.BlockSpec(memory_space=pltpu.VMEM)
    smem = pl.BlockSpec(memory_space=pltpu.SMEM)
    outside = pl.BlockSpec(memory_space=pltpu.HBM)
    return pl.pallas_call(
        finish_kernel,
        out_shape=(
            jax.ShapeDtypeStruct((640, 640), F32),
            jax.ShapeDtypeStruct((640, PANEL), F32),
            jax.ShapeDtypeStruct((2, 640, 128), F32),
        ),
        in_specs=[smem] + [vmem] * 7 + [outside],
        out_specs=(vmem,) * 3,
        scratch_shapes=[pltpu.VMEM((640, 128), jnp.int32), pltpu.SemaphoreType.DMA(())],
        compiler_params=pltpu.CompilerParams(vmem_limit_bytes=36 << 20),
        name="finish_tiles",
    )(bins, sr, sc, s0, low, inv, load, td, delays)


def on_device(spectra, loading, delays, bin_index):
    load = pltpu.with_memory_space_constraint(loading.reshape(80, 128), pltpu.HBM)
    spectra = pltpu.with_memory_space_constraint(spectra, pltpu.HBM)
    delays = pltpu.with_memory_space_constraint(delays, pltpu.HBM)
    sr, sc, s0, td, low, inv, lanes = gather(spectra, delays, load)
    return finish(bin_index, sr, sc, s0, low, inv, lanes, td, delays)


def solution(mesh):
    return jax.shard_map(
        on_device,
        mesh=mesh,
        in_specs=(P(("row", "col"), "freq"), P("freq"), P("row", "col"), P("freq")),
        out_specs=(
            P(("freq", "row"), "col"),
            P(("freq", "row"), None),
            P(None, ("freq", "row"), "col"),
        ),
        check_vma=False,
    )
```
